32 devices in a mesh: dp: 8 (over z, core), ctx: 4 (over y, x).
Axes of the slice: x: 2, y: 2, z: 4, core: 2. Of those that a mesh axis runs over, the one named last changes fastest.
Arguments:
- hidden_in: bfloat16 [16, 1024, 768], P('dp', 'ctx'), may hold values from -6 to 6
- doc_lengths: int32 [16, 4], P('dp'), may hold values from 1 to 1021, as said below
- ln1_gain: bfloat16 [768], P('dp'), may hold values from 0.5 to 1.5
- ln1_bias: bfloat16 [768], P('dp'), may hold values from -3 to 3
- ln2_gain: bfloat16 [768], P('dp'), may hold values from 0.5 to 1.5
- ln2_bias: bfloat16 [768], P('dp'), may hold values from -3 to 3
- qkv_weight: bfloat16 [768, 2304], P('dp'), may hold values from -12 to 12
- qkv_bias: bfloat16 [2304], P('dp'), may hold values from -3 to 3
- dense_weight: bfloat16 [768, 768], P('dp'), may hold values from -1.75 to 1.75
- dense_bias: bfloat16 [768], P('dp'), may hold values from -3 to 3
- fc1_weight: bfloat16 [768, 3072], P('dp'), may hold values from -0.21875 to 0.21875
- fc1_bias: bfloat16 [3072], P('dp'), may hold values from -3 to 3
- fc2_weight: bfloat16 [3072, 768], P('dp'), may hold values from -0.109375 to 0.109375
- fc2_bias: bfloat16 [768], P('dp'), may hold values from -3 to 3
- cotangent: bfloat16 [16, 1024, 768], P('dp', 'ctx'), may hold values from -6 to 6
Outputs:
- block_out: bfloat16 [16, 1024, 768], P('dp', 'ctx')
- input_grad: float32 [16, 1024, 768], P('dp', 'ctx')
- ln1_gain_grad: float32 [768], P('dp')
- ln1_bias_grad: float32 [768], P('dp')
- ln2_gain_grad: float32 [768], P('dp')
- ln2_bias_grad: float32 [768], P('dp')
- qkv_weight_grad: float32 [768, 2304], P('dp')
- qkv_bias_grad: float32 [2304], P('dp')
- dense_weight_grad: float32 [768, 768], P('dp')
- dense_bias_grad: float32 [768], P('dp')
- fc1_weight_grad: float32 [768, 3072], P('dp')
- fc1_bias_grad: float32 [3072], P('dp')
- fc2_weight_grad: float32 [3072, 768], P('dp')
- fc2_bias_grad: float32 [768], P('dp')
The draws below stay inside these ranges and needn't reach their ends.
Inputs may be any that keep to these rules, and one draw needn't show every extreme that they name: `doc_lengths`: each row lists the lengths of the 4 documents packed, in order, into one sequence, summing to 1024; in each row one document, at a position that varies from row to row, is long, and each of the others has 1 to 64 tokens; in the first row every short document has one token.
All inputs are finite; a program needn't handle non-finite values.
Results may differ from the reference program's by a relative error of at most 0.018.
The reference program's roundings to bfloat16 on the way count: a program that leaves them out, or rounds other values in their place, can miss the bound.
Values may be sent and summed in bfloat16 or wider, within the bound.
No kernel may reach another device: no remote copies, remote signals or barrier semaphores. Data moves between devices by JAX's collectives and lax.ppermute only.
A program may use at most 192 MiB of HBM per device.

```python
import math
import jax
import jax.numpy as jnp
from jax import lax

HEADS = 12
HEAD_DIM = 64
D = 768
FF = 3072
ROT = 16
DOCS = 4
BLOCK = 256
LENGTH = 1024
SEQS = 16


def draw_qkv_weight(key, part):
    normal_part = jax.random.truncated_normal(key, -4.0, 4.0, (D, 3 * D), jnp.float32) * D ** (-0.5)
    return normal_part.astype(jnp.bfloat16)


def draw_doc_lengths(key, part):
    short_docs = jax.random.randint(jax.random.fold_in(key, 3), (SEQS, DOCS), 1, BLOCK // 4 + 1, jnp.int32)
    row_number = jnp.arange(SEQS, dtype=jnp.int32)[:, None]
    short_docs = jnp.where(row_number == 0, jnp.ones_like(short_docs), short_docs)
    long_place = jax.random.randint(jax.random.fold_in(key, 5), (SEQS, 1), 0, DOCS, jnp.int32)
    column_number = jnp.arange(DOCS, dtype=jnp.int32)[None, :]
    is_long = column_number == long_place
    others = jnp.where(is_long, jnp.zeros_like(short_docs), short_docs)
    long_length = LENGTH - jnp.sum(others, axis=1, keepdims=True)
    return jnp.where(is_long, long_length, others).astype(jnp.int32)


def level_of(key, extent, split, low, top_value):
    gain = 1.0
    for position, shards_of in split:
        steps = jax.random.uniform(jax.random.fold_in(jax.random.fold_in(key, 6), position), (shards_of,), jnp.float32, low / len(split), top_value / len(split))
        gain = gain * jnp.repeat(jnp.exp(steps), extent[position] // shards_of).reshape((-1,) + (1,) * (len(extent) - 1 - position))
    return gain


def bell_draw(rng, extent, width, reach, cuts=(), kind=jnp.bfloat16):
    values = width * jax.random.normal(rng, extent, jnp.float32)
    if cuts:
        values = values * level_of(rng, extent, cuts, -0.22, 0.18)
    return jnp.clip(values, -reach, reach).astype(kind)


def setup_inputs(seed: int = 0) -> dict:
    key_list = jax.random.split(jax.random.key(seed), 16)
    hidden_in = bell_draw(key_list[0], (SEQS, LENGTH, D), 1.0, 6.0, ((0, 8), (1, 4)))
    doc_lengths = draw_doc_lengths(jax.random.fold_in(key_list[15], 71), 0)
    ln1_gain = jnp.clip(1.0 + 0.1 * jax.random.normal(key_list[2], (D,), jnp.float32), 0.5, 1.5).astype(jnp.bfloat16)
    ln1_bias = bell_draw(key_list[3], (D,), 0.5, 3.0, ((0, 8),))
    ln2_gain = jnp.clip(1.0 + 0.1 * jax.random.normal(key_list[4], (D,), jnp.float32), 0.5, 1.5).astype(jnp.bfloat16)
    ln2_bias = bell_draw(key_list[5], (D,), 0.5, 3.0, ((0, 8),))
    qkv_weight = draw_qkv_weight(jax.random.fold_in(key_list[15], 71), 0)
    qkv_bias = bell_draw(key_list[7], (3 * D,), 0.5, 3.0, ((0, 8),))
    dense_weight = bell_draw(key_list[8], (D, D), (D // 64) ** -0.5, 1.75, ((0, 8),))
    dense_bias = bell_draw(key_list[9], (D,), 0.5, 3.0, ((0, 8),))
    fc1_weight = bell_draw(key_list[10], (D, FF), D ** -0.5, 0.21875, ((0, 8),))
    fc1_bias = bell_draw(key_list[11], (FF,), 0.5, 3.0, ((0, 8),))
    fc2_weight = bell_draw(key_list[12], (FF, D), FF ** -0.5, 0.109375, ((0, 8),))
    fc2_bias = bell_draw(key_list[13], (D,), 0.5, 3.0, ((0, 8),))
    cotangent = bell_draw(key_list[14], (SEQS, LENGTH, D), 1.0, 6.0, ((0, 8), (1, 4)))
    return dict(hidden_in=hidden_in, doc_lengths=doc_lengths, ln1_gain=ln1_gain, ln1_bias=ln1_bias, ln2_gain=ln2_gain, ln2_bias=ln2_bias, qkv_weight=qkv_weight, qkv_bias=qkv_bias, dense_weight=dense_weight, dense_bias=dense_bias, fc1_weight=fc1_weight, fc1_bias=fc1_bias, fc2_weight=fc2_weight, fc2_bias=fc2_bias, cotangent=cotangent)


norm_eps = 1e-05
masked_score = -1e+30
root_half = 0.7071067811865476
inv_root_two_pi = 0.3989422804014327

def rounded(values):
    return lax.optimization_barrier(values.astype(jnp.bfloat16))

def layer_norm(values, norm_gain, norm_shift):
    centre = lax.optimization_barrier(jnp.mean(values, axis=-1, keepdims=True))
    centred = values - centre
    variance = lax.optimization_barrier(jnp.mean(centred * centred, axis=-1, keepdims=True))
    inverse = lax.rsqrt(variance + norm_eps)
    normed = centred * inverse
    return (normed * norm_gain + norm_shift, normed, inverse)

def norm_backward(upstream, norm_gain, normed, inverse):
    scaled = upstream * norm_gain
    residue = scaled - lax.optimization_barrier(jnp.mean(scaled, axis=-1, keepdims=True)) - normed * lax.optimization_barrier(jnp.mean(scaled * normed, axis=-1, keepdims=True))
    return (residue * inverse, lax.optimization_barrier(jnp.sum(upstream * normed, axis=0)), lax.optimization_barrier(jnp.sum(upstream, axis=0)))

def gelu_value(inputs):
    return 0.5 * inputs * (1.0 + lax.erf(inputs * root_half))

def gelu_slope(inputs):
    return 0.5 * (1.0 + lax.erf(inputs * root_half)) + inputs * jnp.exp(-0.5 * inputs * inputs) * inv_root_two_pi

def rotary_tables(positions, rotary):
    half_dims = rotary // 2
    frequency = jnp.exp(jnp.arange(half_dims, dtype=jnp.float32) * (-2.0 * math.log(10000.0) / rotary))
    angles = positions.astype(jnp.float32)[:, None] * frequency[None, :]
    return (jnp.cos(angles), jnp.sin(angles))

def rotate(heads_in, cosine_table, sine_table, direction):
    half_dims = cosine_table.shape[-1]
    cos_grid = cosine_table[:, None, :]
    sin_grid = direction * sine_table[:, None, :]
    first_half = heads_in[..., :half_dims]
    second_half = heads_in[..., half_dims:2 * half_dims]
    return jnp.concatenate([first_half * cos_grid - second_half * sin_grid, second_half * cos_grid + first_half * sin_grid, heads_in[..., 2 * half_dims:]], axis=-1)

def segment_ids(lengths, positions):
    bounds = jnp.cumsum(lengths, axis=1)[:, :-1]
    return lax.optimization_barrier(jnp.sum((positions[None, :, None] >= bounds[:, None, :]).astype(jnp.int32), axis=2))

def reference(hidden_in, doc_lengths, ln1_gain, ln1_bias, ln2_gain, ln2_bias, qkv_weight, qkv_bias, dense_weight, dense_bias, fc1_weight, fc1_bias, fc2_weight, fc2_bias, cotangent):
    model_width = HEADS * HEAD_DIM
    qk_scale = HEAD_DIM ** (-0.5)
    query_len = math.gcd(LENGTH, 512)
    block_count = LENGTH // query_len
    positions = jnp.arange(LENGTH, dtype=jnp.int32)
    cosine_table, sine_table = rotary_tables(positions, ROT)
    first_gain = ln1_gain.astype(jnp.float32)
    first_shift = ln1_bias.astype(jnp.float32)
    second_gain = ln2_gain.astype(jnp.float32)
    second_shift = ln2_bias.astype(jnp.float32)
    qkv_shift = qkv_bias.astype(jnp.float32)
    dense_shift = dense_bias.astype(jnp.float32)
    upper_shift = fc1_bias.astype(jnp.float32)
    lower_shift = fc2_bias.astype(jnp.float32)

    def one_sequence(grad_sums, member):
        seq_in, seq_lengths, seq_cot = member
        segments = segment_ids(seq_lengths[None, :], positions)[0]
        inputs = seq_in.astype(jnp.float32)
        first_out, first_normed, first_inverse = layer_norm(inputs, first_gain, first_shift)
        second_out, second_normed, second_inverse = layer_norm(inputs, second_gain, second_shift)
        attn_in = rounded(first_out)
        mlp_in = rounded(second_out)
        projected = jnp.dot(attn_in, qkv_weight, preferred_element_type=jnp.float32) + qkv_shift
        query_heads = rounded(rotate(projected[:, :model_width].reshape(LENGTH, HEADS, HEAD_DIM), cosine_table, sine_table, 1.0))
        key_heads = rounded(rotate(projected[:, model_width:2 * model_width].reshape(LENGTH, HEADS, HEAD_DIM), cosine_table, sine_table, 1.0))
        value_heads = rounded(projected[:, 2 * model_width:].reshape(LENGTH, HEADS, HEAD_DIM))
        key_wide = key_heads.astype(jnp.float32)
        value_wide = value_heads.astype(jnp.float32)

        def block_scores(row_start):
            query_blk = lax.dynamic_slice_in_dim(query_heads, row_start, query_len, 0).astype(jnp.float32)
            pos_blk = row_start + jnp.arange(query_len, dtype=jnp.int32)
            seg_blk = lax.dynamic_slice_in_dim(segments, row_start, query_len, 0)
            allowed = ((positions[None, :] <= pos_blk[:, None]) & (segments[None, :] == seg_blk[:, None]))[None]
            raw_scores = jnp.einsum('qhd,khd->hqk', query_blk, key_wide) * qk_scale
            return (jnp.where(allowed, raw_scores, masked_score), allowed, query_blk)

        def forward_block(number):
            scores, allowed, query_blk = block_scores(number * query_len)
            row_max = lax.optimization_barrier(jnp.max(scores, axis=-1))
            row_total = lax.optimization_barrier(jnp.sum(jnp.where(allowed, jnp.exp(scores - row_max[..., None]), 0.0), axis=-1))
            log_total = row_max + jnp.log(row_total)
            soft_weights = rounded(jnp.where(allowed, jnp.exp(scores - log_total[..., None]), 0.0))
            mixed = jnp.einsum('hqk,khd->qhd', soft_weights.astype(jnp.float32), value_wide)
            return (rounded(mixed), jnp.transpose(log_total))
        attended_blocks, lse_blocks = lax.map(forward_block, jnp.arange(block_count, dtype=jnp.int32))
        attended_heads = attended_blocks.reshape(LENGTH, HEADS, HEAD_DIM)
        log_total = lse_blocks.reshape(LENGTH, HEADS)
        lse_high = rounded(log_total)
        lse_low = rounded(log_total - lse_high.astype(jnp.float32))
        lse_used = lse_high.astype(jnp.float32) + lse_low.astype(jnp.float32)
        attended = attended_heads.reshape(LENGTH, model_width)
        attn_out = jnp.dot(attended, dense_weight, preferred_element_type=jnp.float32) + dense_shift
        upper = jnp.dot(mlp_in, fc1_weight, preferred_element_type=jnp.float32) + upper_shift
        activated = rounded(gelu_value(upper))
        lower = jnp.dot(activated, fc2_weight, preferred_element_type=jnp.float32) + lower_shift
        block_out = (inputs + attn_out + lower).astype(jnp.bfloat16)
        upstream_f = seq_cot.astype(jnp.float32)
        grad_lower_shift = lax.optimization_barrier(jnp.sum(upstream_f, axis=0))
        grad_lower = jnp.dot(activated.T, seq_cot, preferred_element_type=jnp.float32)
        grad_dense = jnp.dot(attended.T, seq_cot, preferred_element_type=jnp.float32)
        upper_grad = jnp.dot(seq_cot, fc2_weight.T, preferred_element_type=jnp.float32) * gelu_slope(upper)
        grad_upper_shift = lax.optimization_barrier(jnp.sum(upper_grad, axis=0))
        upper_grad_b = rounded(upper_grad)
        grad_upper = jnp.dot(mlp_in.T, upper_grad_b, preferred_element_type=jnp.float32)
        mlp_back = jnp.dot(upper_grad_b, fc1_weight.T, preferred_element_type=jnp.float32)
        out_grad = rounded(jnp.dot(seq_cot, dense_weight.T, preferred_element_type=jnp.float32)).reshape(LENGTH, HEADS, HEAD_DIM)
        out_wide = out_grad.astype(jnp.float32)
        delta = lax.optimization_barrier(jnp.sum(out_wide * attended_heads.astype(jnp.float32), axis=-1))

        def backward_block(carried, number):
            grad_k, grad_v = carried
            row_start = number * query_len
            scores, allowed, query_blk = block_scores(row_start)
            dout_blk = lax.dynamic_slice_in_dim(out_wide, row_start, query_len, 0)
            lse_blk = jnp.transpose(lax.dynamic_slice_in_dim(lse_used, row_start, query_len, 0))
            delta_blk = jnp.transpose(lax.dynamic_slice_in_dim(delta, row_start, query_len, 0))
            weights_back = jnp.where(allowed, jnp.exp(scores - lse_blk[..., None]), 0.0)
            grad_v = grad_v + jnp.einsum('hqk,qhd->khd', rounded(weights_back).astype(jnp.float32), dout_blk)
            prob_grad = jnp.einsum('qhd,khd->hqk', dout_blk, value_wide)
            score_grad = rounded(weights_back * (prob_grad - delta_blk[..., None]) * qk_scale).astype(jnp.float32)
            grad_q_blk = jnp.einsum('hqk,khd->qhd', score_grad, key_wide)
            grad_k = grad_k + jnp.einsum('hqk,qhd->khd', score_grad, query_blk)
            return ((grad_k, grad_v), grad_q_blk)
        zero_heads = jnp.zeros((LENGTH, HEADS, HEAD_DIM), jnp.float32)
        (grad_k, grad_v), grad_q_blocks = lax.scan(backward_block, (zero_heads, zero_heads), jnp.arange(block_count, dtype=jnp.int32))
        grad_q = grad_q_blocks.reshape(LENGTH, HEADS, HEAD_DIM)
        raw_q = rotate(grad_q, cosine_table, sine_table, -1.0).reshape(LENGTH, model_width)
        raw_k = rotate(grad_k, cosine_table, sine_table, -1.0).reshape(LENGTH, model_width)
        qkv_grad = jnp.concatenate([raw_q, raw_k, grad_v.reshape(LENGTH, model_width)], axis=1)
        grad_qkv_shift = lax.optimization_barrier(jnp.sum(qkv_grad, axis=0))
        qkv_grad_b = rounded(qkv_grad)
        grad_qkv = jnp.dot(attn_in.T, qkv_grad_b, preferred_element_type=jnp.float32)
        attn_back = jnp.dot(qkv_grad_b, qkv_weight.T, preferred_element_type=jnp.float32)
        first_part, grad_first_gain, grad_first_shift = norm_backward(attn_back, first_gain, first_normed, first_inverse)
        second_part, grad_second_gain, grad_second_shift = norm_backward(mlp_back, second_gain, second_normed, second_inverse)
        input_grad = upstream_f + first_part + second_part
        terms = (grad_first_gain, grad_first_shift, grad_second_gain, grad_second_shift, grad_qkv, grad_qkv_shift, grad_dense, grad_lower_shift, grad_upper, grad_upper_shift, grad_lower, grad_lower_shift)
        return (jax.tree.map(jnp.add, grad_sums, terms), (block_out, input_grad))
    model_shapes = ((D,), (D,), (D,), (D,), (D, 3 * D), (3 * D,), (D, D), (D,), (D, FF), (FF,), (FF, D), (D,))
    start_sums = tuple((jnp.zeros(shape_one, jnp.float32) for shape_one in model_shapes))
    grad_sums, (block_out, input_grad) = lax.scan(one_sequence, start_sums, (hidden_in, doc_lengths, cotangent))
    return (block_out, input_grad, grad_sums[0], grad_sums[1], grad_sums[2], grad_sums[3], grad_sums[4], grad_sums[5], grad_sums[6], grad_sums[7], grad_sums[8], grad_sums[9], grad_sums[10], grad_sums[11])
```

```python
import functools
import math

import jax
import jax.numpy as jnp
from jax import lax
from jax.experimental import pallas as pl
from jax.experimental.pallas import tpu as pltpu
from jax.sharding import Mesh
from jax.sharding import PartitionSpec as P

HEADS = 12
ROT = 16
TP = 4

norm_eps = 1e-05
far = -1e30
root_half = 0.7071067811865476
inv_root_two_pi = 0.3989422804014327
F32 = jnp.float32
BF16 = jnp.bfloat16


def dot(a, b):
    return jnp.dot(a, b, preferred_element_type=F32)


def dot_nt(a, b):
    return lax.dot_general(a, b, (((1,), (1,)), ((), ())), preferred_element_type=F32)


def dot_tn(a, b):
    return lax.dot_general(a, b, (((0,), (0,)), ((), ())), preferred_element_type=F32)


def gelu_value(inputs):
    return 0.5 * inputs * (1.0 + lax.erf(inputs * root_half))


def gelu_slope(inputs):
    return (
        0.5 * (1.0 + lax.erf(inputs * root_half))
        + inputs * jnp.exp(-0.5 * inputs * inputs) * inv_root_two_pi
    )


def norm_parts(values):
    centre = jnp.mean(values, axis=-1, keepdims=True)
    centred = values - centre
    variance = jnp.mean(centred * centred, axis=-1, keepdims=True)
    inverse = lax.rsqrt(variance + norm_eps)
    return centred * inverse, inverse


class Dims:
    def __init__(self, head_dim, docs, block):
        self.nh = HEADS // TP
        self.hd = head_dim
        self.hw = self.nh * head_dim
        self.docs = docs
        extra = max(docs + 2 * self.nh, 3 * self.nh)
        self.width = -(-(self.hw + extra) // 128) * 128
        self.block = block
        self.scale = head_dim ** (-0.5)


def turn(values, cos, sin, lane, d, direction):
    half = ROT // 2
    ahead = pltpu.roll(values, d.width - half, 1)
    behind = pltpu.roll(values, half, 1)
    partner = jnp.where(lane % d.hd < half, -ahead, behind)
    return values * cos + partner * (sin * direction)


def head_mask(lane, h, d):
    return (lane >= h * d.hd) & (lane < (h + 1) * d.hd)


def forward_kernel(
    d, bounds, x, gain, shift, w, bias, cos, sin, normed_out, q_out, k_out, v_out, att_out
):
    seq = pl.program_id(0)
    length = x.shape[1]
    blk, wd = d.block, d.width
    lane = lax.broadcasted_iota(jnp.int32, (blk, wd), 1)
    row = lax.broadcasted_iota(jnp.int32, (blk, wd), 0)
    row_s = lax.broadcasted_iota(jnp.int32, (blk, blk), 0)
    col_s = lax.broadcasted_iota(jnp.int32, (blk, blk), 1)
    lse_lane = d.hw + d.docs
    for i in range(length // blk):
        rows = pl.ds(i * blk, blk)
        normed, _ = norm_parts(x[0, rows, :].astype(F32))
        a = (normed * gain[...] + shift[...]).astype(BF16)
        normed_out[0, rows, :] = a
        proj = dot(a, w[...]) + bias[...]
        c, s = cos[rows, :], sin[rows, :]
        q = turn(proj[:, :wd], c, s, lane, d, 1.0).astype(BF16).astype(F32) * d.scale
        k = turn(proj[:, wd : 2 * wd], c, s, lane, d, 1.0)
        v = proj[:, 2 * wd :]
        pos = row + i * blk
        seg = jnp.zeros((blk, wd), jnp.int32)
        start = 0
        for n in range(d.docs - 1):
            start = start + bounds[seq, n]
            seg = seg + (pos >= start).astype(jnp.int32)
        same = (lane - d.hw) == seg
        in_seg = (lane >= d.hw) & (lane < lse_lane)
        q = jnp.where(lane < d.hw, q, jnp.where(in_seg & same, 1.0, 0.0))
        k = jnp.where(
            lane < d.hw,
            k,
            jnp.where(
                in_seg,
                jnp.where(same, 0.0, far),
                jnp.where(lane < lse_lane + 2 * d.nh, 1.0, 0.0),
            ),
        )
        v = jnp.where(lane < d.hw, v, jnp.where(lane < d.hw + 3 * d.nh, 1.0, 0.0))
        k_out[0, rows, :] = k.astype(BF16)
        v_out[0, rows, :] = v.astype(BF16)
        total = jnp.zeros((blk, wd), F32)
        q_final = q
        for h in range(d.nh):
            mine = head_mask(lane, h, d)
            qh = jnp.where(mine | in_seg, q, 0.0).astype(BF16)
            near = dot_nt(qh, k_out[0, rows, :])
            near = jnp.where(col_s <= row_s, near, far)
            top = jnp.max(near, axis=1, keepdims=True)
            if i:
                past = dot_nt(qh, k_out[0, : i * blk, :])
                top = jnp.maximum(top, jnp.max(past, axis=1, keepdims=True))
            near = jnp.exp(near - top)
            count = jnp.sum(near, axis=1, keepdims=True)
            mixed = dot(near.astype(BF16), v_out[0, rows, :])
            if i:
                past = jnp.exp(past - top)
                count = count + jnp.sum(past, axis=1, keepdims=True)
                mixed = mixed + dot(past.astype(BF16), v_out[0, : i * blk, :])
            total = jnp.where(mine, mixed / count, total)
            lse = top + jnp.log(count)
            high = lse.astype(BF16).astype(F32)
            low = lse - high
            q_final = jnp.where(lane == lse_lane + 2 * h, -high, q_final)
            q_final = jnp.where(lane == lse_lane + 2 * h + 1, -low, q_final)
        q_out[0, rows, :] = q_final.astype(BF16)
        att_out[0, rows, :] = total.astype(BF16)


def backward_kernel(
    d, cot, dense, att, q_in, k_in, v_in, cos, sin, grad_out, bias_out, dout, douth, qh, dq
):
    length = cot.shape[1]
    blk, wd = d.block, d.width
    nb = length // blk
    lane = lax.broadcasted_iota(jnp.int32, (blk, wd), 1)
    row_s = lax.broadcasted_iota(jnp.int32, (blk, blk), 0)
    col_s = lax.broadcasted_iota(jnp.int32, (blk, blk), 1)
    lse_lane = d.hw + d.docs
    in_seg = (lane >= d.hw) & (lane < lse_lane)
    for i in range(nb):
        rows = pl.ds(i * blk, blk)
        og = dot_nt(cot[0, rows, :], dense[...]).astype(BF16).astype(F32)
        both = og * att[0, rows, :].astype(F32)
        full = og
        q = q_in[0, rows, :].astype(F32)
        for h in range(d.nh):
            mine = head_mask(lane, h, d)
            delta = jnp.sum(jnp.where(mine, both, 0.0), axis=1, keepdims=True)
            for piece in range(3):
                part = delta.astype(BF16).astype(F32)
                delta = delta - part
                full = jnp.where(lane == d.hw + 3 * h + piece, -part, full)
            douth[h, rows, :] = jnp.where(mine, og, 0.0).astype(BF16)
            qh[h, rows, :] = jnp.where(mine, q, 0.0).astype(BF16)
        dout[rows, :] = full.astype(BF16)
    dq[...] = jnp.zeros_like(dq)
    sums_k = jnp.zeros((1, wd), F32)
    sums_v = jnp.zeros((1, wd), F32)
    for j in range(nb):
        rows = pl.ds(j * blk, blk)
        rest = pl.ds(j * blk, length - j * blk)
        k = k_in[0, rows, :]
        v = v_in[0, rows, :]
        dk = jnp.zeros((blk, wd), F32)
        dv = jnp.zeros((blk, wd), F32)
        for h in range(d.nh):
            mine = head_mask(lane, h, d)
            lse_mine = (lane >= lse_lane + 2 * h) & (lane < lse_lane + 2 * h + 2)
            delta_mine = (lane >= d.hw + 3 * h) & (lane < d.hw + 3 * h + 3)
            kh = jnp.where(mine | in_seg | lse_mine, k.astype(F32), 0.0).astype(BF16)
            vh = jnp.where(mine | delta_mine, v.astype(F32), 0.0).astype(BF16)
            st = dot_nt(kh, q_in[0, rest, :])
            dp = dot_nt(vh, dout[rest, :])
            first = jnp.where(col_s >= row_s, st[:, :blk], far)
            if j < nb - 1:
                st = jnp.concatenate([first, st[:, blk:]], axis=1)
            else:
                st = first
            p = jnp.exp(st)
            ds = (p * dp).astype(BF16)
            dv = dv + dot(p.astype(BF16), douth[h, rest, :])
            dk = dk + dot(ds, qh[h, rest, :])
            dq[rest, :] += dot_tn(ds, kh)
        dk = turn(dk, cos[rows, :], sin[rows, :], lane, d, -1.0)
        sums_k = sums_k + jnp.sum(dk, axis=0, keepdims=True)
        sums_v = sums_v + jnp.sum(dv, axis=0, keepdims=True)
        grad_out[0, rows, wd : 2 * wd] = dk.astype(BF16)
        grad_out[0, rows, 2 * wd :] = dv.astype(BF16)
    sums_q = jnp.zeros((1, wd), F32)
    for i in range(nb):
        rows = pl.ds(i * blk, blk)
        part = jnp.where(lane < d.hw, dq[rows, :], 0.0) * d.scale
        part = turn(part, cos[rows, :], sin[rows, :], lane, d, -1.0)
        sums_q = sums_q + jnp.sum(part, axis=0, keepdims=True)
        grad_out[0, rows, :wd] = part.astype(BF16)
    bias_out[0] = jnp.broadcast_to(
        jnp.concatenate([sums_q, sums_k, sums_v], axis=1), bias_out.shape[1:]
    )


def whole(shape):
    return pl.BlockSpec(shape, lambda *_: (0,) * len(shape))


def per_seq(shape):
    return pl.BlockSpec((1,) + shape, lambda s, *_: (s,) + (0,) * len(shape))


def attention_forward(d, lengths, x, gain, shift, w, bias, cos, sin):
    seqs, length, model = x.shape
    wd = d.width
    row_type = jax.ShapeDtypeStruct((seqs, length, wd), BF16)
    pairs = seqs * d.nh * length * length // 2
    return pl.pallas_call(
        functools.partial(forward_kernel, d),
        grid_spec=pltpu.PrefetchScalarGridSpec(
            num_scalar_prefetch=1,
            grid=(seqs,),
            in_specs=[
                per_seq((length, model)),
                whole((1, model)),
                whole((1, model)),
                whole((model, 3 * wd)),
                whole((1, 3 * wd)),
                whole((length, wd)),
                whole((length, wd)),
            ],
            out_specs=[per_seq((length, model))] + [per_seq((length, wd))] * 4,
        ),
        out_shape=[jax.ShapeDtypeStruct(x.shape, BF16)] + [row_type] * 4,
        cost_estimate=pl.CostEstimate(
            flops=2 * seqs * length * model * 3 * wd + 4 * pairs * wd,
            bytes_accessed=seqs * length * (4 * model + 8 * wd),
            transcendentals=pairs,
        ),
        name="attention_forward",
    )(lengths, x, gain, shift, w, bias, cos, sin)


def attention_backward(d, cot, dense, att, q, k, v, cos, sin):
    seqs, length, model = cot.shape
    wd = d.width
    pairs = seqs * d.nh * length * length // 2
    return pl.pallas_call(
        functools.partial(backward_kernel, d),
        grid=(seqs,),
        in_specs=[per_seq((length, model)), whole((wd, model))]
        + [per_seq((length, wd))] * 4
        + [whole((length, wd))] * 2,
        out_specs=[per_seq((length, 3 * wd)), per_seq((8, 3 * wd))],
        out_shape=[
            jax.ShapeDtypeStruct((seqs, length, 3 * wd), BF16),
            jax.ShapeDtypeStruct((seqs, 8, 3 * wd), F32),
        ],
        scratch_shapes=[
            pltpu.VMEM((length, wd), BF16),
            pltpu.VMEM((d.nh, length, wd), BF16),
            pltpu.VMEM((d.nh, length, wd), BF16),
            pltpu.VMEM((length, wd), F32),
        ],
        cost_estimate=pl.CostEstimate(
            flops=2 * seqs * length * model * wd + 10 * pairs * wd,
            bytes_accessed=seqs * length * (2 * model + 14 * wd),
            transcendentals=pairs,
        ),
        name="attention_backward",
    )(cot, dense, att, q, k, v, cos, sin)


def pick(values, index, axis=0):
    return lax.dynamic_index_in_dim(values, index, axis, keepdims=False)


def ordered(own, other, index, axis):
    return jnp.where(
        index == 0, jnp.stack([own, other], axis), jnp.stack([other, own], axis)
    )


def swap(values, axis):
    return lax.ppermute(values, axis, [(0, 1), (1, 0)])


def shards(
    sizes,
    hidden_in,
    doc_lengths,
    ln1_gain,
    ln1_bias,
    ln2_gain,
    ln2_bias,
    qkv_weight,
    qkv_bias,
    dense_weight,
    dense_bias,
    fc1_weight,
    fc1_bias,
    fc2_weight,
    fc2_bias,
    cotangent,
):
    nz, ny = sizes
    zi, ci = lax.axis_index("z"), lax.axis_index("core")
    yi, xi = lax.axis_index("y"), lax.axis_index("x")
    peer = 1 - ci
    seqs, block, model = hidden_in.shape
    rows = ln1_gain.shape[0]
    hidden = fc1_weight.shape[1]
    piece = hidden // (nz * TP)
    d = Dims(model // HEADS, doc_lengths.shape[1], block)
    hw, wd = d.hw, d.width
    length = block * ny * 2
    direct = ny == 2 and seqs % 2 == 0
    group = 2 * seqs // ny
    tokens = group * length

    def over_z(chunk):
        if nz == 1:
            return chunk[None]
        gathered = jnp.zeros((nz,) + chunk.shape, chunk.dtype)
        gathered = lax.dynamic_update_index_in_dim(gathered, chunk, zi, 0)
        for k in range(1, nz):
            got = lax.ppermute(chunk, "z", [(i, (i + k) % nz) for i in range(nz)])
            gathered = lax.dynamic_update_index_in_dim(gathered, got, (zi - k) % nz, 0)
        return gathered

    def sum_z(parts):
        total = pick(parts, zi).astype(F32)
        for k in range(1, nz):
            sent = pick(parts, (zi + k) % nz)
            got = lax.ppermute(sent, "z", [(i, (i + k) % nz) for i in range(nz)])
            total = total + got.astype(F32)
        return total.astype(BF16)

    def sum_y(part):
        if ny == 2:
            return (part.astype(F32) + swap(part, "y").astype(F32)).astype(BF16)
        return lax.psum(part, "y")

    def gather_tokens(values):
        if direct:
            halves = values.reshape(ny, seqs // ny, block, model)
            got = swap(pick(halves, 1 - yi), "y")
            mine = ordered(pick(halves, yi), got, yi, 1)
            got = swap(mine, "x")
            mine = ordered(mine, got, xi, 2).reshape(group // 2, length, model)
            got = swap(mine, "core")
            return jnp.concatenate([mine, got], axis=0)
        plane = lax.all_gather(values, "core", axis=0, tiled=True)
        plane = lax.all_gather(plane, ("y", "x"), axis=1, tiled=True)
        return lax.dynamic_slice_in_dim(plane, yi * group, group, 0)

    def scatter_tokens(values):
        if direct:
            values = values.reshape(2, group // 2, ny, 2, block, model)
            total = values[0].astype(F32) + swap(values[1], "core").astype(F32)
            got = swap(pick(total, 1 - xi, 2).astype(BF16), "x")
            total = (pick(total, xi, 2) + got.astype(F32)).astype(BF16)
            got = swap(pick(total, 1 - yi, 1), "y")
            return ordered(pick(total, yi, 1), got, yi, 0).reshape(seqs, block, model)
        plane = jnp.zeros((2 * seqs, length, model), BF16)
        plane = lax.dynamic_update_slice_in_dim(plane, values, yi * group, 0)
        plane = lax.psum_scatter(plane, "core", scatter_dimension=0, tiled=True)
        return lax.psum_scatter(plane, ("y", "x"), scatter_dimension=1, tiled=True)

    x = gather_tokens(hidden_in)

    def columns(matrix, core):
        return matrix.reshape(rows, nz, 2, 2, piece)[:, :, core, xi, :].reshape(rows, nz * piece)

    fc1_mine = ordered(columns(fc1_weight, ci), swap(columns(fc1_weight, peer), "core"), ci, 0)
    fc1_chunk = fc1_mine.reshape(2 * rows, nz * piece)
    heads_split = qkv_weight.reshape(rows, 3, TP, hw)
    qkv_mine = ordered(
        pick(heads_split, 2 * ci + xi, 2).reshape(rows, 3 * hw),
        swap(pick(heads_split, 2 * peer + xi, 2).reshape(rows, 3 * hw), "core"),
        ci,
        0,
    )
    qkv_chunk = qkv_mine.reshape(2 * rows, 3 * hw)
    small = jnp.concatenate(
        [
            ln1_gain,
            ln1_bias,
            ln2_gain,
            ln2_bias,
            dense_bias,
            fc2_bias,
            qkv_bias,
            fc1_bias,
        ]
    )
    small = ordered(small, swap(small, "core"), ci, 0)
    small_len = small.size
    small_rows = -(-small_len // (nz * piece * 16)) * 16
    small = jnp.pad(small.reshape(-1), (0, small_rows * nz * piece - small_len))
    fc1_chunk = jnp.concatenate([fc1_chunk, small.reshape(small_rows, nz * piece)], axis=0)
    fc1_all = over_z(fc1_chunk)
    upper_matrix = fc1_all[:, : 2 * rows, :].reshape(model, nz * piece)
    small = fc1_all[:, 2 * rows :, :].reshape(nz, -1)[:, :small_len].reshape(nz, 2, -1)

    def vector(start, size):
        return small[:, :, start : start + size].reshape(-1).astype(F32)

    first_gain, first_shift, second_gain, second_shift, dense_shift, lower_shift = (
        vector(n * rows, rows) for n in range(6)
    )
    qkv_shift = vector(6 * rows, 3 * rows).reshape(3, TP, hw)
    qkv_shift = pick(qkv_shift, 2 * ci + xi, 1)
    upper_shift = vector(9 * rows, hidden // (2 * nz)).reshape(nz, 2, 2, piece)
    upper_shift = upper_shift[:, ci, xi, :].reshape(1, nz * piece)

    fc2_chunk = pick(fc2_weight.reshape(2, piece, model), xi)
    low_all = over_z(jnp.concatenate([fc2_chunk, dense_weight], axis=0))
    lower_matrix = low_all[:, :piece].reshape(nz * piece, model)
    dense_mine = low_all[:, piece:]
    dense_all = ordered(dense_mine, swap(dense_mine, "core"), ci, 1).reshape(TP, hw, model)
    dense_matrix = pick(dense_all, 2 * ci + xi)
    dense_pad = jnp.pad(dense_matrix, ((0, wd - hw), (0, 0)))

    qkv_all = over_z(qkv_chunk).reshape(model, 3, hw)
    qkv_pad = jnp.pad(qkv_all, ((0, 0), (0, 0), (0, wd - hw))).reshape(model, 3 * wd)
    qkv_shift = jnp.pad(qkv_shift, ((0, 0), (0, wd - hw))).reshape(1, 3 * wd)

    cot = gather_tokens(cotangent)

    lane = jnp.arange(wd, dtype=jnp.int32)
    feature = lane % d.hd
    turned = (lane < hw) & (feature < ROT)
    frequency = jnp.exp(
        (feature % (ROT // 2)).astype(F32) * (-2.0 * math.log(10000.0) / ROT)
    )
    angles = jnp.arange(length, dtype=F32)[:, None] * frequency[None, :]
    cos = jnp.where(turned[None, :], jnp.cos(angles), 1.0)
    sin = jnp.where(turned[None, :], jnp.sin(angles), 0.0)

    if direct:
        lengths_mine = pick(doc_lengths.reshape(ny, seqs // ny, -1), yi)
        lengths_peer = swap(pick(doc_lengths.reshape(ny, seqs // ny, -1), yi), "core")
        lengths = jnp.concatenate([lengths_mine, lengths_peer], axis=0)
    else:
        lengths = lax.all_gather(doc_lengths, "core", axis=0, tiled=True)
        lengths = lax.dynamic_slice_in_dim(lengths, yi * group, group, 0)

    attn_in, q, k, v, att = attention_forward(
        d,
        lengths,
        x,
        first_gain[None, :],
        first_shift[None, :],
        qkv_pad,
        qkv_shift,
        cos,
        sin,
    )

    x_flat = x.reshape(tokens, model)
    cot_flat = cot.reshape(tokens, model)
    normed, _ = norm_parts(x_flat.astype(F32))
    mlp_in = (normed * second_gain + second_shift).astype(BF16)
    upper = dot(mlp_in, upper_matrix) + upper_shift
    activated = gelu_value(upper).astype(BF16)
    att_flat = att.reshape(tokens, wd)
    out_part = (dot(activated, lower_matrix) + dot(att_flat, dense_pad)).astype(BF16)
    out_mine = scatter_tokens(out_part.reshape(group, length, model))
    block_out = (
        hidden_in.astype(F32) + out_mine.astype(F32) + (dense_shift + lower_shift)
    ).astype(BF16)

    upper_grad = dot_nt(cot_flat, lower_matrix) * gelu_slope(upper)
    grad_upper_shift = jnp.sum(upper_grad, axis=0)
    upper_grad_b = upper_grad.astype(BF16)
    grad_lower = dot_tn(activated, cot_flat).astype(BF16).reshape(nz, piece, model)
    grad_upper = dot_tn(mlp_in, upper_grad_b).astype(BF16).reshape(nz, 2 * rows, nz * piece)
    if nz * piece == model:
        both = sum_y(sum_z(jnp.concatenate([grad_upper, grad_lower], axis=1)))
        grad_upper, grad_lower = both[: 2 * rows], both[2 * rows :]
    else:
        grad_upper, grad_lower = sum_y(sum_z(grad_upper)), sum_y(sum_z(grad_lower))
    mlp_back = dot_nt(upper_grad_b, upper_matrix)

    grad_b, bias_parts = attention_backward(d, cot, dense_pad, att, q, k, v, cos, sin)
    grad_flat = grad_b.reshape(tokens, 3 * wd)
    attn_back = dot_nt(grad_flat, qkv_pad)
    grad_qkv = dot_tn(attn_in.reshape(tokens, model), grad_flat).astype(BF16)
    grad_qkv = grad_qkv.reshape(model, 3, wd)[:, :, :hw].reshape(nz, 2 * rows, 3 * hw)
    grad_dense = dot_tn(att_flat, cot_flat)[:hw].astype(BF16)

    split = grad_dense.reshape(hw, 2, 2, hw)
    part = split[:, ci].reshape(hw, 2, hw)
    got = swap(split[:, peer], "core")
    part = ordered(part, got, ci, 0)
    got = swap(pick(part, 1 - xi, 2), "x")
    part = ordered(pick(part, xi, 2), got, xi, 1)
    grad_dense = part.reshape(nz, 2 * rows, hw)

    first_grads = [jnp.sum(attn_back * normed, axis=0), jnp.sum(attn_back, axis=0)]
    second_grads = [jnp.sum(mlp_back * normed, axis=0), jnp.sum(mlp_back, axis=0)]
    grad_shift = jnp.sum(cotangent.astype(F32), axis=(0, 1))
    grad_qkv_shift = jnp.sum(bias_parts[:, 0], axis=0).reshape(3, wd)[:, :hw].reshape(-1)
    vectors = jnp.concatenate(
        first_grads + second_grads + [grad_shift, grad_upper_shift, grad_qkv_shift]
    ).astype(BF16)
    cols = 4 * hw
    vector_rows = -(-vectors.size // (cols * 16)) * 16
    vectors = jnp.pad(vectors, (0, vector_rows * cols - vectors.size)).reshape(vector_rows, cols)
    chunk = jnp.concatenate([grad_qkv, grad_dense], axis=2)
    chunk = jnp.concatenate([chunk, jnp.broadcast_to(vectors, (nz,) + vectors.shape)], axis=1)
    chunk = sum_y(sum_z(chunk))

    def rows_of(part, extra):
        halves = part[: 2 * rows].reshape(2, rows, part.shape[1])
        sent = jnp.concatenate([pick(halves, peer), extra], axis=0)
        own = jnp.concatenate([pick(halves, ci), extra], axis=0)
        pair = ordered(own, swap(sent, "core"), ci, 0)
        return ordered(pair, swap(pair, "x"), xi, 1)

    tail = rows_of(chunk, chunk[2 * rows :]).astype(F32)
    parts = tail[:, :, :rows]
    out_qkv = parts[..., : 3 * hw].reshape(TP, rows, 3, hw)
    out_qkv = jnp.transpose(out_qkv, (1, 2, 0, 3)).reshape(rows, 3 * model)
    out_dense = parts[..., 3 * hw :].reshape(TP, rows, hw)
    out_dense = jnp.transpose(out_dense, (1, 0, 2)).reshape(rows, model)
    flat = tail[:, :, rows:].reshape(TP, -1)
    summed = flat[0] + flat[1] + flat[2] + flat[3]
    mine = zi * 2 + ci

    def own_rows(n):
        return lax.dynamic_slice_in_dim(summed, n * model + mine * rows, rows)

    out_upper_shift = flat[:, 5 * model : 5 * model + nz * piece].reshape(2, 2, nz, piece)
    out_upper_shift = pick(pick(out_upper_shift, ci), zi, 1).reshape(-1)
    at = 5 * model + nz * piece
    out_qkv_shift = flat[:, at : at + 3 * hw].reshape(TP, 3, hw)
    out_qkv_shift = jnp.transpose(out_qkv_shift, (1, 0, 2)).reshape(-1)
    out_qkv_shift = lax.dynamic_slice_in_dim(out_qkv_shift, mine * 3 * rows, 3 * rows)

    out_upper = rows_of(grad_upper, grad_upper[:0]).astype(F32)
    out_upper = out_upper.reshape(2, 2, rows, nz, piece)
    out_upper = jnp.transpose(out_upper, (2, 3, 0, 1, 4)).reshape(rows, hidden)
    out_lower = ordered(grad_lower, swap(grad_lower, "x"), xi, 0)
    out_lower = out_lower.reshape(2 * piece, model).astype(F32)

    scaled = attn_back * first_gain + mlp_back * second_gain
    scaled = scatter_tokens(scaled.astype(BF16).reshape(group, length, model)).astype(F32)
    normed, inverse = norm_parts(hidden_in.astype(F32))
    residue = (
        scaled
        - jnp.mean(scaled, axis=-1, keepdims=True)
        - normed * jnp.mean(scaled * normed, axis=-1, keepdims=True)
    )
    input_grad = cotangent.astype(F32) + residue * inverse
    return (
        block_out,
        input_grad,
        own_rows(0),
        own_rows(1),
        own_rows(2),
        own_rows(3),
        out_qkv,
        out_qkv_shift,
        out_dense,
        own_rows(4),
        out_upper,
        out_upper_shift,
        out_lower,
        own_rows(4),
    )


def solution(mesh):
    nz, ny = mesh.shape["dp"] // 2, mesh.shape["ctx"] // 2
    fine = Mesh(mesh.devices.reshape(nz, 2, ny, 2), ("z", "core", "y", "x"))
    dp, ctx = ("z", "core"), ("y", "x")
    tokens = P(dp, ctx, None)
    vector, matrix = P(dp), P(dp, None)
    return jax.shard_map(
        functools.partial(shards, (nz, ny)),
        mesh=fine,
        in_specs=(
            tokens,
            matrix,
            vector,
            vector,
            vector,
            vector,
            matrix,
            vector,
            matrix,
            vector,
            matrix,
            vector,
            matrix,
            vector,
            tokens,
        ),
        out_specs=(
            tokens,
            tokens,
            vector,
            vector,
            vector,
            vector,
            matrix,
            vector,
            matrix,
            vector,
            matrix,
            vector,
            matrix,
            vector,
        ),
        check_vma=False,
    )
```

```python
import functools
import math

import jax
import jax.numpy as jnp
from jax import lax
from jax.experimental import pallas as pl
from jax.experimental.pallas import tpu as pltpu
from jax.sharding import Mesh
from jax.sharding import PartitionSpec as P

HEADS = 12
ROT = 16
TP = 4

norm_eps = 1e-05
far = -1e30
root_half = 0.7071067811865476
inv_root_two_pi = 0.3989422804014327
F32 = jnp.float32
BF16 = jnp.bfloat16


def dot(a, b):
    return jnp.dot(a, b, preferred_element_type=F32)


def dot_nt(a, b):
    return lax.dot_general(a, b, (((1,), (1,)), ((), ())), preferred_element_type=F32)


def dot_tn(a, b):
    return lax.dot_general(a, b, (((0,), (0,)), ((), ())), preferred_element_type=F32)


def gelu_value(inputs):
    return 0.5 * inputs * (1.0 + lax.erf(inputs * root_half))


def gelu_slope(inputs):
    return (
        0.5 * (1.0 + lax.erf(inputs * root_half))
        + inputs * jnp.exp(-0.5 * inputs * inputs) * inv_root_two_pi
    )


def norm_parts(values):
    centre = jnp.mean(values, axis=-1, keepdims=True)
    centred = values - centre
    variance = jnp.mean(centred * centred, axis=-1, keepdims=True)
    inverse = lax.rsqrt(variance + norm_eps)
    return centred * inverse, inverse


class Dims:
    def __init__(self, head_dim, docs, block):
        self.nh = HEADS // TP
        self.hd = head_dim
        self.hw = self.nh * head_dim
        self.docs = docs
        extra = max(docs + 2 * self.nh, 3 * self.nh)
        self.width = -(-(self.hw + extra) // 128) * 128
        self.block = block
        self.scale = head_dim ** (-0.5)


def turn(values, cos, sin, lane, d, direction):
    half = ROT // 2
    ahead = pltpu.roll(values, d.width - half, 1)
    behind = pltpu.roll(values, half, 1)
    partner = jnp.where(lane % d.hd < half, -ahead, behind)
    return values * cos + partner * (sin * direction)


def head_mask(lane, h, d):
    return (lane >= h * d.hd) & (lane < (h + 1) * d.hd)


def prep_kernel(d, info, qkv, fc1, fc2, dense, *rest):
    small, (q_own, q_sent, f_own, f_sent, low_first, low_second) = rest[:8], rest[8:]
    core, x_at, first = info[1], info[3], info[4]
    rows, hw = d.rows, d.hw
    for c in range(2):
        for x in range(2):

            @pl.when(x_at == x)
            def _():
                wide = fc1[...]
                parts = []
                for z in range(d.nz):
                    at = ((z * 2 + c) * 2 + x) * d.piece
                    parts.append(wide[:, at : at + d.piece])
                chunk = jnp.concatenate(parts, axis=1)
                at = (2 * c + x) * hw
                heads = jnp.concatenate(
                    [qkv[:, t * d.model + at : t * d.model + at + hw] for t in range(3)], axis=1
                )

                @pl.when(core == c)
                def _():
                    f_own[...] = chunk
                    q_own[:rows, :] = heads

                @pl.when(core != c)
                def _():
                    f_sent[...] = chunk
                    q_sent[:rows, :] = heads

    for out in (q_own, q_sent):
        out[rows:, :] = jnp.zeros((out.shape[0] - rows, out.shape[1]), BF16)
        n = rows
        for ref in small:
            count = ref.shape[1] // rows
            for e in range(count):
                out[n : n + 1, :rows] = ref[:, e * rows : (e + 1) * rows]
                n += 1
    half, dhalf = d.piece // 2, rows // 2
    for out, which in ((low_first, first), (low_second, 1 - first)):
        for x in range(2):
            for y in range(2):

                @pl.when((x_at == x) & (which == y))
                def _():
                    at = x * d.piece + y * half
                    out[:half, :] = fc2[at : at + half, :]
                    out[half:, :] = dense[y * dhalf : (y + 1) * dhalf, :]


def forward_kernel(d, info, *refs):
    nz = d.nz
    x0, x1 = refs[:2]
    chunks = refs[2 : 2 + 2 * nz]
    cos, sin, normed_out, q_out, k_out, v_out, att_out, vec_out, w, units, bias = refs[2 + 2 * nz :]
    seq = pl.program_id(0)
    length = x0.shape[1]
    blk, wd, rows, hw = d.block, d.width, d.rows, d.hw

    @pl.when(seq == 0)
    def _():
        w[...] = jnp.zeros_like(w)
        bias[...] = jnp.zeros_like(bias)
        for which in range(2):
            for k in range(nz):
                ref = chunks[which * nz + k]
                block = lax.rem(info[0] - k + nz, nz)
                half = info[4] if which == 0 else 1 - info[4]
                at = pl.multiple_of((block * 2 + half) * rows, 16)
                for t in range(3):
                    w[pl.ds(at, rows), t * wd : t * wd + hw] = ref[:rows, t * hw : (t + 1) * hw]
                small = ref[rows : rows + 16, :128].astype(F32)
                for n in range(13):
                    units[n, pl.ds(block * 2 + half, 1), :] = small[n : n + 1, :]
        vec_out[...] = jnp.zeros_like(vec_out)
        for n in range(4):
            for o in range(2 * nz):
                vec_out[n : n + 1, o * rows : (o + 1) * rows] = units[n, o : o + 1, :rows]
        for o in range(2 * nz):
            vec_out[4:5, o * rows : (o + 1) * rows] = (
                units[4, o : o + 1, :rows] + units[5, o : o + 1, :rows]
            )
        per = d.piece // rows
        for z in range(nz):
            for e in range(per):
                got = units[9 + per * info[3] + e, pl.ds(2 * z + info[1], 1), :rows]
                vec_out[5:6, z * d.piece + e * rows : z * d.piece + (e + 1) * rows] = got
        place = 2 * info[1] + info[3]
        for t in range(3):
            for e in range(hw // rows):
                u = t * (d.model // rows) + place * (hw // rows) + e
                got = units[6 + lax.rem(u, 3), pl.ds(lax.div(u, 3), 1), :rows]
                bias[0:1, t * wd + e * rows : t * wd + (e + 1) * rows] = got

    lane = lax.broadcasted_iota(jnp.int32, (blk, wd), 1)
    row = lax.broadcasted_iota(jnp.int32, (blk, wd), 0)
    row_s = lax.broadcasted_iota(jnp.int32, (blk, blk), 0)
    col_s = lax.broadcasted_iota(jnp.int32, (blk, blk), 1)
    lse_lane = d.hw + d.docs
    gain, shift = vec_out[0:1, :], vec_out[1:2, :]
    for i in range(length // blk):
        at = pl.ds(i * blk, blk)
        xb = jnp.where(seq == 0, x0[0, at, :], x1[0, at, :])
        normed, _ = norm_parts(xb.astype(F32))
        a = (normed * gain + shift).astype(BF16)
        normed_out[0, at, :] = a
        proj = dot(a, w[...]) + bias[0:1, :]
        c, s = cos[at, :], sin[at, :]
        q = turn(proj[:, :wd], c, s, lane, d, 1.0).astype(BF16).astype(F32) * d.scale
        k = turn(proj[:, wd : 2 * wd], c, s, lane, d, 1.0)
        v = proj[:, 2 * wd :]
        pos = row + i * blk
        seg = jnp.zeros((blk, wd), jnp.int32)
        start = 0
        for n in range(d.docs - 1):
            start = start + info[8 + seq * d.docs + n]
            seg = seg + (pos >= start).astype(jnp.int32)
        same = (lane - d.hw) == seg
        in_seg = (lane >= d.hw) & (lane < lse_lane)
        q = jnp.where(lane < d.hw, q, jnp.where(in_seg & same, 1.0, 0.0))
        k = jnp.where(
            lane < d.hw,
            k,
            jnp.where(
                in_seg,
                jnp.where(same, 0.0, far),
                jnp.where(lane < lse_lane + 2 * d.nh, 1.0, 0.0),
            ),
        )
        v = jnp.where(lane < d.hw, v, jnp.where(lane < d.hw + 3 * d.nh, 1.0, 0.0))
        k_out[0, at, :] = k.astype(BF16)
        v_out[0, at, :] = v.astype(BF16)
        total = jnp.zeros((blk, wd), F32)
        q_final = q
        for h in range(d.nh):
            mine = head_mask(lane, h, d)
            qh = jnp.where(mine | in_seg, q, 0.0).astype(BF16)
            near = dot_nt(qh, k_out[0, at, :])
            near = jnp.where(col_s <= row_s, near, far)
            top = jnp.max(near, axis=1, keepdims=True)
            if i:
                past = dot_nt(qh, k_out[0, : i * blk, :])
                top = jnp.maximum(top, jnp.max(past, axis=1, keepdims=True))
            near = jnp.exp(near - top)
            count = jnp.sum(near, axis=1, keepdims=True)
            mixed = dot(near.astype(BF16), v_out[0, at, :])
            if i:
                past = jnp.exp(past - top)
                count = count + jnp.sum(past, axis=1, keepdims=True)
                mixed = mixed + dot(past.astype(BF16), v_out[0, : i * blk, :])
            total = jnp.where(mine, mixed / count, total)
            lse = top + jnp.log(count)
            high = lse.astype(BF16).astype(F32)
            low = lse - high
            q_final = jnp.where(lane == lse_lane + 2 * h, -high, q_final)
            q_final = jnp.where(lane == lse_lane + 2 * h + 1, -low, q_final)
        q_out[0, at, :] = q_final.astype(BF16)
        att_out[0, at, :] = total.astype(BF16)


def mlp_kernel(d, steps, info, *refs):
    nz = d.nz
    x0, x1, c0, c1, att = refs[:5]
    ups = refs[5 : 5 + 2 * nz]
    lows = refs[5 + 2 * nz : 5 + 4 * nz]
    dense_own, dense_got, vec = refs[5 + 4 * nz : 8 + 4 * nz]
    outs = refs[8 + 4 * nz :]
    out0, out1, back, vec_out, keep, sent = outs[:6]
    grads = outs[6 : 6 + nz]
    up, low, dense, d_up, d_low, d_dense, sums = outs[6 + nz :]
    t = pl.program_id(0)
    rows, piece, wd, model = d.rows, d.piece, d.width, d.model

    @pl.when(t == 0)
    def _():
        for which in range(2):
            for k in range(nz):
                block = lax.rem(info[0] - k + nz, nz)
                half = info[4] if which == 0 else 1 - info[4]
                at = pl.multiple_of((block * 2 + half) * rows, 16)
                up[pl.ds(at, rows), :] = ups[which * nz + k][...]
                at = pl.multiple_of((block * 2 + half) * (piece // 2), 16)
                low[pl.ds(at, piece // 2), :] = lows[which * nz + k][: piece // 2, :]
        for b in range(nz // TP):
            take = pl.ds(b * rows, rows)
            at = pl.multiple_of((2 * b + info[1]) * rows, 16)
            dense[pl.ds(at, rows), :] = dense_own[take, :]
            at = pl.multiple_of((2 * b + 1 - info[1]) * rows, 16)
            dense[pl.ds(at, rows), :] = dense_got[take, :]
        for ref in (d_up, d_low, d_dense, sums):
            ref[...] = jnp.zeros_like(ref)

    mine = t < steps // d.group if d.group > 1 else t >= 0
    cot = jnp.where(mine, c0[0], c1[0])
    xb = jnp.where(mine, x0[0], x1[0]).astype(F32)
    normed, _ = norm_parts(xb)
    a = (normed * vec[2:3, :] + vec[3:4, :]).astype(BF16)
    upper = dot(a, up[...]) + vec[5:6, :]
    phi = 0.5 * (1.0 + lax.erf(upper * root_half))
    act = (upper * phi).astype(BF16)
    slope = phi + upper * jnp.exp(-0.5 * upper * upper) * inv_root_two_pi
    ug = dot_nt(cot, low[...]) * slope
    ugb = ug.astype(BF16)
    at_b = att[0][:, : d.hw]
    out = (dot(act, low[...]) + dot(at_b, dense[...])).astype(BF16)

    @pl.when(mine)
    def _():
        out0[0] = out

    if d.group > 1:

        @pl.when(jnp.logical_not(mine))
        def _():
            out1[0] = out

    d_low[...] += dot_tn(act, cot)
    d_up[...] += dot_tn(a, ugb)
    d_dense[...] += dot_tn(at_b, cot)
    mb = dot_nt(ugb, up[...])
    back[0] = (mb * vec[2:3, :]).astype(BF16)
    sums[0:1, :] += jnp.sum(mb * normed, axis=0, keepdims=True)
    sums[1:2, :] += jnp.sum(mb, axis=0, keepdims=True)
    sums[2:3, :] += jnp.sum(cot.astype(F32), axis=0, keepdims=True) * (1.0 / TP)
    sums[3:4, :] += jnp.sum(ug, axis=0, keepdims=True)

    @pl.when(t == steps - 1)
    def _():
        vec_out[...] = sums[...]
        half = model // 2
        for c in range(2):

            @pl.when(info[1] == c)
            def _():
                keep[...] = d_dense[:, c * half : (c + 1) * half].astype(BF16)
                sent[...] = d_dense[:, (1 - c) * half : (2 - c) * half].astype(BF16)

        for k in range(nz):
            block = lax.rem(info[0] + k, nz)
            at = pl.multiple_of(block * 2 * rows, 16)
            grads[k][: 2 * rows, :] = d_up[pl.ds(at, 2 * rows), :].astype(BF16)
            at = pl.multiple_of(block * piece, 16)
            grads[k][2 * rows :, :] = d_low[pl.ds(at, piece), :].astype(BF16)


def backward_kernel(d, info, *refs):
    nz = d.nz
    x0, x1, c0, c1, back, normed_in, att, q_in, k_in, v_in = refs[:10]
    chunks = refs[10 : 10 + 2 * nz]
    dense_own, dense_got, d_keep, d_got, vec, vec_mlp, cos, sin = refs[10 + 2 * nz : 18 + 2 * nz]
    outs = refs[18 + 2 * nz :]
    g0, g1 = outs[:2]
    grads = outs[2 : 2 + nz]
    w, dense, grad, dw, dw_dense, sums, dout, douth, qh, dq = outs[2 + nz :]
    seq = pl.program_id(0)
    length = x0.shape[1]
    blk, wd, rows, hw, model = d.block, d.width, d.rows, d.hw, d.model
    nb = length // blk

    @pl.when(seq == 0)
    def _():
        w[...] = jnp.zeros_like(w)
        for which in range(2):
            for k in range(nz):
                ref = chunks[which * nz + k]
                block = lax.rem(info[0] - k + nz, nz)
                half = info[4] if which == 0 else 1 - info[4]
                at = pl.multiple_of((block * 2 + half) * rows, 16)
                for t in range(3):
                    w[pl.ds(at, rows), t * wd : t * wd + hw] = ref[:rows, t * hw : (t + 1) * hw]
        dense[hw:, :] = jnp.zeros((wd - hw, model), BF16)
        for b in range(nz // TP):
            take = pl.ds(b * rows, rows)
            at = pl.multiple_of((2 * b + info[1]) * rows, 16)
            dense[pl.ds(at, rows), :] = dense_own[take, :]
            at = pl.multiple_of((2 * b + 1 - info[1]) * rows, 16)
            dense[pl.ds(at, rows), :] = dense_got[take, :]
        dw[...] = jnp.zeros_like(dw)
        sums[...] = jnp.zeros_like(sums)

    lane = lax.broadcasted_iota(jnp.int32, (blk, wd), 1)
    row_s = lax.broadcasted_iota(jnp.int32, (blk, blk), 0)
    col_s = lax.broadcasted_iota(jnp.int32, (blk, blk), 1)
    lse_lane = d.hw + d.docs
    in_seg = (lane >= d.hw) & (lane < lse_lane)
    for i in range(nb):
        at = pl.ds(i * blk, blk)
        cot = jnp.where(seq == 0, c0[0, at, :], c1[0, at, :])
        og = dot_nt(cot, dense[...]).astype(BF16).astype(F32)
        both = og * att[0, at, :].astype(F32)
        full = og
        q = q_in[0, at, :].astype(F32)
        for h in range(d.nh):
            mine = head_mask(lane, h, d)
            delta = jnp.sum(jnp.where(mine, both, 0.0), axis=1, keepdims=True)
            for piece in range(3):
                part = delta.astype(BF16).astype(F32)
                delta = delta - part
                full = jnp.where(lane == d.hw + 3 * h + piece, -part, full)
            douth[h, at, :] = jnp.where(mine, og, 0.0).astype(BF16)
            qh[h, at, :] = jnp.where(mine, q, 0.0).astype(BF16)
        dout[at, :] = full.astype(BF16)
    dq[...] = jnp.zeros_like(dq)
    sums_k = jnp.zeros((1, wd), F32)
    sums_v = jnp.zeros((1, wd), F32)
    for j in range(nb):
        at = pl.ds(j * blk, blk)
        rest = pl.ds(j * blk, length - j * blk)
        k = k_in[0, at, :]
        v = v_in[0, at, :]
        dk = jnp.zeros((blk, wd), F32)
        dv = jnp.zeros((blk, wd), F32)
        for h in range(d.nh):
            mine = head_mask(lane, h, d)
            lse_mine = (lane >= lse_lane + 2 * h) & (lane < lse_lane + 2 * h + 2)
            delta_mine = (lane >= d.hw + 3 * h) & (lane < d.hw + 3 * h + 3)
            kh = jnp.where(mine | in_seg | lse_mine, k.astype(F32), 0.0).astype(BF16)
            vh = jnp.where(mine | delta_mine, v.astype(F32), 0.0).astype(BF16)
            st = dot_nt(kh, q_in[0, rest, :])
            dp = dot_nt(vh, dout[rest, :])
            first = jnp.where(col_s >= row_s, st[:, :blk], far)
            if j < nb - 1:
                st = jnp.concatenate([first, st[:, blk:]], axis=1)
            else:
                st = first
            p = jnp.exp(st)
            ds = (p * dp).astype(BF16)
            dv = dv + dot(p.astype(BF16), douth[h, rest, :])
            dk = dk + dot(ds, qh[h, rest, :])
            dq[rest, :] += dot_tn(ds, kh)
        dk = turn(dk, cos[at, :], sin[at, :], lane, d, -1.0)
        sums_k = sums_k + jnp.sum(dk, axis=0, keepdims=True)
        sums_v = sums_v + jnp.sum(dv, axis=0, keepdims=True)
        grad[at, wd : 2 * wd] = dk.astype(BF16)
        grad[at, 2 * wd :] = dv.astype(BF16)
    sums_q = jnp.zeros((1, wd), F32)
    for i in range(nb):
        at = pl.ds(i * blk, blk)
        part = jnp.where(lane < d.hw, dq[at, :], 0.0) * d.scale
        part = turn(part, cos[at, :], sin[at, :], lane, d, -1.0)
        sums_q = sums_q + jnp.sum(part, axis=0, keepdims=True)
        grad[at, :wd] = part.astype(BF16)
    sums[2:3, :] += jnp.concatenate([sums_q, sums_k, sums_v], axis=1)
    dw[...] += dot_tn(normed_in[0], grad[...])
    for i in range(nb):
        at = pl.ds(i * blk, blk)
        ab = dot_nt(grad[at, :], w[...])
        xb = jnp.where(seq == 0, x0[0, at, :], x1[0, at, :]).astype(F32)
        normed, _ = norm_parts(xb)
        sums[0:1, :model] += jnp.sum(ab * normed, axis=0, keepdims=True)
        sums[1:2, :model] += jnp.sum(ab, axis=0, keepdims=True)
        total = (ab * vec[0:1, :] + back[0, at, :].astype(F32)).astype(BF16)

        @pl.when(seq == 0)
        def _():
            g0[0, at, :] = total

        if d.group > 1:

            @pl.when(seq == 1)
            def _():
                g1[0, at, :] = total

    @pl.when(seq == d.group - 1)
    def _():
        for x in range(2):
            for c in range(2):

                @pl.when((info[3] == x) & (info[1] == c))
                def _():
                    place = lambda cc, xx: pl.ds((2 * cc + xx) * hw, hw)
                    dw_dense[place(c, x), :] = d_keep[:hw, x * hw : (x + 1) * hw]
                    dw_dense[place(1 - c, x), :] = d_keep[hw:, x * hw : (x + 1) * hw]
                    dw_dense[place(c, 1 - x), :] = d_got[:hw, :]
                    dw_dense[place(1 - c, 1 - x), :] = d_got[hw:, :]

        for k in range(nz):
            block = lax.rem(info[0] + k, nz)
            at = pl.multiple_of(block * 2 * rows, 16)
            part = dw[pl.ds(at, 2 * rows), :].astype(BF16)
            for t in range(3):
                grads[k][: 2 * rows, t * hw : (t + 1) * hw] = part[:, t * wd : t * wd + hw]
            grads[k][: 2 * rows, 3 * hw :] = dw_dense[pl.ds(at, 2 * rows), :]
            tail = jnp.zeros((16, 4 * hw), F32)
            grads[k][2 * rows :, :] = tail.astype(BF16)
            lines = [
                sums[0:1, :model],
                sums[1:2, :model],
                vec_mlp[0:1, :],
                vec_mlp[1:2, :],
                vec_mlp[2:3, :],
                vec_mlp[3:4, :],
            ]
            for n, line in enumerate(lines):
                grads[k][2 * rows + n : 2 * rows + n + 1, :] = line.astype(BF16)
            for t in range(3):
                grads[k][2 * rows + 6 : 2 * rows + 7, t * hw : (t + 1) * hw] = sums[
                    2:3, t * wd : t * wd + hw
                ].astype(BF16)


def chosen(c, x, info, own, core_got, x_own, x_got):
    first = jnp.where(info[3] == x, own, x_own)
    second = jnp.where(info[3] == x, core_got, x_got)
    return jnp.where(info[1] == c, first, second)


def upper_kernel(d, info, own, core_got, x_own, x_got, low, low_got, out_up, out_low):
    for c in range(2):
        for x in range(2):
            part = chosen(c, x, info, own[...], core_got[...], x_own[...], x_got[...]).astype(F32)
            for z in range(d.nz):
                at = ((z * 2 + c) * 2 + x) * d.piece
                out_up[:, at : at + d.piece] = part[:, z * d.piece : (z + 1) * d.piece]
    for x in range(2):
        mine = jnp.where(info[3] == x, low[...], low_got[...])
        out_low[x * d.piece : (x + 1) * d.piece, :] = mine.astype(F32)


def tail_kernel(d, info, own, core_got, x_own, x_got, *outs):
    out_qkv, out_dense, v0, v1, v2, v3, v4, v_up, v_qkv, scratch = outs
    rows, hw, model = d.rows, d.hw, d.model
    summed = None
    ups = []
    for c in range(2):
        for x in range(2):
            part = chosen(c, x, info, own[...], core_got[...], x_own[...], x_got[...]).astype(F32)
            place = 2 * c + x
            for t in range(3):
                at = t * model + place * hw
                out_qkv[:, at : at + hw] = part[:rows, t * hw : (t + 1) * hw]
                scratch[0:1, at : at + hw] = part[rows + 6 : rows + 7, t * hw : (t + 1) * hw]
            out_dense[:, place * hw : (place + 1) * hw] = part[:rows, 3 * hw :]
            vectors = part[rows : rows + 8, :]
            summed = vectors if summed is None else summed + vectors
            ups.append(vectors[5:6, :])
    mine = info[0] * 2 + info[1]
    turned = pltpu.roll(summed, lax.rem(model - mine * rows, model), 1)
    for n, ref in enumerate((v0, v1, v2, v3, v4)):
        ref[...] = turned[n : n + 1, :rows]
    for x in range(2):
        line = jnp.where(info[1] == 0, ups[x], ups[2 + x])
        line = jnp.broadcast_to(line, (8, line.shape[1]))
        line = pltpu.roll(line, lax.rem(model - info[0] * d.piece, model), 1)
        v_up[:, x * d.piece : (x + 1) * d.piece] = line[0:1, : d.piece]
    line = jnp.broadcast_to(scratch[0:1, :], (8, 3 * model))
    line = pltpu.roll(line, lax.rem(3 * model - mine * 3 * rows, 3 * model), 1)
    v_qkv[...] = line[0:1, : 3 * rows]


def whole(shape):
    return pl.BlockSpec(shape, lambda *_: (0,) * len(shape))


def whole_of(arrays):
    return [whole(a.shape) for a in arrays]


def per_seq(shape):
    return pl.BlockSpec((1,) + shape, lambda s, *_: (s,) + (0,) * len(shape))


def call(kernel, name, info, grid, inputs, in_specs, out_shape, out_specs, scratch, cost):
    return pl.pallas_call(
        kernel,
        grid_spec=pltpu.PrefetchScalarGridSpec(
            num_scalar_prefetch=1,
            grid=grid,
            in_specs=in_specs,
            out_specs=out_specs,
            scratch_shapes=scratch,
        ),
        out_shape=out_shape,
        cost_estimate=pl.CostEstimate(flops=cost[0], bytes_accessed=cost[1], transcendentals=0),
        name=name,
    )(info, *inputs)


def of(shape, dtype=BF16):
    return jax.ShapeDtypeStruct(shape, dtype)


def pick(values, index, axis=0):
    return lax.dynamic_index_in_dim(values, index, axis, keepdims=False)


def ordered(own, other, index, axis):
    return jnp.where(index == 0, jnp.stack([own, other], axis), jnp.stack([other, own], axis))


def swap(values, axis):
    return lax.ppermute(values, axis, [(0, 1), (1, 0)])


def shards(
    sizes,
    hidden_in,
    doc_lengths,
    ln1_gain,
    ln1_bias,
    ln2_gain,
    ln2_bias,
    qkv_weight,
    qkv_bias,
    dense_weight,
    dense_bias,
    fc1_weight,
    fc1_bias,
    fc2_weight,
    fc2_bias,
    cotangent,
):
    nz, ny = sizes
    zi, ci = lax.axis_index("z"), lax.axis_index("core")
    yi, xi = lax.axis_index("y"), lax.axis_index("x")
    peer = 1 - ci
    seqs, block, model = hidden_in.shape
    rows = ln1_gain.shape[0]
    hidden = fc1_weight.shape[1]
    piece = hidden // (nz * TP)
    length = block * ny * 2
    direct = ny == 2 and seqs == 2
    group = 2 * seqs // ny
    d = Dims(model // HEADS, doc_lengths.shape[1], block)
    d.nz, d.rows, d.piece, d.model, d.group = nz, rows, piece, model, group
    hw, wd = d.hw, d.width
    first = yi if ny == 2 else jnp.zeros_like(yi)

    def shift(values, k):
        return lax.ppermute(values, "z", [(i, (i + k) % nz) for i in range(nz)])

    def gathered(half, other):
        firsts = [half] + [shift(half, k) for k in range(1, nz)]
        if ny == 2:
            seconds = [other] + [swap(a, "y") for a in firsts[1:]]
        else:
            seconds = [other] + [shift(other, k) for k in range(1, nz)]
        return firsts + seconds

    def sum_z(parts):
        total = parts[0].astype(F32)
        for k in range(1, nz):
            total = total + shift(parts[k], k).astype(F32)
        return total.astype(BF16)

    def sum_y(part):
        if ny == 2:
            return (part.astype(F32) + swap(part, "y").astype(F32)).astype(BF16)
        return lax.psum(part, "y")

    def gather_tokens(values):
        if direct:
            got = swap(pick(values, 1 - yi), "y")
            mine = ordered(pick(values, yi), got, yi, 0)
            got = swap(mine, "x")
            mine = ordered(mine, got, xi, 1).reshape(1, length, model)
            return mine, swap(mine, "core")
        plane = lax.all_gather(values, "core", axis=0, tiled=True)
        plane = lax.all_gather(plane, ("y", "x"), axis=1, tiled=True)
        plane = lax.dynamic_slice_in_dim(plane, yi * group, group, 0)
        return plane[:1], plane[group - 1 :]

    def scatter_tokens(own, other):
        if direct:
            own = own.reshape(ny, 2, block, model)
            got = swap(other, "core").reshape(ny, 2, block, model)
            sent = (pick(own, 1 - xi, 1).astype(F32) + pick(got, 1 - xi, 1).astype(F32)).astype(BF16)
            kept = pick(own, xi, 1).astype(F32) + pick(got, xi, 1).astype(F32)
            total = (kept + swap(sent, "x").astype(F32)).astype(BF16)
            got = swap(pick(total, 1 - yi), "y")
            return ordered(pick(total, yi), got, yi, 0)
        values = jnp.concatenate([own, other], axis=0)[:group]
        plane = jnp.zeros((2 * seqs, length, model), BF16)
        plane = lax.dynamic_update_slice_in_dim(plane, values, yi * group, 0)
        plane = lax.psum_scatter(plane, "core", scatter_dimension=0, tiled=True)
        return lax.psum_scatter(plane, ("y", "x"), scatter_dimension=1, tiled=True)

    if direct:
        lengths = pick(doc_lengths, yi)
        lengths = jnp.concatenate([lengths, swap(lengths, "core")])
    else:
        lengths = lax.all_gather(doc_lengths, "core", axis=0, tiled=True)
        lengths = lax.dynamic_slice_in_dim(lengths, yi * group, group, 0).reshape(-1)
    places = jnp.stack([zi, ci, yi, xi, first, yi, yi, yi]).astype(jnp.int32)
    info = jnp.concatenate([places, lengths.astype(jnp.int32)])

    x0, x1 = gather_tokens(hidden_in)

    small = [ln1_gain, ln1_bias, ln2_gain, ln2_bias, dense_bias, fc2_bias, qkv_bias, fc1_bias]
    inputs = [qkv_weight, fc1_weight, fc2_weight, dense_weight] + [s[None, :] for s in small]
    q_type, f_type = of((rows + 16, 3 * hw)), of((rows, nz * piece))
    low_type = of((piece // 2 + rows // 2, model))
    out_shape = [q_type, q_type, f_type, f_type, low_type, low_type]
    q_own, q_sent, f_own, f_sent, low_first, low_second = call(
        functools.partial(prep_kernel, d),
        "prep",
        places,
        (1,),
        inputs,
        whole_of(inputs),
        out_shape,
        whole_of(out_shape),
        [],
        (0, 8 * rows * hidden),
    )
    q_got, f_got = swap(q_sent, "core"), swap(f_sent, "core")
    near = first == ci
    q_all = gathered(jnp.where(near, q_own, q_got), jnp.where(near, q_got, q_own))
    f_all = gathered(jnp.where(near, f_own, f_got), jnp.where(near, f_got, f_own))
    low_all = gathered(low_first, low_second)

    cot0, cot1 = gather_tokens(cotangent)

    def dense_rows(place):
        blocks = []
        for b in range(nz // TP):
            halves = []
            for n in range(2):
                total = low_all[n * nz][piece // 2 :]
                for k in range(1, nz):
                    here = lax.rem(zi - k + nz, nz) == place * (nz // TP) + b
                    total = jnp.where(here, low_all[n * nz + k][piece // 2 :], total)
                halves.append(total)
            blocks.append(ordered(halves[0], halves[1], first, 0).reshape(rows, model))
        return jnp.concatenate(blocks, axis=0)

    dense_own = dense_rows(2 * ci + xi)
    dense_got = swap(dense_rows(2 * peer + xi), "core")

    lane = jnp.arange(wd, dtype=jnp.int32)
    feature = lane % d.hd
    turned = (lane < hw) & (feature < ROT)
    frequency = jnp.exp((feature % (ROT // 2)).astype(F32) * (-2.0 * math.log(10000.0) / ROT))
    angles = jnp.arange(length, dtype=F32)[:, None] * frequency[None, :]
    cos = jnp.where(turned[None, :], jnp.cos(angles), 1.0)
    sin = jnp.where(turned[None, :], jnp.sin(angles), 0.0)

    pairs = group * d.nh * length * length // 2
    row_type = of((group, length, wd))
    token_type = of((1, length, model))
    inputs = [x0, x1] + q_all + [cos, sin]
    normed_in, q, k, v, att, vec = call(
        functools.partial(forward_kernel, d),
        "attention_forward",
        info,
        (group,),
        inputs,
        whole_of(inputs),
        [of((group, length, model))] + [row_type] * 4 + [of((8, model), F32)],
        [per_seq((length, model))] + [per_seq((length, wd))] * 4 + [whole((8, model))],
        [
            pltpu.VMEM((model, 3 * wd), BF16),
            pltpu.VMEM((16, max(8, 2 * nz), 128), F32),
            pltpu.VMEM((8, 3 * wd), F32),
        ],
        (2 * group * length * model * 3 * wd + 4 * pairs * wd, group * length * 2 * (2 * model + 4 * wd)),
    )

    tile = 512 if length % 512 == 0 else block
    steps = group * length // tile
    per = length // tile

    def early(t, *_):
        return (0, jnp.minimum(t, per - 1), 0)

    def late(t, *_):
        return (0, jnp.maximum(t - per * (group - 1), 0), 0)

    wide = (1, tile, model)
    pair = [pl.BlockSpec(wide, early), pl.BlockSpec(wide, late)]
    flat = lambda t, *_: (lax.div(t, per), lax.rem(t, per), 0)
    inputs = [x0, x1, cot0, cot1, att] + f_all + low_all + [dense_own, dense_got, vec]
    out_shape = [
        token_type,
        token_type,
        of((group, length, model)),
        of((8, model), F32),
        of((hw, model // 2)),
        of((hw, model // 2)),
    ] + [of((2 * rows + piece, model))] * nz
    out0, out1, back, vec_mlp, d_keep, d_sent, *up_parts = call(
        functools.partial(mlp_kernel, d, steps),
        "mlp",
        info,
        (steps,),
        inputs,
        pair + pair + [pl.BlockSpec((1, tile, wd), flat)] + whole_of(inputs[5:]),
        out_shape,
        pair + [pl.BlockSpec(wide, flat)] + whole_of(out_shape[3:]),
        [
            pltpu.VMEM((model, nz * piece), BF16),
            pltpu.VMEM((nz * piece, model), BF16),
            pltpu.VMEM((hw, model), BF16),
            pltpu.VMEM((model, nz * piece), F32),
            pltpu.VMEM((nz * piece, model), F32),
            pltpu.VMEM((hw, model), F32),
            pltpu.VMEM((8, model), F32),
        ],
        (12 * group * length * model * model, group * length * 10 * model),
    )

    out_mine = scatter_tokens(out0, out1)
    block_out = (hidden_in.astype(F32) + out_mine.astype(F32) + vec[4]).astype(BF16)

    up_sum = sum_y(sum_z(up_parts))
    sent = lax.dynamic_slice_in_dim(up_sum, peer * rows, rows)
    up_own = lax.dynamic_slice_in_dim(up_sum, ci * rows, rows)
    up_got = swap(sent, "core")
    low_own = up_sum[2 * rows :]

    d_keep = jnp.concatenate([d_keep, swap(d_sent, "core")], axis=0)
    d_cols = d_keep.reshape(2 * hw, 2, hw)
    d_got = swap(pick(d_cols, 1 - xi, 1), "x")

    inputs = [x0, x1, cot0, cot1, back, normed_in, att, q, k, v] + q_all
    inputs += [dense_own, dense_got, d_keep, d_got, vec, vec_mlp, cos, sin]
    out_shape = [token_type, token_type] + [of((2 * rows + 16, 4 * hw))] * nz
    g0, g1, *parts = call(
        functools.partial(backward_kernel, d),
        "attention_backward",
        info,
        (group,),
        inputs,
        whole_of(inputs[:4])
        + [per_seq((length, model))] * 2
        + [per_seq((length, wd))] * 4
        + whole_of(inputs[10:]),
        out_shape,
        whole_of(out_shape),
        [
            pltpu.VMEM((model, 3 * wd), BF16),
            pltpu.VMEM((wd, model), BF16),
            pltpu.VMEM((length, 3 * wd), BF16),
            pltpu.VMEM((model, 3 * wd), F32),
            pltpu.VMEM((model, hw), BF16),
            pltpu.VMEM((8, 3 * wd), F32),
            pltpu.VMEM((length, wd), BF16),
            pltpu.VMEM((d.nh, length, wd), BF16),
            pltpu.VMEM((d.nh, length, wd), BF16),
            pltpu.VMEM((length, wd), F32),
        ],
        (
            2 * group * length * model * 7 * wd + 10 * pairs * wd,
            group * length * 2 * (5 * model + 4 * wd),
        ),
    )
    chunk = sum_y(sum_z(parts))
    tail = chunk[2 * rows :]
    own = jnp.concatenate([lax.dynamic_slice_in_dim(chunk, ci * rows, rows), tail], axis=0)
    sent = jnp.concatenate([lax.dynamic_slice_in_dim(chunk, peer * rows, rows), tail], axis=0)
    core_got = swap(sent, "core")

    inputs = [up_own, up_got, swap(up_own, "x"), swap(up_got, "x"), low_own, swap(low_own, "x")]
    out_shape = [of((rows, hidden), F32), of((2 * piece, model), F32)]
    out_upper, out_lower = call(
        functools.partial(upper_kernel, d),
        "upper_out",
        info,
        (1,),
        inputs,
        whole_of(inputs),
        out_shape,
        whole_of(out_shape),
        [],
        (0, 12 * rows * hidden),
    )
    inputs = [own, core_got, swap(own, "x"), swap(core_got, "x")]
    line = of((1, rows), F32)
    out_shape = [of((rows, 3 * model), F32), of((rows, model), F32)] + [line] * 5
    out_shape += [of((1, 2 * piece), F32), of((1, 3 * rows), F32)]
    out_qkv, out_dense, v0, v1, v2, v3, v4, v_up, v_qkv = call(
        functools.partial(tail_kernel, d),
        "tail_out",
        info,
        (1,),
        inputs,
        whole_of(inputs),
        out_shape,
        whole_of(out_shape),
        [pltpu.VMEM((8, 3 * model), F32)],
        (0, 24 * rows * model),
    )

    scaled = scatter_tokens(g0, g1).astype(F32)
    normed, inverse = norm_parts(hidden_in.astype(F32))
    residue = (
        scaled
        - jnp.mean(scaled, axis=-1, keepdims=True)
        - normed * jnp.mean(scaled * normed, axis=-1, keepdims=True)
    )
    input_grad = cotangent.astype(F32) + residue * inverse
    return (
        block_out,
        input_grad,
        v0[0],
        v1[0],
        v2[0],
        v3[0],
        out_qkv,
        v_qkv[0],
        out_dense,
        v4[0],
        out_upper,
        v_up[0],
        out_lower,
        v4[0],
    )


def solution(mesh):
    nz, ny = mesh.shape["dp"] // 2, mesh.shape["ctx"] // 2
    fine = Mesh(mesh.devices.reshape(nz, 2, ny, 2), ("z", "core", "y", "x"))
    dp, ctx = ("z", "core"), ("y", "x")
    tokens = P(dp, ctx, None)
    vector, matrix = P(dp), P(dp, None)
    return jax.shard_map(
        functools.partial(shards, (nz, ny)),
        mesh=fine,
        in_specs=(
            tokens,
            matrix,
            vector,
            vector,
            vector,
            vector,
            matrix,
            vector,
            matrix,
            vector,
            matrix,
            vector,
            matrix,
            vector,
            tokens,
        ),
        out_specs=(
            tokens,
            tokens,
            vector,
            vector,
            vector,
            vector,
            matrix,
            vector,
            matrix,
            vector,
            matrix,
            vector,
            matrix,
            vector,
        ),
        check_vma=False,
    )
```

```python
import functools
import math

import jax
import jax.numpy as jnp
from jax import lax
from jax.experimental import pallas as pl
from jax.experimental.pallas import tpu as pltpu
from jax.sharding import Mesh
from jax.sharding import PartitionSpec as P


HEADS = 12
ROT = 16
TP = 4

norm_eps = 1e-05
far = -1e30
root_half = 0.7071067811865476
inv_root_two_pi = 0.3989422804014327
F32 = jnp.float32
BF16 = jnp.bfloat16


def dot(a, b):
    return jnp.dot(a, b, preferred_element_type=F32)


def dot_nt(a, b):
    return lax.dot_general(a, b, (((1,), (1,)), ((), ())), preferred_element_type=F32)


def dot_tn(a, b):
    return lax.dot_general(a, b, (((0,), (0,)), ((), ())), preferred_element_type=F32)


def norm_parts(values):
    centre = jnp.mean(values, axis=-1, keepdims=True)
    centred = values - centre
    variance = jnp.mean(centred * centred, axis=-1, keepdims=True)
    inverse = lax.rsqrt(variance + norm_eps)
    return centred * inverse, inverse


class Dims:
    def __init__(self, head_dim, docs, block):
        self.nh = HEADS // TP
        self.hd = head_dim
        self.hw = self.nh * head_dim
        self.docs = docs
        extra = max(docs + 2 * self.nh, 3 * self.nh)
        self.width = -(-(self.hw + extra) // 128) * 128
        self.block = block
        self.scale = head_dim ** (-0.5)


def turn(values, cos, sin, lane, d, direction):
    half = ROT // 2
    ahead = pltpu.roll(values, d.width - half, 1)
    behind = pltpu.roll(values, half, 1)
    partner = jnp.where(lane % d.hd < half, -ahead, behind)
    return values * cos + partner * (sin * direction)


def head_mask(lane, h, d):
    return (lane >= h * d.hd) & (lane < (h + 1) * d.hd)


def prep_kernel(d, info, qkv, fc1, fc2, dense, *rest):
    small, (q_own, q_sent, f_own, f_sent, low_first, low_second) = rest[:8], rest[8:]
    core, x_at, first = info[1], info[3], info[4]
    rows, hw = d.rows, d.hw
    for c in range(2):
        for x in range(2):

            @pl.when(x_at == x)
            def _():
                wide = fc1[...]
                parts = []
                for z in range(d.nz):
                    at = ((z * 2 + c) * 2 + x) * d.piece
                    parts.append(wide[:, at : at + d.piece])
                chunk = jnp.concatenate(parts, axis=1)
                at = (2 * c + x) * hw
                heads = jnp.concatenate(
                    [qkv[:, t * d.model + at : t * d.model + at + hw] for t in range(3)], axis=1
                )

                @pl.when(core == c)
                def _():
                    f_own[:rows, :] = chunk
                    q_own[...] = heads

                @pl.when(core != c)
                def _():
                    f_sent[:rows, :] = chunk
                    q_sent[...] = heads

    for out in (f_own, f_sent):
        out[rows:, :] = jnp.zeros((out.shape[0] - rows, out.shape[1]), BF16)
        n = rows
        for ref in small:
            count = ref.shape[1] // rows
            for e in range(count):
                out[n : n + 1, :rows] = ref[:, e * rows : (e + 1) * rows]
                n += 1
    half, dhalf = d.piece // 2, rows // 2
    for out, which in ((low_first, first), (low_second, 1 - first)):
        for x in range(2):
            for y in range(2):

                @pl.when((x_at == x) & (which == y))
                def _():
                    at = x * d.piece + y * half
                    out[:half, :] = fc2[at : at + half, :]
                    out[half:, :] = dense[y * dhalf : (y + 1) * dhalf, :]


def place_heads(d, info, chunks, w):
    w[...] = jnp.zeros_like(w)
    for k, ref in enumerate(chunks):
        block = lax.rem(info[0] - k + d.nz, d.nz)
        for c in range(2):
            at = pl.multiple_of((block * 2 + c) * d.rows, 16)
            for t in range(3):
                w[pl.ds(at, d.rows), t * d.width : t * d.width + d.hw] = ref[
                    c, : d.rows, t * d.hw : (t + 1) * d.hw
                ]


def read_small(d, info, chunks, units, vec, bias):
    nz, rows, hw, wd = d.nz, d.rows, d.hw, d.width
    for which in range(2):
        for k in range(nz):
            block = lax.rem(info[0] - k + nz, nz)
            half = info[4] if which == 0 else 1 - info[4]
            units[block * 2 + half] = chunks[which * nz + k][rows : rows + 16, :128].astype(F32)
    vec[...] = jnp.zeros_like(vec)
    bias[...] = jnp.zeros_like(bias)
    for n in range(4):
        for o in range(2 * nz):
            vec[n : n + 1, o * rows : (o + 1) * rows] = units[o, n : n + 1, :rows]
    for o in range(2 * nz):
        vec[4:5, o * rows : (o + 1) * rows] = units[o, 4:5, :rows] + units[o, 5:6, :rows]
    per = d.piece // rows
    for z in range(nz):
        for e in range(per):
            got = units[2 * z + info[1], pl.ds(9 + per * info[3] + e, 1), :rows]
            vec[5:6, z * d.piece + e * rows : z * d.piece + (e + 1) * rows] = got
    place = 2 * info[1] + info[3]
    for t in range(3):
        for e in range(hw // rows):
            u = t * (d.model // rows) + place * (hw // rows) + e
            got = units[lax.div(u, 3), pl.ds(6 + lax.rem(u, 3), 1), :rows]
            bias[0:1, t * wd + e * rows : t * wd + (e + 1) * rows] = got


def read_dense(d, info, own, got, dense):
    dense[d.hw :, :] = jnp.zeros((dense.shape[0] - d.hw, d.model), BF16)
    for b in range(d.nz // TP):
        take = pl.ds(b * d.rows, d.rows)
        at = pl.multiple_of((2 * b + info[1]) * d.rows, 16)
        dense[pl.ds(at, d.rows), :] = own[take, :]
        at = pl.multiple_of((2 * b + 1 - info[1]) * d.rows, 16)
        dense[pl.ds(at, d.rows), :] = got[take, :]


def forward_kernel(d, info, *refs):
    nz, group = d.nz, d.group
    x, cot, out_in = refs[:3]
    chunks, refs = refs[3 : 3 + nz], refs[3 + nz :]
    dense_own, dense_got, vec, bias, cos, sin = refs[:6]
    outs, refs = refs[6 : 6 + group], refs[6 + group :]
    q_out, k_out, v_out, att_out = refs[:4]
    dense_parts, refs = refs[4:8], refs[8:]
    w, dense, d_dense, out_all = refs
    seq = pl.program_id(0)
    length = x.shape[1]
    blk, wd = d.block, d.width

    @pl.when(seq == 0)
    def _():
        place_heads(d, info, chunks, w)
        read_dense(d, info, dense_own, dense_got, dense)
        d_dense[...] = jnp.zeros_like(d_dense)

    lane = lax.broadcasted_iota(jnp.int32, (blk, wd), 1)
    row = lax.broadcasted_iota(jnp.int32, (blk, wd), 0)
    row_s = lax.broadcasted_iota(jnp.int32, (blk, blk), 0)
    col_s = lax.broadcasted_iota(jnp.int32, (blk, blk), 1)
    lse_lane = d.hw + d.docs
    in_seg = (lane >= d.hw) & (lane < lse_lane)
    for i in range(length // blk):
        at = pl.ds(i * blk, blk)
        normed, _ = norm_parts(x[0, at, :].astype(F32))
        a = (normed * vec[0:1, :] + vec[1:2, :]).astype(BF16)
        proj = dot(a, w[...]) + bias[0:1, :]
        c, s = cos[at, :], sin[at, :]
        q = turn(proj[:, :wd], c, s, lane, d, 1.0).astype(BF16).astype(F32) * d.scale
        k = turn(proj[:, wd : 2 * wd], c, s, lane, d, 1.0)
        v = proj[:, 2 * wd :]
        pos = row + i * blk
        seg = jnp.zeros((blk, wd), jnp.int32)
        start = 0
        for n in range(d.docs - 1):
            start = start + info[8 + seq * d.docs + n]
            seg = seg + (pos >= start).astype(jnp.int32)
        same = (lane - d.hw) == seg
        q = jnp.where(lane < d.hw, q, jnp.where(in_seg & same, 1.0, 0.0))
        k = jnp.where(
            lane < d.hw,
            k,
            jnp.where(
                in_seg,
                jnp.where(same, 0.0, far),
                jnp.where(lane < lse_lane + 2 * d.nh, 1.0, 0.0),
            ),
        )
        v = jnp.where(lane < d.hw, v, jnp.where(lane < d.hw + 3 * d.nh, 1.0, 0.0))
        k_out[0, at, :] = k.astype(BF16)
        v_out[0, at, :] = v.astype(BF16)
        total = jnp.zeros((blk, wd), F32)
        q_final = q
        for h in range(d.nh):
            mine = head_mask(lane, h, d)
            qh = jnp.where(mine | in_seg, q, 0.0).astype(BF16)
            near = dot_nt(qh, k_out[0, at, :])
            near = jnp.where(col_s <= row_s, near, far)
            top = jnp.max(near, axis=1, keepdims=True)
            if i:
                past = dot_nt(qh, k_out[0, : i * blk, :])
                top = jnp.maximum(top, jnp.max(past, axis=1, keepdims=True))
            near = jnp.exp(near - top)
            number = jnp.sum(near, axis=1, keepdims=True)
            mixed = dot(near.astype(BF16), v_out[0, at, :])
            if i:
                past = jnp.exp(past - top)
                number = number + jnp.sum(past, axis=1, keepdims=True)
                mixed = mixed + dot(past.astype(BF16), v_out[0, : i * blk, :])
            total = jnp.where(mine, mixed / number, total)
            lse = top + jnp.log(number)
            high = lse.astype(BF16).astype(F32)
            low = lse - high
            q_final = jnp.where(lane == lse_lane + 2 * h, -high, q_final)
            q_final = jnp.where(lane == lse_lane + 2 * h + 1, -low, q_final)
        q_out[0, at, :] = q_final.astype(BF16)
        total = total.astype(BF16)
        att_out[0, at, :] = total
        out = out_in[0, at, :].astype(F32) + dot(total, dense[...])
        out_all[0, at, :] = out.astype(BF16)

    for n, ref in enumerate(outs):

        @pl.when(seq == n)
        def _():
            ref[...] = out_all[...]

    d_dense[...] += dot_tn(att_out[0], cot[0])

    @pl.when(seq == group - 1)
    def _():
        for c in range(2):
            for at_x in range(2):

                @pl.when((info[1] == c) & (info[3] == at_x))
                def _():
                    for n, ref in enumerate(dense_parts):
                        place = 2 * (c ^ (n // 2)) + (at_x ^ (n % 2))
                        ref[...] = d_dense[: d.hw, place * d.hw : (place + 1) * d.hw].astype(BF16)


def mlp_kernel(d, steps, count, info, *refs):
    nz, group = d.nz, d.group
    x_pieces, refs = refs[: group * count], refs[group * count :]
    cot_pieces, refs = refs[: group * count], refs[group * count :]
    ups, lows, refs = refs[: 2 * nz], refs[2 * nz : 4 * nz], refs[4 * nz :]
    x_out, cot_out, out, back, sums_out, vec, bias = refs[:7]
    grads, refs = refs[7 : 7 + nz], refs[7 + nz :]
    xs, cots, up, low, d_up, d_low, sums, units, sems = refs
    t = pl.program_id(0)
    rows, piece = d.rows, d.piece

    def copies(seq):
        made = []
        for n in range(count):
            size = d.block if count > 1 else xs.shape[1]
            at = 0
            if count > 1:
                y = lax.rem(info[2] + n % 2, 2)
                x_at = lax.rem(info[3] + n // 2, 2)
                at = pl.multiple_of((y * 2 + x_at) * d.block, d.block)
            for which, (pieces, target) in enumerate(((x_pieces, xs), (cot_pieces, cots))):
                source = pieces[seq * count + n]
                source = source if count > 1 else source.at[0]
                sem = sems.at[(seq * count + n) * 2 + which]
                made.append(
                    pltpu.make_async_copy(source, target.at[seq, pl.ds(at, size), :], sem)
                )
        return made

    @pl.when(t == 0)
    def _():
        for seq in range(group):
            for one in copies(seq):
                one.start()

    @pl.when(t == 0)
    def _():
        read_small(d, info, ups, units, vec, bias)
        for which in range(2):
            for k in range(nz):
                block = lax.rem(info[0] - k + nz, nz)
                half = info[4] if which == 0 else 1 - info[4]
                at = pl.multiple_of((block * 2 + half) * rows, 16)
                up[pl.ds(at, rows), :] = ups[which * nz + k][:rows, :]
                at = pl.multiple_of((block * 2 + half) * (piece // 2), 16)
                low[pl.ds(at, piece // 2), :] = lows[which * nz + k][: piece // 2, :]
        for ref in (d_up, d_low, sums):
            ref[...] = jnp.zeros_like(ref)

    tile = x_out.shape[1]
    per = steps // group
    for seq in range(group):

        @pl.when(t == seq * per)
        def _():
            for one in copies(seq):
                one.wait()

    at = pl.ds(pl.multiple_of(lax.rem(t, per) * tile, tile), tile)
    cot = cots[lax.div(t, per), at, :]
    cot_out[0] = cot
    xb = xs[lax.div(t, per), at, :]
    x_out[0] = xb
    normed, _ = norm_parts(xb.astype(F32))
    a = (normed * vec[2:3, :] + vec[3:4, :]).astype(BF16)
    upper = dot(a, up[...]) + vec[5:6, :]
    phi = 0.5 * (1.0 + lax.erf(upper * root_half))
    act = (upper * phi).astype(BF16)
    slope = phi + upper * jnp.exp(-0.5 * upper * upper) * inv_root_two_pi
    ug = dot_nt(cot, low[...]) * slope
    ugb = ug.astype(BF16)
    out[0] = dot(act, low[...]).astype(BF16)
    d_low[...] += dot_tn(act, cot)
    d_up[...] += dot_tn(a, ugb)
    mb = dot_nt(ugb, up[...])
    back[0] = (mb * vec[2:3, :]).astype(BF16)
    sums[0:1, :] += jnp.sum(mb * normed, axis=0, keepdims=True)
    sums[1:2, :] += jnp.sum(mb, axis=0, keepdims=True)
    sums[2:3, :] += jnp.sum(cot.astype(F32), axis=0, keepdims=True) * (1.0 / TP)
    sums[3:4, :] += jnp.sum(ug, axis=0, keepdims=True)

    @pl.when(t == steps - 1)
    def _():
        sums_out[...] = sums[...]
        for k in range(nz):
            block = lax.rem(info[0] + k, nz)
            at = pl.multiple_of(block * 2 * rows, 16)
            grads[k][: 2 * rows, :] = d_up[pl.ds(at, 2 * rows), :].astype(BF16)
            at = pl.multiple_of(block * piece, 16)
            grads[k][2 * rows :, :] = d_low[pl.ds(at, piece), :].astype(BF16)


def backward_kernel(d, info, *refs):
    nz, group = d.nz, d.group
    x, cots, back, att, q_in, k_in, v_in = refs[:7]
    chunks, refs = refs[7 : 7 + nz], refs[7 + nz :]
    dense_own, dense_got, vec, cos, sin, vec_mlp = refs[:6]
    d_parts = refs[6:10]
    gs, refs = refs[10 : 10 + group], refs[10 + group :]
    grads, refs = refs[:nz], refs[nz:]
    dw, sums, dw_dense, w, dense, grad, dout, douth, qh, dq, normed_in, g_all = refs
    step = pl.program_id(0)
    length = x.shape[1]
    blk, wd, rows, hw, model = d.block, d.width, d.rows, d.hw, d.model
    nb = length // blk

    @pl.when(step == 0)
    def _():
        place_heads(d, info, chunks, w)
        read_dense(d, info, dense_own, dense_got, dense)
        dw[...] = jnp.zeros_like(dw)
        sums[...] = jnp.zeros_like(sums)

    lane = lax.broadcasted_iota(jnp.int32, (blk, wd), 1)
    row_s = lax.broadcasted_iota(jnp.int32, (blk, blk), 0)
    col_s = lax.broadcasted_iota(jnp.int32, (blk, blk), 1)
    lse_lane = d.hw + d.docs
    in_seg = (lane >= d.hw) & (lane < lse_lane)

    def block_rows(i):
        return pl.ds(pl.multiple_of(i * blk, blk), blk)

    for i in range(nb):
        at = pl.ds(i * blk, blk)
        og = dot_nt(cots[0, at, :], dense[...]).astype(BF16).astype(F32)
        both = og * att[0, at, :].astype(F32)
        full = og
        q = q_in[0, at, :].astype(F32)
        for h in range(d.nh):
            mine = head_mask(lane, h, d)
            delta = jnp.sum(jnp.where(mine, both, 0.0), axis=1, keepdims=True)
            for piece in range(3):
                part = delta.astype(BF16).astype(F32)
                delta = delta - part
                full = jnp.where(lane == d.hw + 3 * h + piece, -part, full)
            douth[h, at, :] = jnp.where(mine, og, 0.0).astype(BF16)
            qh[h, at, :] = jnp.where(mine, q, 0.0).astype(BF16)
        dout[at, :] = full.astype(BF16)
    dq[...] = jnp.zeros_like(dq)
    for j in range(nb):
        at = pl.ds(j * blk, blk)
        rest = pl.ds(j * blk, length - j * blk)
        k = k_in[0, at, :].astype(F32)
        v = v_in[0, at, :].astype(F32)
        dk = jnp.zeros((blk, wd), F32)
        dv = jnp.zeros((blk, wd), F32)
        for h in range(d.nh):
            mine = head_mask(lane, h, d)
            lse_mine = (lane >= lse_lane + 2 * h) & (lane < lse_lane + 2 * h + 2)
            delta_mine = (lane >= d.hw + 3 * h) & (lane < d.hw + 3 * h + 3)
            kh = jnp.where(mine | in_seg | lse_mine, k, 0.0).astype(BF16)
            vh = jnp.where(mine | delta_mine, v, 0.0).astype(BF16)
            st = dot_nt(kh, q_in[0, rest, :])
            dp = dot_nt(vh, dout[rest, :])
            first = jnp.where(col_s >= row_s, st[:, :blk], far)
            if j < nb - 1:
                st = jnp.concatenate([first, st[:, blk:]], axis=1)
            else:
                st = first
            p = jnp.exp(st)
            ds = (p * dp).astype(BF16)
            dv = dv + dot(p.astype(BF16), douth[h, rest, :])
            dk = dk + dot(ds, qh[h, rest, :])
            dq[rest, :] += dot_tn(ds, kh)
        dk = turn(dk, cos[at, :], sin[at, :], lane, d, -1.0)
        for n, value in ((1, dk), (2, dv)):
            sums[2:3, n * wd : (n + 1) * wd] += jnp.sum(value, axis=0, keepdims=True)
            grad[at, n * wd : (n + 1) * wd] = value.astype(BF16)

    def finish(i, _):
        at = block_rows(i)
        part = jnp.where(lane < d.hw, dq[at, :], 0.0) * d.scale
        part = turn(part, cos[at, :], sin[at, :], lane, d, -1.0)
        sums[2:3, :wd] += jnp.sum(part, axis=0, keepdims=True)
        grad[at, :wd] = part.astype(BF16)
        ab = dot_nt(grad[at, :], w[...])
        normed, _ = norm_parts(x[0, at, :].astype(F32))
        normed_in[at, :] = (normed * vec[0:1, :] + vec[1:2, :]).astype(BF16)
        sums[0:1, :model] += jnp.sum(ab * normed, axis=0, keepdims=True)
        sums[1:2, :model] += jnp.sum(ab, axis=0, keepdims=True)
        g_all[0, at, :] = (ab * vec[0:1, :] + back[0, at, :].astype(F32)).astype(BF16)
        return 0

    lax.fori_loop(0, nb, finish, 0)
    for n, ref in enumerate(gs):

        @pl.when(step == group - 1 - n)
        def _():
            ref[...] = g_all[...]

    dw[...] += dot_tn(normed_in[...], grad[...])

    @pl.when(step == group - 1)
    def _():
        for x_at in range(2):
            for c in range(2):

                @pl.when((info[3] == x_at) & (info[1] == c))
                def _():
                    for n, ref in enumerate(d_parts):
                        place = 2 * (c ^ (n // 2)) + (x_at ^ (n % 2))
                        dw_dense[place * hw : (place + 1) * hw, :] = ref[...]

        lines = [
            sums[0:1, :model],
            sums[1:2, :model],
            vec_mlp[0:1, :],
            vec_mlp[1:2, :],
            vec_mlp[2:3, :],
            vec_mlp[3:4, :],
        ]
        for k in range(nz):
            block = lax.rem(info[0] + k, nz)
            at = pl.multiple_of(block * 2 * rows, 16)
            part = dw[pl.ds(at, 2 * rows), :].astype(BF16)
            for t in range(3):
                grads[k][: 2 * rows, t * hw : (t + 1) * hw] = part[:, t * wd : t * wd + hw]
            grads[k][: 2 * rows, 3 * hw :] = dw_dense[pl.ds(at, 2 * rows), :]
            grads[k][2 * rows :, :] = jnp.zeros((16, 4 * hw), BF16)
            for n, line in enumerate(lines):
                grads[k][2 * rows + n : 2 * rows + n + 1, :] = line.astype(BF16)
            for t in range(3):
                grads[k][2 * rows + 6 : 2 * rows + 7, t * hw : (t + 1) * hw] = sums[
                    2:3, t * wd : t * wd + hw
                ].astype(BF16)


def chosen(c, x, info, own, core_got, x_own, x_got):
    first = jnp.where(info[3] == x, own, x_own)
    second = jnp.where(info[3] == x, core_got, x_got)
    return jnp.where(info[1] == c, first, second)


def upper_kernel(d, info, own, core_got, x_own, x_got, low, low_got, out_up, out_low):
    for c in range(2):
        for x in range(2):
            part = chosen(c, x, info, own[...], core_got[...], x_own[...], x_got[...]).astype(F32)
            for z in range(d.nz):
                at = ((z * 2 + c) * 2 + x) * d.piece
                out_up[:, at : at + d.piece] = part[:, z * d.piece : (z + 1) * d.piece]
    for x in range(2):
        mine = jnp.where(info[3] == x, low[...], low_got[...])
        out_low[x * d.piece : (x + 1) * d.piece, :] = mine.astype(F32)


def tail_kernel(d, info, own, core_got, x_own, x_got, *outs):
    out_qkv, out_dense, v0, v1, v2, v3, v4, v_up, v_qkv, scratch = outs
    rows, hw, model = d.rows, d.hw, d.model
    summed = None
    ups = []
    for c in range(2):
        for x in range(2):
            part = chosen(c, x, info, own[...], core_got[...], x_own[...], x_got[...]).astype(F32)
            place = 2 * c + x
            for t in range(3):
                at = t * model + place * hw
                out_qkv[:, at : at + hw] = part[:rows, t * hw : (t + 1) * hw]
                scratch[0:1, at : at + hw] = part[rows + 6 : rows + 7, t * hw : (t + 1) * hw]
            out_dense[:, place * hw : (place + 1) * hw] = part[:rows, 3 * hw :]
            vectors = part[rows : rows + 8, :]
            summed = vectors if summed is None else summed + vectors
            ups.append(vectors[5:6, :])
    mine = info[0] * 2 + info[1]
    turned = pltpu.roll(summed, lax.rem(model - mine * rows, model), 1)
    for n, ref in enumerate((v0, v1, v2, v3, v4)):
        ref[...] = turned[n, :rows]
    for x in range(2):
        line = jnp.where(info[1] == 0, ups[x], ups[2 + x])
        line = jnp.broadcast_to(line, (8, line.shape[1]))
        line = pltpu.roll(line, lax.rem(model - info[0] * d.piece, model), 1)
        scratch[1:2, x * d.piece : (x + 1) * d.piece] = line[0:1, : d.piece]
    v_up[...] = scratch[1, : 2 * d.piece]
    line = jnp.broadcast_to(scratch[0:1, :], (8, 3 * model))
    line = pltpu.roll(line, lax.rem(3 * model - mine * 3 * rows, 3 * model), 1)
    v_qkv[...] = line[0, : 3 * rows]


def whole(shape):
    return pl.BlockSpec(shape, lambda *_: (0,) * len(shape))


def whole_of(arrays):
    return [whole(a.shape) for a in arrays]


def per_seq(shape):
    return pl.BlockSpec((1,) + shape, lambda s, *_: (s,) + (0,) * len(shape))


def call(kernel, info, grid, inputs, in_specs, out_shape, out_specs, scratch, cost, aliases=None):
    return pl.pallas_call(
        kernel,
        grid_spec=pltpu.PrefetchScalarGridSpec(
            num_scalar_prefetch=1,
            grid=grid,
            in_specs=in_specs,
            out_specs=out_specs,
            scratch_shapes=scratch,
        ),
        out_shape=out_shape,
        input_output_aliases=aliases or {},
        cost_estimate=pl.CostEstimate(flops=cost[0], bytes_accessed=cost[1], transcendentals=0),
    )(info, *inputs)


def of(shape, dtype=BF16):
    return jax.ShapeDtypeStruct(shape, dtype)


def pick(values, index, axis=0):
    return lax.dynamic_index_in_dim(values, index, axis, keepdims=False)


def ordered(own, other, index, axis):
    return jnp.where(index == 0, jnp.stack([own, other], axis), jnp.stack([other, own], axis))


def swap(values, axis):
    return lax.ppermute(values, axis, [(0, 1), (1, 0)])


def shards(
    sizes,
    hidden_in,
    doc_lengths,
    ln1_gain,
    ln1_bias,
    ln2_gain,
    ln2_bias,
    qkv_weight,
    qkv_bias,
    dense_weight,
    dense_bias,
    fc1_weight,
    fc1_bias,
    fc2_weight,
    fc2_bias,
    cotangent,
):
    nz, ny = sizes
    zi, ci = lax.axis_index("z"), lax.axis_index("core")
    yi, xi = lax.axis_index("y"), lax.axis_index("x")
    peer = 1 - ci
    seqs, block, model = hidden_in.shape
    rows = ln1_gain.shape[0]
    hidden = fc1_weight.shape[1]
    piece = hidden // (nz * TP)
    length = block * ny * 2
    direct = ny == 2 and seqs == 2
    group = 2 * seqs // ny
    d = Dims(model // HEADS, doc_lengths.shape[1], block)
    d.nz, d.rows, d.piece, d.model, d.group = nz, rows, piece, model, group
    hw, wd = d.hw, d.width
    first = yi if ny == 2 else jnp.zeros_like(yi)

    def shift(values, k):
        return lax.ppermute(values, "z", [(i, (i + k) % nz) for i in range(nz)])

    def gathered(half, other):
        firsts = [half] + [shift(half, k) for k in range(1, nz)]
        if ny == 2:
            seconds = [other] + [swap(firsts[k], "y") for k in range(1, nz)]
        else:
            seconds = [other] + [shift(other, k) for k in range(1, nz)]
        return firsts + seconds

    def sum_z(parts):
        total = parts[0].astype(F32)
        for k in range(1, nz):
            total = total + shift(parts[k], k).astype(F32)
        return total.astype(BF16)

    def sum_y(part):
        if ny == 2:
            return (part.astype(F32) + swap(part, "y").astype(F32)).astype(BF16)
        return lax.psum(part, "y")

    def gather_tokens(values):
        if direct:
            mine, sent = pick(values, yi), pick(values, 1 - yi)
            got = swap(sent, "y")
            own = [mine, got, swap(mine, "x"), swap(got, "x")]
            return [own, [swap(a, "core") for a in own]]
        plane = lax.all_gather(values, "core", axis=0, tiled=True)
        plane = lax.all_gather(plane, ("y", "x"), axis=1, tiled=True)
        plane = lax.dynamic_slice_in_dim(plane, yi * group, group, 0)
        return [[plane[n : n + 1]] for n in range(group)]

    def scatter_tokens(values):
        if direct:
            own = values[0].reshape(ny, 2, block, model)
            got = swap(values[1], "core").reshape(ny, 2, block, model)
            sent = (pick(own, 1 - xi, 1).astype(F32) + pick(got, 1 - xi, 1).astype(F32)).astype(BF16)
            kept = pick(own, xi, 1).astype(F32) + pick(got, xi, 1).astype(F32)
            total = (kept + swap(sent, "x").astype(F32)).astype(BF16)
            got = swap(pick(total, 1 - yi), "y")
            return ordered(pick(total, yi), got, yi, 0)
        plane = jnp.zeros((2 * seqs, length, model), BF16)
        plane = lax.dynamic_update_slice_in_dim(plane, jnp.concatenate(values), yi * group, 0)
        plane = lax.psum_scatter(plane, "core", scatter_dimension=0, tiled=True)
        return lax.psum_scatter(plane, ("y", "x"), scatter_dimension=1, tiled=True)

    if direct:
        lengths = pick(doc_lengths, yi)
        lengths = jnp.concatenate([lengths, swap(lengths, "core")])
    else:
        lengths = lax.all_gather(doc_lengths, "core", axis=0, tiled=True)
        lengths = lax.dynamic_slice_in_dim(lengths, yi * group, group, 0).reshape(-1)
    places = jnp.stack([zi, ci, yi, xi, first, yi, yi, yi]).astype(jnp.int32)
    info = jnp.concatenate([places, lengths.astype(jnp.int32)])

    x_pieces = gather_tokens(hidden_in)
    count = len(x_pieces[0])

    small = [ln1_gain, ln1_bias, ln2_gain, ln2_bias, dense_bias, fc2_bias, qkv_bias, fc1_bias]
    inputs = [qkv_weight, fc1_weight, fc2_weight, dense_weight] + [s[None, :] for s in small]
    q_type, f_type = of((rows, 3 * hw)), of((rows + 16, nz * piece))
    low_type = of((piece // 2 + rows // 2, model))
    out_shape = [q_type, q_type, f_type, f_type, low_type, low_type]
    q_own, q_sent, f_own, f_sent, low_first, low_second = call(
        functools.partial(prep_kernel, d),
        places,
        (1,),
        inputs,
        whole_of(inputs),
        out_shape,
        whole_of(out_shape),
        [],
        (0, 8 * rows * hidden),
    )
    q_got, f_got = swap(q_sent, "core"), swap(f_sent, "core")
    near = first == ci
    q_pair = ordered(q_own, q_got, ci, 0)
    q_all = [q_pair] + [shift(q_pair, k) for k in range(1, nz)]
    f_all = gathered(jnp.where(near, f_own, f_got), jnp.where(near, f_got, f_own))
    low_all = gathered(low_first, low_second)

    cot_pieces = gather_tokens(cotangent)

    def dense_rows(place):
        blocks = []
        for b in range(nz // TP):
            halves = []
            for n in range(2):
                total = low_all[n * nz][piece // 2 :]
                for k in range(1, nz):
                    here = lax.rem(zi - k + nz, nz) == place * (nz // TP) + b
                    total = jnp.where(here, low_all[n * nz + k][piece // 2 :], total)
                halves.append(total)
            blocks.append(ordered(halves[0], halves[1], first, 0).reshape(rows, model))
        return jnp.concatenate(blocks, axis=0)

    dense_own = dense_rows(2 * ci + xi)
    dense_got = swap(dense_rows(2 * peer + xi), "core")

    lane = jnp.arange(wd, dtype=jnp.int32)
    feature = lane % d.hd
    turned = (lane < hw) & (feature < ROT)
    frequency = jnp.exp((feature % (ROT // 2)).astype(F32) * (-2.0 * math.log(10000.0) / ROT))
    angles = jnp.arange(length, dtype=F32)[:, None] * frequency[None, :]
    cos = jnp.where(turned[None, :], jnp.cos(angles), 1.0)
    sin = jnp.where(turned[None, :], jnp.sin(angles), 0.0)

    pairs = d.nh * length * length // 2
    token_type = of((1, length, model))
    tokens_type = of((group, length, model))
    tile = block
    steps = group * length // tile
    per = length // tile
    tiles = pl.BlockSpec((1, tile, model), lambda t, *_: (lax.div(t, per), lax.rem(t, per), 0))
    wide = of((8, 3 * wd), F32)
    inputs = [a for one in x_pieces for a in one] + [a for one in cot_pieces for a in one]
    inputs += f_all + low_all
    out_shape = [tokens_type] * 4 + [of((8, model), F32)] * 2 + [wide]
    out_shape += [of((2 * rows + piece, model))] * nz
    x, cot, out, back, vec_mlp, vec, bias, *up_parts = call(
        functools.partial(mlp_kernel, d, steps, count),
        info,
        (steps,),
        inputs,
        [pl.BlockSpec(memory_space=pl.ANY)] * (2 * group * count) + whole_of(inputs[2 * group * count :]),
        out_shape,
        [tiles] * 4 + whole_of(out_shape[4:]),
        [
            pltpu.VMEM((group, length, model), BF16),
            pltpu.VMEM((group, length, model), BF16),
            pltpu.VMEM((model, nz * piece), BF16),
            pltpu.VMEM((nz * piece, model), BF16),
            pltpu.VMEM((model, nz * piece), F32),
            pltpu.VMEM((nz * piece, model), F32),
            pltpu.VMEM((8, model), F32),
            pltpu.VMEM((2 * nz, 16, 128), F32),
            pltpu.SemaphoreType.DMA((2 * group * count,)),
        ],
        (12 * group * length * model * model, group * length * 12 * model),
    )
    rows_type = of((group, length, wd))
    inputs = [x, cot, out] + q_all + [dense_own, dense_got, vec, bias, cos, sin]
    out_shape = [token_type] * group + [rows_type] * 4 + [of((hw, hw))] * 4
    done = call(
        functools.partial(forward_kernel, d),
        info,
        (group,),
        inputs,
        [per_seq((length, model))] * 3 + whole_of(inputs[3:]),
        out_shape,
        whole_of(out_shape[:group]) + [per_seq((length, wd))] * 4 + whole_of(out_shape[group + 4 :]),
        [
            pltpu.VMEM((model, 3 * wd), BF16),
            pltpu.VMEM((wd, model), BF16),
            pltpu.VMEM((wd, model), F32),
            pltpu.VMEM((1, length, model), BF16),
        ],
        (
            group * (2 * length * model * 5 * wd + 4 * pairs * wd),
            group * length * 2 * (4 * model + 4 * wd),
        ),
    )
    outs = list(done[:group])
    q, k, v, att = done[group : group + 4]
    d_own, d_own_x, d_sent, d_sent_x = done[group + 4 :]

    out_mine = scatter_tokens(outs)
    block_out = (hidden_in.astype(F32) + out_mine.astype(F32) + vec[4]).astype(BF16)

    up_sum = sum_y(sum_z(up_parts))
    low_own = up_sum[2 * rows :]
    sent = lax.dynamic_slice_in_dim(up_sum, peer * rows, rows)
    up_own = lax.dynamic_slice_in_dim(up_sum, ci * rows, rows)
    up_got = swap(sent, "core")

    d_got, d_got_x = swap(d_sent, "core"), swap(d_sent_x, "core")
    d_parts = [d_own, swap(d_own_x, "x"), d_got, swap(d_got_x, "x")]

    def turned_seq(width):
        return pl.BlockSpec((1, length, width), lambda s, *_: (group - 1 - s, 0, 0))

    inputs = [x, cot, back, att, q, k, v] + q_all
    inputs += [dense_own, dense_got, vec, cos, sin, vec_mlp] + d_parts
    out_shape = [token_type] * group + [of((2 * rows + 16, 4 * hw))] * nz
    done = call(
        functools.partial(backward_kernel, d),
        info,
        (group,),
        inputs,
        [turned_seq(model)] * 3 + [turned_seq(wd)] * 4 + whole_of(inputs[7:]),
        out_shape,
        whole_of(out_shape),
        [
            pltpu.VMEM((model, 3 * wd), F32),
            pltpu.VMEM((8, 3 * wd), F32),
            pltpu.VMEM((model, hw), BF16),
            pltpu.VMEM((model, 3 * wd), BF16),
            pltpu.VMEM((wd, model), BF16),
            pltpu.VMEM((length, 3 * wd), BF16),
            pltpu.VMEM((length, wd), BF16),
            pltpu.VMEM((d.nh, length, wd), BF16),
            pltpu.VMEM((d.nh, length, wd), BF16),
            pltpu.VMEM((length, wd), F32),
            pltpu.VMEM((length, model), BF16),
            pltpu.VMEM((1, length, model), BF16),
        ],
        (
            2 * group * length * model * 7 * wd + 10 * group * pairs * wd,
            group * length * 2 * (4 * model + 4 * wd),
        ),
    )
    gs, state = list(done[:group]), done[group:]
    chunk = sum_y(sum_z(state))
    tail = chunk[2 * rows :]
    own = jnp.concatenate([lax.dynamic_slice_in_dim(chunk, ci * rows, rows), tail], axis=0)
    sent = jnp.concatenate([lax.dynamic_slice_in_dim(chunk, peer * rows, rows), tail], axis=0)
    core_got = swap(sent, "core")

    inputs = [up_own, up_got, swap(up_own, "x"), swap(up_got, "x")]
    inputs += [low_own, swap(low_own, "x")]
    out_shape = [of((rows, hidden), F32), of((2 * piece, model), F32)]
    out_upper, out_lower = call(
        functools.partial(upper_kernel, d),
        info,
        (1,),
        inputs,
        whole_of(inputs),
        out_shape,
        whole_of(out_shape),
        [],
        (0, 12 * rows * hidden),
    )
    inputs = [own, core_got, swap(own, "x"), swap(core_got, "x")]
    line = of((rows,), F32)
    out_shape = [of((rows, 3 * model), F32), of((rows, model), F32)] + [line] * 5
    out_shape += [of((2 * piece,), F32), of((3 * rows,), F32)]
    out_qkv, out_dense, v0, v1, v2, v3, v4, v_up, v_qkv = call(
        functools.partial(tail_kernel, d),
        info,
        (1,),
        inputs,
        whole_of(inputs),
        out_shape,
        whole_of(out_shape),
        [pltpu.VMEM((8, 3 * model), F32)],
        (0, 24 * rows * model),
    )

    scaled = scatter_tokens(gs).astype(F32)
    normed, inverse = norm_parts(hidden_in.astype(F32))
    residue = (
        scaled
        - jnp.mean(scaled, axis=-1, keepdims=True)
        - normed * jnp.mean(scaled * normed, axis=-1, keepdims=True)
    )
    input_grad = cotangent.astype(F32) + residue * inverse
    return (
        block_out,
        input_grad,
        v0,
        v1,
        v2,
        v3,
        out_qkv,
        v_qkv,
        out_dense,
        v4,
        out_upper,
        v_up,
        out_lower,
        v4,
    )


def solution(mesh):
    nz, ny = mesh.shape["dp"] // 2, mesh.shape["ctx"] // 2
    fine = Mesh(mesh.devices.reshape(nz, 2, ny, 2), ("z", "core", "y", "x"))
    dp, ctx = ("z", "core"), ("y", "x")
    tokens = P(dp, ctx, None)
    vector, matrix = P(dp), P(dp, None)

    def body(*args):
        return shards((nz, ny), *args)

    return jax.shard_map(
        body,
        mesh=fine,
        in_specs=(
            tokens,
            matrix,
            vector,
            vector,
            vector,
            vector,
            matrix,
            vector,
            matrix,
            vector,
            matrix,
            vector,
            matrix,
            vector,
            tokens,
        ),
        out_specs=(
            tokens,
            tokens,
            vector,
            vector,
            vector,
            vector,
            matrix,
            vector,
            matrix,
            vector,
            matrix,
            vector,
            matrix,
            vector,
        ),
        check_vma=False,
    )
```

```python
import functools
import math

import jax
import jax.numpy as jnp
from jax import lax
from jax.experimental import pallas as pl
from jax.experimental.pallas import tpu as pltpu
from jax.sharding import Mesh
from jax.sharding import PartitionSpec as P


HEADS = 12
ROT = 16
TP = 4

norm_eps = 1e-05
far = -1e30
root_half = 0.7071067811865476
inv_root_two_pi = 0.3989422804014327
F32 = jnp.float32
BF16 = jnp.bfloat16


def dot(a, b):
    return jnp.dot(a, b, preferred_element_type=F32)


def dot_nt(a, b):
    return lax.dot_general(a, b, (((1,), (1,)), ((), ())), preferred_element_type=F32)


def dot_tn(a, b):
    return lax.dot_general(a, b, (((0,), (0,)), ((), ())), preferred_element_type=F32)


def norm_parts(values):
    centre = jnp.mean(values, axis=-1, keepdims=True)
    centred = values - centre
    variance = jnp.mean(centred * centred, axis=-1, keepdims=True)
    inverse = lax.rsqrt(variance + norm_eps)
    return centred * inverse, inverse


class Dims:
    def __init__(self, head_dim, docs, block):
        self.nh = HEADS // TP
        self.hd = head_dim
        self.hw = self.nh * head_dim
        self.docs = docs
        extra = max(docs + 2 * self.nh, 3 * self.nh)
        self.width = -(-(self.hw + extra) // 128) * 128
        self.block = block
        self.scale = head_dim ** (-0.5)


def turn(values, cos, sin, lane, d, direction):
    half = ROT // 2
    ahead = pltpu.roll(values, d.width - half, 1)
    behind = pltpu.roll(values, half, 1)
    partner = jnp.where(lane % d.hd < half, -ahead, behind)
    return values * cos + partner * (sin * direction)


def head_mask(lane, h, d):
    return (lane >= h * d.hd) & (lane < (h + 1) * d.hd)


def prep_kernel(d, info, qkv, fc1, fc2, *rest):
    small, (q_own, q_sent, f_own, f_sent, low_first, low_second) = rest[:8], rest[8:]
    core, x_at, first = info[1], info[3], info[4]
    rows, hw = d.rows, d.hw
    for c in range(2):
        for x in range(2):

            @pl.when(x_at == x)
            def _():
                wide = fc1[...]
                parts = []
                for z in range(d.nz):
                    at = ((z * 2 + c) * 2 + x) * d.piece
                    parts.append(wide[:, at : at + d.piece])
                chunk = jnp.concatenate(parts, axis=1)
                at = (2 * c + x) * hw
                heads = jnp.concatenate(
                    [qkv[:, t * d.model + at : t * d.model + at + hw] for t in range(3)], axis=1
                )

                @pl.when(core == c)
                def _():
                    f_own[:rows, :] = chunk
                    q_own[...] = heads

                @pl.when(core != c)
                def _():
                    f_sent[:rows, :] = chunk
                    q_sent[...] = heads

    for out in (f_own, f_sent):
        out[rows:, :] = jnp.zeros((out.shape[0] - rows, out.shape[1]), BF16)
        n = rows
        for ref in small:
            line = ref[...].reshape(1, ref.shape[0])
            for e in range(ref.shape[0] // rows):
                out[n : n + 1, :rows] = line[:, e * rows : (e + 1) * rows]
                n += 1
    half = d.piece // 2
    for out, which in ((low_first, first), (low_second, 1 - first)):
        for x in range(2):
            for y in range(2):

                @pl.when((x_at == x) & (which == y))
                def _():
                    at = x * d.piece + y * half
                    out[...] = fc2[at : at + half, :]


def place_heads(d, info, chunks, w):
    w[...] = jnp.zeros_like(w)
    for k, ref in enumerate(chunks):
        block = lax.rem(info[0] - k + d.nz, d.nz)
        for c in range(2):
            at = pl.multiple_of((block * 2 + c) * d.rows, 16)
            for t in range(3):
                w[pl.ds(at, d.rows), t * d.width : t * d.width + d.hw] = ref[
                    c, : d.rows, t * d.hw : (t + 1) * d.hw
                ]


def read_small(d, info, chunks, units, vec, bias):
    nz, rows, hw, wd = d.nz, d.rows, d.hw, d.width
    for which in range(2):
        for k in range(nz):
            block = lax.rem(info[0] - k + nz, nz)
            half = info[4] if which == 0 else 1 - info[4]
            units[block * 2 + half] = chunks[which * nz + k][rows : rows + 16, :128].astype(F32)
    vec[...] = jnp.zeros_like(vec)
    bias[...] = jnp.zeros_like(bias)
    for n in range(4):
        for o in range(2 * nz):
            vec[n : n + 1, o * rows : (o + 1) * rows] = units[o, n : n + 1, :rows]
    for o in range(2 * nz):
        vec[4:5, o * rows : (o + 1) * rows] = units[o, 4:5, :rows] + units[o, 5:6, :rows]
    per = d.piece // rows
    for z in range(nz):
        for e in range(per):
            got = units[2 * z + info[1], pl.ds(9 + per * info[3] + e, 1), :rows]
            vec[5:6, z * d.piece + e * rows : z * d.piece + (e + 1) * rows] = got
    place = 2 * info[1] + info[3]
    for t in range(3):
        for e in range(hw // rows):
            u = t * (d.model // rows) + place * (hw // rows) + e
            got = units[lax.div(u, 3), pl.ds(6 + lax.rem(u, 3), 1), :rows]
            bias[0:1, t * wd + e * rows : t * wd + (e + 1) * rows] = got


def read_dense(d, info, own, got, dense):
    dense[d.hw :, :] = jnp.zeros((dense.shape[0] - d.hw, d.model), BF16)
    for b in range(d.nz // TP):
        take = pl.ds(b * d.rows, d.rows)
        at = pl.multiple_of((2 * b + info[1]) * d.rows, 16)
        dense[pl.ds(at, d.rows), :] = own[take, :]
        at = pl.multiple_of((2 * b + 1 - info[1]) * d.rows, 16)
        dense[pl.ds(at, d.rows), :] = got[take, :]


def forward_kernel(d, info, *refs):
    nz, group = d.nz, d.group
    x, cot, out_in = refs[:3]
    chunks, refs = refs[3 : 3 + nz], refs[3 + nz :]
    dense_own, dense_got, vec, bias, cos, sin = refs[:6]
    outs, refs = refs[6 : 6 + group], refs[6 + group :]
    q_out, k_out, v_out, att_out = refs[:4]
    dense_parts, refs = refs[4:8], refs[8:]
    w, dense, d_dense, out_all = refs
    seq = pl.program_id(0)
    length = x.shape[1]
    blk, wd = d.block, d.width

    @pl.when(seq == 0)
    def _():
        place_heads(d, info, chunks, w)
        read_dense(d, info, dense_own, dense_got, dense)
        d_dense[...] = jnp.zeros_like(d_dense)

    lane = lax.broadcasted_iota(jnp.int32, (blk, wd), 1)
    row = lax.broadcasted_iota(jnp.int32, (blk, wd), 0)
    row_s = lax.broadcasted_iota(jnp.int32, (blk, blk), 0)
    col_s = lax.broadcasted_iota(jnp.int32, (blk, blk), 1)
    lse_lane = d.hw + d.docs
    in_seg = (lane >= d.hw) & (lane < lse_lane)
    for i in range(length // blk):
        at = pl.ds(i * blk, blk)
        normed, _ = norm_parts(x[0, at, :].astype(F32))
        a = (normed * vec[0:1, :] + vec[1:2, :]).astype(BF16)
        proj = dot(a, w[...]) + bias[0:1, :]
        c, s = cos[at, :], sin[at, :]
        q = turn(proj[:, :wd], c, s, lane, d, 1.0).astype(BF16).astype(F32) * d.scale
        k = turn(proj[:, wd : 2 * wd], c, s, lane, d, 1.0)
        v = proj[:, 2 * wd :]
        pos = row + i * blk
        seg = jnp.zeros((blk, wd), jnp.int32)
        start = 0
        for n in range(d.docs - 1):
            start = start + info[8 + seq * d.docs + n]
            seg = seg + (pos >= start).astype(jnp.int32)
        same = (lane - d.hw) == seg
        q = jnp.where(lane < d.hw, q, jnp.where(in_seg & same, 1.0, 0.0))
        k = jnp.where(
            lane < d.hw,
            k,
            jnp.where(
                in_seg,
                jnp.where(same, 0.0, far),
                jnp.where(lane < lse_lane + 2 * d.nh, 1.0, 0.0),
            ),
        )
        v = jnp.where(lane < d.hw, v, jnp.where(lane < d.hw + 3 * d.nh, 1.0, 0.0))
        k_out[0, at, :] = k.astype(BF16)
        v_out[0, at, :] = v.astype(BF16)
        total = jnp.zeros((blk, wd), F32)
        q_final = q
        for h in range(d.nh):
            mine = head_mask(lane, h, d)
            qh = jnp.where(mine | in_seg, q, 0.0).astype(BF16)
            near = dot_nt(qh, k_out[0, at, :])
            near = jnp.where(col_s <= row_s, near, far)
            top = jnp.max(near, axis=1, keepdims=True)
            if i:
                past = dot_nt(qh, k_out[0, : i * blk, :])
                top = jnp.maximum(top, jnp.max(past, axis=1, keepdims=True))
            near = jnp.exp(near - top)
            number = jnp.sum(near, axis=1, keepdims=True)
            mixed = dot(near.astype(BF16), v_out[0, at, :])
            if i:
                past = jnp.exp(past - top)
                number = number + jnp.sum(past, axis=1, keepdims=True)
                mixed = mixed + dot(past.astype(BF16), v_out[0, : i * blk, :])
            total = jnp.where(mine, mixed / number, total)
            lse = top + jnp.log(number)
            high = lse.astype(BF16).astype(F32)
            low = lse - high
            q_final = jnp.where(lane == lse_lane + 2 * h, -high, q_final)
            q_final = jnp.where(lane == lse_lane + 2 * h + 1, -low, q_final)
        q_out[0, at, :] = q_final.astype(BF16)
        total = total.astype(BF16)
        att_out[0, at, :] = total
        out = out_in[0, at, :].astype(F32) + dot(total, dense[...])
        out_all[0, at, :] = out.astype(BF16)

    for n, ref in enumerate(outs):

        @pl.when(seq == n)
        def _():
            ref[...] = out_all[...]

    d_dense[...] += dot_tn(att_out[0], cot[0])

    @pl.when(seq == group - 1)
    def _():
        for c in range(2):
            for at_x in range(2):

                @pl.when((info[1] == c) & (info[3] == at_x))
                def _():
                    for n, ref in enumerate(dense_parts):
                        place = 2 * (c ^ (n // 2)) + (at_x ^ (n % 2))
                        ref[...] = d_dense[: d.hw, place * d.hw : (place + 1) * d.hw].astype(BF16)


def mlp_kernel(d, steps, count, info, *refs):
    nz, group = d.nz, d.group
    x_pieces, refs = refs[: group * count], refs[group * count :]
    cot_pieces, refs = refs[: group * count], refs[group * count :]
    ups, lows, refs = refs[: 2 * nz], refs[2 * nz : 4 * nz], refs[4 * nz :]
    x_out, cot_out, out, back, sums_out, vec, bias = refs[:7]
    grads, refs = refs[7 : 7 + nz], refs[7 + nz :]
    xs, cots, up, low, d_up, d_low, sums, units, sems = refs
    t = pl.program_id(0)
    rows, piece = d.rows, d.piece

    def copies(seq):
        made = []
        for n in range(count):
            size = d.block if count > 1 else xs.shape[1]
            at = 0
            if count > 1:
                y = lax.rem(info[2] + n % 2, 2)
                x_at = lax.rem(info[3] + n // 2, 2)
                at = pl.multiple_of((y * 2 + x_at) * d.block, d.block)
            for which, (pieces, target) in enumerate(((x_pieces, xs), (cot_pieces, cots))):
                source = pieces[seq * count + n]
                source = source if count > 1 else source.at[0]
                sem = sems.at[(seq * count + n) * 2 + which]
                made.append(
                    pltpu.make_async_copy(source, target.at[seq, pl.ds(at, size), :], sem)
                )
        return made

    @pl.when(t == 0)
    def _():
        for seq in range(group):
            for one in copies(seq):
                one.start()

    @pl.when(t == 0)
    def _():
        read_small(d, info, ups, units, vec, bias)
        for which in range(2):
            for k in range(nz):
                block = lax.rem(info[0] - k + nz, nz)
                half = info[4] if which == 0 else 1 - info[4]
                at = pl.multiple_of((block * 2 + half) * rows, 16)
                up[pl.ds(at, rows), :] = ups[which * nz + k][:rows, :]
                at = pl.multiple_of((block * 2 + half) * (piece // 2), 16)
                low[pl.ds(at, piece // 2), :] = lows[which * nz + k][: piece // 2, :]
        for ref in (d_up, d_low, sums):
            ref[...] = jnp.zeros_like(ref)

    tile = x_out.shape[1]
    per = steps // group
    for seq in range(group):

        @pl.when(t == seq * per)
        def _():
            for one in copies(seq):
                one.wait()

    at = pl.ds(pl.multiple_of(lax.rem(t, per) * tile, tile), tile)
    cot = cots[lax.div(t, per), at, :]
    cot_out[0] = cot
    xb = xs[lax.div(t, per), at, :]
    x_out[0] = xb
    normed, _ = norm_parts(xb.astype(F32))
    a = (normed * vec[2:3, :] + vec[3:4, :]).astype(BF16)
    upper = dot(a, up[...]) + vec[5:6, :]
    phi = 0.5 * (1.0 + lax.erf(upper * root_half))
    act = (upper * phi).astype(BF16)
    slope = phi + upper * jnp.exp(-0.5 * upper * upper) * inv_root_two_pi
    ug = dot_nt(cot, low[...]) * slope
    ugb = ug.astype(BF16)
    out[0] = dot(act, low[...]).astype(BF16)
    d_low[...] += dot_tn(act, cot)
    d_up[...] += dot_tn(a, ugb)
    mb = dot_nt(ugb, up[...])
    back[0] = (mb * vec[2:3, :]).astype(BF16)
    sums[0:1, :] += jnp.sum(mb * normed, axis=0, keepdims=True)
    sums[1:2, :] += jnp.sum(mb, axis=0, keepdims=True)
    sums[2:3, :] += jnp.sum(cot.astype(F32), axis=0, keepdims=True) * (1.0 / TP)
    sums[3:4, :] += jnp.sum(ug, axis=0, keepdims=True)

    @pl.when(t == steps - 1)
    def _():
        sums_out[...] = sums[...]
        for k in range(nz):
            block = lax.rem(info[0] + k, nz)
            at = pl.multiple_of(block * 2 * rows, 16)
            grads[k][: 2 * rows, :] = d_up[pl.ds(at, 2 * rows), :].astype(BF16)
            at = pl.multiple_of(block * piece, 16)
            grads[k][2 * rows :, :] = d_low[pl.ds(at, piece), :].astype(BF16)


def backward_kernel(d, info, *refs):
    nz, group = d.nz, d.group
    x, cots, back, att, q_in, k_in, v_in = refs[:7]
    chunks, refs = refs[7 : 7 + nz], refs[7 + nz :]
    dense_own, dense_got, vec, cos, sin, vec_mlp = refs[:6]
    d_parts = refs[6:10]
    gs, refs = refs[10 : 10 + group], refs[10 + group :]
    grads, refs = refs[:nz], refs[nz:]
    dw, sums, dw_dense, w, dense, grad, dout, douth, qh, dq, normed_in, g_all = refs
    step = pl.program_id(0)
    length = x.shape[1]
    blk, wd, rows, hw, model = d.block, d.width, d.rows, d.hw, d.model
    nb = length // blk

    @pl.when(step == 0)
    def _():
        place_heads(d, info, chunks, w)
        read_dense(d, info, dense_own, dense_got, dense)
        dw[...] = jnp.zeros_like(dw)
        sums[...] = jnp.zeros_like(sums)

    lane = lax.broadcasted_iota(jnp.int32, (blk, wd), 1)
    row_s = lax.broadcasted_iota(jnp.int32, (blk, blk), 0)
    col_s = lax.broadcasted_iota(jnp.int32, (blk, blk), 1)
    lse_lane = d.hw + d.docs
    in_seg = (lane >= d.hw) & (lane < lse_lane)

    def block_rows(i):
        return pl.ds(pl.multiple_of(i * blk, blk), blk)

    for i in range(nb):
        at = pl.ds(i * blk, blk)
        og = dot_nt(cots[0, at, :], dense[...]).astype(BF16).astype(F32)
        both = og * att[0, at, :].astype(F32)
        full = og
        q = q_in[0, at, :].astype(F32)
        for h in range(d.nh):
            mine = head_mask(lane, h, d)
            delta = jnp.sum(jnp.where(mine, both, 0.0), axis=1, keepdims=True)
            for piece in range(3):
                part = delta.astype(BF16).astype(F32)
                delta = delta - part
                full = jnp.where(lane == d.hw + 3 * h + piece, -part, full)
            douth[h, at, :] = jnp.where(mine, og, 0.0).astype(BF16)
            qh[h, at, :] = jnp.where(mine, q, 0.0).astype(BF16)
        dout[at, :] = full.astype(BF16)
    dq[...] = jnp.zeros_like(dq)
    for j in range(nb):
        at = pl.ds(j * blk, blk)
        rest = pl.ds(j * blk, length - j * blk)
        k = k_in[0, at, :].astype(F32)
        v = v_in[0, at, :].astype(F32)
        dk = jnp.zeros((blk, wd), F32)
        dv = jnp.zeros((blk, wd), F32)
        for h in range(d.nh):
            mine = head_mask(lane, h, d)
            lse_mine = (lane >= lse_lane + 2 * h) & (lane < lse_lane + 2 * h + 2)
            delta_mine = (lane >= d.hw + 3 * h) & (lane < d.hw + 3 * h + 3)
            kh = jnp.where(mine | in_seg | lse_mine, k, 0.0).astype(BF16)
            vh = jnp.where(mine | delta_mine, v, 0.0).astype(BF16)
            st = dot_nt(kh, q_in[0, rest, :])
            dp = dot_nt(vh, dout[rest, :])
            first = jnp.where(col_s >= row_s, st[:, :blk], far)
            if j < nb - 1:
                st = jnp.concatenate([first, st[:, blk:]], axis=1)
            else:
                st = first
            p = jnp.exp(st)
            ds = (p * dp).astype(BF16)
            dv = dv + dot(p.astype(BF16), douth[h, rest, :])
            dk = dk + dot(ds, qh[h, rest, :])
            dq[rest, :] += dot_tn(ds, kh)
        dk = turn(dk, cos[at, :], sin[at, :], lane, d, -1.0)
        for n, value in ((1, dk), (2, dv)):
            sums[2:3, n * wd : (n + 1) * wd] += jnp.sum(value, axis=0, keepdims=True)
            grad[at, n * wd : (n + 1) * wd] = value.astype(BF16)

    def finish(i, _):
        at = block_rows(i)
        part = jnp.where(lane < d.hw, dq[at, :], 0.0) * d.scale
        part = turn(part, cos[at, :], sin[at, :], lane, d, -1.0)
        sums[2:3, :wd] += jnp.sum(part, axis=0, keepdims=True)
        grad[at, :wd] = part.astype(BF16)
        ab = dot_nt(grad[at, :], w[...])
        normed, _ = norm_parts(x[0, at, :].astype(F32))
        normed_in[at, :] = (normed * vec[0:1, :] + vec[1:2, :]).astype(BF16)
        sums[0:1, :model] += jnp.sum(ab * normed, axis=0, keepdims=True)
        sums[1:2, :model] += jnp.sum(ab, axis=0, keepdims=True)
        g_all[0, at, :] = (ab * vec[0:1, :] + back[0, at, :].astype(F32)).astype(BF16)
        return 0

    lax.fori_loop(0, nb, finish, 0)
    for n, ref in enumerate(gs):

        @pl.when(step == group - 1 - n)
        def _():
            ref[...] = g_all[...]

    dw[...] += dot_tn(normed_in[...], grad[...])

    @pl.when(step == group - 1)
    def _():
        for x_at in range(2):
            for c in range(2):

                @pl.when((info[3] == x_at) & (info[1] == c))
                def _():
                    for n, ref in enumerate(d_parts):
                        place = 2 * (c ^ (n // 2)) + (x_at ^ (n % 2))
                        dw_dense[place * hw : (place + 1) * hw, :] = ref[...]

        lines = [
            sums[0:1, :model],
            sums[1:2, :model],
            vec_mlp[0:1, :],
            vec_mlp[1:2, :],
            vec_mlp[2:3, :],
            vec_mlp[3:4, :],
        ]
        for k in range(nz):
            block = lax.rem(info[0] + k, nz)
            at = pl.multiple_of(block * 2 * rows, 16)
            part = dw[pl.ds(at, 2 * rows), :].astype(BF16)
            for t in range(3):
                grads[k][: 2 * rows, t * hw : (t + 1) * hw] = part[:, t * wd : t * wd + hw]
            grads[k][: 2 * rows, 3 * hw :] = dw_dense[pl.ds(at, 2 * rows), :]
            grads[k][2 * rows :, :] = jnp.zeros((16, 4 * hw), BF16)
            for n, line in enumerate(lines):
                grads[k][2 * rows + n : 2 * rows + n + 1, :] = line.astype(BF16)
            for t in range(3):
                grads[k][2 * rows + 6 : 2 * rows + 7, t * hw : (t + 1) * hw] = sums[
                    2:3, t * wd : t * wd + hw
                ].astype(BF16)


def chosen(c, x, info, own, core_got, x_own, x_got):
    first = jnp.where(info[3] == x, own, x_own)
    second = jnp.where(info[3] == x, core_got, x_got)
    return jnp.where(info[1] == c, first, second)


def upper_kernel(d, info, own, core_got, x_own, x_got, low, low_got, out_up, out_low):
    for c in range(2):
        for x in range(2):
            part = chosen(c, x, info, own[...], core_got[...], x_own[...], x_got[...]).astype(F32)
            for z in range(d.nz):
                at = ((z * 2 + c) * 2 + x) * d.piece
                out_up[:, at : at + d.piece] = part[:, z * d.piece : (z + 1) * d.piece]
    for x in range(2):
        mine = jnp.where(info[3] == x, low[...], low_got[...])
        out_low[x * d.piece : (x + 1) * d.piece, :] = mine.astype(F32)


def tail_kernel(d, info, own, core_got, x_own, x_got, *outs):
    out_qkv, out_dense, v0, v1, v2, v3, v4, v_up, v_qkv, scratch = outs
    rows, hw, model = d.rows, d.hw, d.model
    summed = None
    ups = []
    for c in range(2):
        for x in range(2):
            part = chosen(c, x, info, own[...], core_got[...], x_own[...], x_got[...]).astype(F32)
            place = 2 * c + x
            for t in range(3):
                at = t * model + place * hw
                out_qkv[:, at : at + hw] = part[:rows, t * hw : (t + 1) * hw]
                scratch[0:1, at : at + hw] = part[rows + 6 : rows + 7, t * hw : (t + 1) * hw]
            out_dense[:, place * hw : (place + 1) * hw] = part[:rows, 3 * hw :]
            vectors = part[rows : rows + 8, :]
            summed = vectors if summed is None else summed + vectors
            ups.append(vectors[5:6, :])
    mine = info[0] * 2 + info[1]
    turned = pltpu.roll(summed, lax.rem(model - mine * rows, model), 1)
    for n, ref in enumerate((v0, v1, v2, v3, v4)):
        ref[...] = turned[n, :rows]
    for x in range(2):
        line = jnp.where(info[1] == 0, ups[x], ups[2 + x])
        line = jnp.broadcast_to(line, (8, line.shape[1]))
        line = pltpu.roll(line, lax.rem(model - info[0] * d.piece, model), 1)
        scratch[1:2, x * d.piece : (x + 1) * d.piece] = line[0:1, : d.piece]
    v_up[...] = scratch[1, : 2 * d.piece]
    line = jnp.broadcast_to(scratch[0:1, :], (8, 3 * model))
    line = pltpu.roll(line, lax.rem(3 * model - mine * 3 * rows, 3 * model), 1)
    v_qkv[...] = line[0, : 3 * rows]


def whole(shape):
    return pl.BlockSpec(shape, lambda *_: (0,) * len(shape))


def whole_of(arrays):
    return [whole(a.shape) for a in arrays]


def per_seq(shape):
    return pl.BlockSpec((1,) + shape, lambda s, *_: (s,) + (0,) * len(shape))


def call(kernel, info, grid, inputs, in_specs, out_shape, out_specs, scratch, cost, aliases=None):
    return pl.pallas_call(
        kernel,
        grid_spec=pltpu.PrefetchScalarGridSpec(
            num_scalar_prefetch=1,
            grid=grid,
            in_specs=in_specs,
            out_specs=out_specs,
            scratch_shapes=scratch,
        ),
        out_shape=out_shape,
        input_output_aliases=aliases or {},
        cost_estimate=pl.CostEstimate(flops=cost[0], bytes_accessed=cost[1], transcendentals=0),
    )(info, *inputs)


def of(shape, dtype=BF16):
    return jax.ShapeDtypeStruct(shape, dtype)


def pick(values, index, axis=0):
    return lax.dynamic_index_in_dim(values, index, axis, keepdims=False)


def ordered(own, other, index, axis):
    return jnp.where(index == 0, jnp.stack([own, other], axis), jnp.stack([other, own], axis))


def swap(values, axis):
    return lax.ppermute(values, axis, [(0, 1), (1, 0)])


def shards(
    sizes,
    hidden_in,
    doc_lengths,
    ln1_gain,
    ln1_bias,
    ln2_gain,
    ln2_bias,
    qkv_weight,
    qkv_bias,
    dense_weight,
    dense_bias,
    fc1_weight,
    fc1_bias,
    fc2_weight,
    fc2_bias,
    cotangent,
):
    nz, ny = sizes
    zi, ci = lax.axis_index("z"), lax.axis_index("core")
    yi, xi = lax.axis_index("y"), lax.axis_index("x")
    peer = 1 - ci
    seqs, block, model = hidden_in.shape
    rows = ln1_gain.shape[0]
    hidden = fc1_weight.shape[1]
    piece = hidden // (nz * TP)
    length = block * ny * 2
    direct = ny == 2 and seqs == 2
    group = 2 * seqs // ny
    d = Dims(model // HEADS, doc_lengths.shape[1], block)
    d.nz, d.rows, d.piece, d.model, d.group = nz, rows, piece, model, group
    hw, wd = d.hw, d.width
    first = yi if ny == 2 else jnp.zeros_like(yi)

    def shift(values, k):
        return lax.ppermute(values, "z", [(i, (i + k) % nz) for i in range(nz)])

    def gathered(half, other):
        firsts = [half] + [shift(half, k) for k in range(1, nz)]
        if ny == 2:
            seconds = [other] + [swap(firsts[k], "y") for k in range(1, nz)]
        else:
            seconds = [other] + [shift(other, k) for k in range(1, nz)]
        return firsts + seconds

    def sum_z(parts):
        got = [shift(parts[k], k) for k in range(1, nz)]
        total = parts[0].astype(F32)
        for part in got:
            total = total + part.astype(F32)
        return total.astype(BF16)

    def sum_y(part):
        if ny == 2:
            got = swap(part, "y")
            return (part.astype(F32) + got.astype(F32)).astype(BF16)
        return lax.psum(part, "y")

    def gather_tokens(values):
        if direct:
            mine, sent = pick(values, yi), pick(values, 1 - yi)
            got = swap(sent, "y")
            own = [mine, got, swap(mine, "x"), swap(got, "x")]
            return [own, [swap(a, "core") for a in own]]
        plane = lax.all_gather(values, "core", axis=0, tiled=True)
        plane = lax.all_gather(plane, ("y", "x"), axis=1, tiled=True)
        plane = lax.dynamic_slice_in_dim(plane, yi * group, group, 0)
        return [[plane[n : n + 1]] for n in range(group)]

    def scatter_tokens(values):
        if direct:
            own = values[0].reshape(ny, 2, block, model)
            got = swap(values[1], "core").reshape(ny, 2, block, model)
            sent = pick(own, 1 - xi, 1).astype(F32) + pick(got, 1 - xi, 1).astype(F32)
            sent = sent.astype(BF16)
            kept = pick(own, xi, 1).astype(F32) + pick(got, xi, 1).astype(F32)
            arrived = swap(sent, "x")
            total = (kept + arrived.astype(F32)).astype(BF16)
            got = swap(pick(total, 1 - yi), "y")
            return ordered(pick(total, yi), got, yi, 0)
        plane = jnp.zeros((2 * seqs, length, model), BF16)
        plane = lax.dynamic_update_slice_in_dim(plane, jnp.concatenate(values), yi * group, 0)
        plane = lax.psum_scatter(plane, "core", scatter_dimension=0, tiled=True)
        return lax.psum_scatter(plane, ("y", "x"), scatter_dimension=1, tiled=True)

    if direct:
        lengths = pick(doc_lengths, yi)
        lengths = jnp.concatenate([lengths, swap(lengths, "core")])
    else:
        lengths = lax.all_gather(doc_lengths, "core", axis=0, tiled=True)
        lengths = lax.dynamic_slice_in_dim(lengths, yi * group, group, 0).reshape(-1)
    places = jnp.stack([zi, ci, yi, xi, first, yi, yi, yi]).astype(jnp.int32)
    info = jnp.concatenate([places, lengths.astype(jnp.int32)])

    x_pieces = gather_tokens(hidden_in)
    count = len(x_pieces[0])

    small = [ln1_gain, ln1_bias, ln2_gain, ln2_bias, dense_bias, fc2_bias, qkv_bias, fc1_bias]
    inputs = [qkv_weight, fc1_weight, fc2_weight] + small
    q_type, f_type = of((rows, 3 * hw)), of((rows + 16, nz * piece))
    low_type = of((piece // 2, model))
    out_shape = [q_type, q_type, f_type, f_type, low_type, low_type]
    q_own, q_sent, f_own, f_sent, low_first, low_second = call(
        functools.partial(prep_kernel, d),
        places,
        (1,),
        inputs,
        whole_of(inputs),
        out_shape,
        whole_of(out_shape),
        [],
        (0, 8 * rows * hidden),
    )
    q_got, f_got = swap(q_sent, "core"), swap(f_sent, "core")
    near = first == ci
    q_pair = ordered(q_own, q_got, ci, 0)
    q_all = [q_pair] + [shift(q_pair, k) for k in range(1, nz)]
    f_all = gathered(jnp.where(near, f_own, f_got), jnp.where(near, f_got, f_own))
    low_all = gathered(low_first, low_second)

    cot_pieces = gather_tokens(cotangent)

    dense_all = [dense_weight] + [shift(dense_weight, k) for k in range(1, nz)]

    def dense_rows(place):
        blocks = []
        for b in range(nz // TP):
            total = dense_all[0]
            for k in range(1, nz):
                here = lax.rem(zi - k + nz, nz) == place * (nz // TP) + b
                total = jnp.where(here, dense_all[k], total)
            blocks.append(total)
        return jnp.concatenate(blocks, axis=0)

    dense_own = dense_rows(2 * ci + xi)
    dense_got = swap(dense_rows(2 * peer + xi), "core")

    lane = jnp.arange(wd, dtype=jnp.int32)
    feature = lane % d.hd
    turned = (lane < hw) & (feature < ROT)
    frequency = jnp.exp((feature % (ROT // 2)).astype(F32) * (-2.0 * math.log(10000.0) / ROT))
    angles = jnp.arange(length, dtype=F32)[:, None] * frequency[None, :]
    cos = jnp.where(turned[None, :], jnp.cos(angles), 1.0)
    sin = jnp.where(turned[None, :], jnp.sin(angles), 0.0)

    pairs = d.nh * length * length // 2
    token_type = of((1, length, model))
    tokens_type = of((group, length, model))
    tile = block
    steps = group * length // tile
    per = length // tile
    tiles = pl.BlockSpec((1, tile, model), lambda t, *_: (lax.div(t, per), lax.rem(t, per), 0))
    wide = of((8, 3 * wd), F32)
    inputs = [a for one in x_pieces for a in one] + [a for one in cot_pieces for a in one]
    inputs += f_all + low_all
    out_shape = [tokens_type] * 4 + [of((8, model), F32)] * 2 + [wide]
    out_shape += [of((2 * rows + piece, model))] * nz
    x, cot, out, back, vec_mlp, vec, bias, *up_parts = call(
        functools.partial(mlp_kernel, d, steps, count),
        info,
        (steps,),
        inputs,
        [pl.BlockSpec(memory_space=pl.ANY)] * (2 * group * count) + whole_of(inputs[2 * group * count :]),
        out_shape,
        [tiles] * 4 + whole_of(out_shape[4:]),
        [
            pltpu.VMEM((group, length, model), BF16),
            pltpu.VMEM((group, length, model), BF16),
            pltpu.VMEM((model, nz * piece), BF16),
            pltpu.VMEM((nz * piece, model), BF16),
            pltpu.VMEM((model, nz * piece), F32),
            pltpu.VMEM((nz * piece, model), F32),
            pltpu.VMEM((8, model), F32),
            pltpu.VMEM((2 * nz, 16, 128), F32),
            pltpu.SemaphoreType.DMA((2 * group * count,)),
        ],
        (12 * group * length * model * model, group * length * 12 * model),
    )
    rows_type = of((group, length, wd))
    inputs = [x, cot, out] + q_all + [dense_own, dense_got, vec, bias, cos, sin]
    out_shape = [token_type] * group + [rows_type] * 4 + [of((hw, hw))] * 4
    done = call(
        functools.partial(forward_kernel, d),
        info,
        (group,),
        inputs,
        [per_seq((length, model))] * 3 + whole_of(inputs[3:]),
        out_shape,
        whole_of(out_shape[:group]) + [per_seq((length, wd))] * 4 + whole_of(out_shape[group + 4 :]),
        [
            pltpu.VMEM((model, 3 * wd), BF16),
            pltpu.VMEM((wd, model), BF16),
            pltpu.VMEM((wd, model), F32),
            pltpu.VMEM((1, length, model), BF16),
        ],
        (
            group * (2 * length * model * 5 * wd + 4 * pairs * wd),
            group * length * 2 * (4 * model + 4 * wd),
        ),
    )
    outs = list(done[:group])
    q, k, v, att = done[group : group + 4]
    d_own, d_own_x, d_sent, d_sent_x = done[group + 4 :]

    out_mine = scatter_tokens(outs)
    block_out = (hidden_in.astype(F32) + out_mine.astype(F32) + vec[4]).astype(BF16)

    up_sum = sum_y(sum_z(up_parts))
    low_own = up_sum[2 * rows :]
    sent = lax.dynamic_slice_in_dim(up_sum, peer * rows, rows)
    up_own = lax.dynamic_slice_in_dim(up_sum, ci * rows, rows)
    up_got = swap(sent, "core")

    d_got, d_got_x = swap(d_sent, "core"), swap(d_sent_x, "core")
    d_parts = [d_own, swap(d_own_x, "x"), d_got, swap(d_got_x, "x")]

    def turned_seq(width):
        return pl.BlockSpec((1, length, width), lambda s, *_: (group - 1 - s, 0, 0))

    inputs = [x, cot, back, att, q, k, v] + q_all
    inputs += [dense_own, dense_got, vec, cos, sin, vec_mlp] + d_parts
    out_shape = [token_type] * group + [of((2 * rows + 16, 4 * hw))] * nz
    done = call(
        functools.partial(backward_kernel, d),
        info,
        (group,),
        inputs,
        [turned_seq(model)] * 3 + [turned_seq(wd)] * 4 + whole_of(inputs[7:]),
        out_shape,
        whole_of(out_shape),
        [
            pltpu.VMEM((model, 3 * wd), F32),
            pltpu.VMEM((8, 3 * wd), F32),
            pltpu.VMEM((model, hw), BF16),
            pltpu.VMEM((model, 3 * wd), BF16),
            pltpu.VMEM((wd, model), BF16),
            pltpu.VMEM((length, 3 * wd), BF16),
            pltpu.VMEM((length, wd), BF16),
            pltpu.VMEM((d.nh, length, wd), BF16),
            pltpu.VMEM((d.nh, length, wd), BF16),
            pltpu.VMEM((length, wd), F32),
            pltpu.VMEM((length, model), BF16),
            pltpu.VMEM((1, length, model), BF16),
        ],
        (
            2 * group * length * model * 7 * wd + 10 * group * pairs * wd,
            group * length * 2 * (4 * model + 4 * wd),
        ),
    )
    gs, state = list(done[:group]), done[group:]
    chunk = sum_y(sum_z(state))
    tail = chunk[2 * rows :]
    own = jnp.concatenate([lax.dynamic_slice_in_dim(chunk, ci * rows, rows), tail], axis=0)
    sent = jnp.concatenate([lax.dynamic_slice_in_dim(chunk, peer * rows, rows), tail], axis=0)
    core_got = swap(sent, "core")

    inputs = [up_own, up_got, swap(up_own, "x"), swap(up_got, "x")]
    inputs += [low_own, swap(low_own, "x")]
    out_shape = [of((rows, hidden), F32), of((2 * piece, model), F32)]
    out_upper, out_lower = call(
        functools.partial(upper_kernel, d),
        info,
        (1,),
        inputs,
        whole_of(inputs),
        out_shape,
        whole_of(out_shape),
        [],
        (0, 12 * rows * hidden),
    )
    inputs = [own, core_got, swap(own, "x"), swap(core_got, "x")]
    line = of((rows,), F32)
    out_shape = [of((rows, 3 * model), F32), of((rows, model), F32)] + [line] * 5
    out_shape += [of((2 * piece,), F32), of((3 * rows,), F32)]
    out_qkv, out_dense, v0, v1, v2, v3, v4, v_up, v_qkv = call(
        functools.partial(tail_kernel, d),
        info,
        (1,),
        inputs,
        whole_of(inputs),
        out_shape,
        whole_of(out_shape),
        [pltpu.VMEM((8, 3 * model), F32)],
        (0, 24 * rows * model),
    )

    scaled = scatter_tokens(gs).astype(F32)
    normed, inverse = norm_parts(hidden_in.astype(F32))
    residue = (
        scaled
        - jnp.mean(scaled, axis=-1, keepdims=True)
        - normed * jnp.mean(scaled * normed, axis=-1, keepdims=True)
    )
    input_grad = cotangent.astype(F32) + residue * inverse
    return (
        block_out,
        input_grad,
        v0,
        v1,
        v2,
        v3,
        out_qkv,
        v_qkv,
        out_dense,
        v4,
        out_upper,
        v_up,
        out_lower,
        v4,
    )


def solution(mesh):
    nz, ny = mesh.shape["dp"] // 2, mesh.shape["ctx"] // 2
    fine = Mesh(mesh.devices.reshape(nz, 2, ny, 2), ("z", "core", "y", "x"))
    dp, ctx = ("z", "core"), ("y", "x")
    tokens = P(dp, ctx, None)
    vector, matrix = P(dp), P(dp, None)

    def body(*args):
        return shards((nz, ny), *args)

    return jax.shard_map(
        body,
        mesh=fine,
        in_specs=(
            tokens,
            matrix,
            vector,
            vector,
            vector,
            vector,
            matrix,
            vector,
            matrix,
            vector,
            matrix,
            vector,
            matrix,
            vector,
            tokens,
        ),
        out_specs=(
            tokens,
            tokens,
            vector,
            vector,
            vector,
            vector,
            matrix,
            vector,
            matrix,
            vector,
            matrix,
            vector,
            matrix,
            vector,
        ),
        check_vma=False,
    )
```

```python
import functools
import math

import jax
import jax.numpy as jnp
from jax import lax
from jax.experimental import pallas as pl
from jax.experimental.pallas import tpu as pltpu
from jax.sharding import Mesh
from jax.sharding import PartitionSpec as P


HEADS = 12
ROT = 16
TP = 4

norm_eps = 1e-05
far = -1e30
root_half = 0.7071067811865476
inv_root_two_pi = 0.3989422804014327
F32 = jnp.float32
BF16 = jnp.bfloat16


def dot(a, b):
    return jnp.dot(a, b, preferred_element_type=F32)


def dot_nt(a, b):
    return lax.dot_general(a, b, (((1,), (1,)), ((), ())), preferred_element_type=F32)


def dot_tn(a, b):
    return lax.dot_general(a, b, (((0,), (0,)), ((), ())), preferred_element_type=F32)


def norm_parts(values):
    centre = jnp.mean(values, axis=-1, keepdims=True)
    centred = values - centre
    variance = jnp.mean(centred * centred, axis=-1, keepdims=True)
    inverse = lax.rsqrt(variance + norm_eps)
    return centred * inverse, inverse


class Dims:
    def __init__(self, head_dim, docs, block):
        self.nh = HEADS // TP
        self.hd = head_dim
        self.hw = self.nh * head_dim
        self.docs = docs
        extra = max(docs + 2 * self.nh, 3 * self.nh)
        self.width = -(-(self.hw + extra) // 128) * 128
        self.block = block
        self.scale = head_dim ** (-0.5)


def turn(values, cos, sin, lane, d, direction):
    half = ROT // 2
    ahead = pltpu.roll(values, d.width - half, 1)
    behind = pltpu.roll(values, half, 1)
    partner = jnp.where(lane % d.hd < half, -ahead, behind)
    copies = values.shape[1] // cos.shape[1]
    cos = jnp.concatenate([cos] * copies, axis=1)
    sin = jnp.concatenate([sin] * copies, axis=1)
    return values * cos + partner * (sin * direction)


def head_mask(lane, h, d):
    return (lane >= h * d.hd) & (lane < (h + 1) * d.hd)


def prep_kernel(d, info, qkv, fc1, fc2, *rest):
    small, (q_own, q_sent, f_own, f_sent, low_first, low_second) = rest[:8], rest[8:]
    core, x_at, first = info[1], info[3], info[4]
    rows, hw = d.rows, d.hw
    for c in range(2):
        for x in range(2):

            @pl.when(x_at == x)
            def _():
                wide = fc1[...]
                parts = []
                for z in range(d.nz):
                    at = ((z * 2 + c) * 2 + x) * d.piece
                    parts.append(wide[:, at : at + d.piece])
                chunk = jnp.concatenate(parts, axis=1)
                at = (2 * c + x) * hw
                heads = jnp.concatenate(
                    [qkv[:, t * d.model + at : t * d.model + at + hw] for t in range(3)], axis=1
                )

                @pl.when(core == c)
                def _():
                    f_own[:rows, :] = chunk
                    q_own[...] = heads

                @pl.when(core != c)
                def _():
                    f_sent[:rows, :] = chunk
                    q_sent[...] = heads

    for out in (f_own, f_sent):
        out[rows:, :] = jnp.zeros((out.shape[0] - rows, out.shape[1]), BF16)
        n = rows
        for ref in small:
            line = ref[...].reshape(1, ref.shape[0])
            for e in range(ref.shape[0] // rows):
                out[n : n + 1, :rows] = line[:, e * rows : (e + 1) * rows]
                n += 1
    half = d.piece // 2
    for out, which in ((low_first, first), (low_second, 1 - first)):
        for x in range(2):
            for y in range(2):

                @pl.when((x_at == x) & (which == y))
                def _():
                    at = x * d.piece + y * half
                    out[...] = fc2[at : at + half, :]


def place_heads(d, info, chunks, w):
    w[...] = jnp.zeros_like(w)
    for k, ref in enumerate(chunks):
        block = lax.rem(info[0] - k + d.nz, d.nz)
        for c in range(2):
            at = pl.multiple_of((block * 2 + c) * d.rows, 16)
            for t in range(3):
                w[pl.ds(at, d.rows), t * d.width : t * d.width + d.hw] = ref[
                    c, : d.rows, t * d.hw : (t + 1) * d.hw
                ]


def read_small(d, info, chunks, units, vec, bias):
    nz, rows, hw, wd = d.nz, d.rows, d.hw, d.width
    for which in range(2):
        for k in range(nz):
            block = lax.rem(info[0] - k + nz, nz)
            half = info[4] if which == 0 else 1 - info[4]
            units[block * 2 + half] = chunks[which * nz + k][rows : rows + 16, :128].astype(F32)
    vec[...] = jnp.zeros_like(vec)
    bias[...] = jnp.zeros_like(bias)
    for n in range(4):
        for o in range(2 * nz):
            vec[n : n + 1, o * rows : (o + 1) * rows] = units[o, n : n + 1, :rows]
    for o in range(2 * nz):
        vec[4:5, o * rows : (o + 1) * rows] = units[o, 4:5, :rows] + units[o, 5:6, :rows]
    per = d.piece // rows
    for z in range(nz):
        for e in range(per):
            got = units[2 * z + info[1], pl.ds(9 + per * info[3] + e, 1), :rows]
            vec[5:6, z * d.piece + e * rows : z * d.piece + (e + 1) * rows] = got
    place = 2 * info[1] + info[3]
    for t in range(3):
        for e in range(hw // rows):
            u = t * (d.model // rows) + place * (hw // rows) + e
            got = units[lax.div(u, 3), pl.ds(6 + lax.rem(u, 3), 1), :rows]
            bias[0:1, t * wd + e * rows : t * wd + (e + 1) * rows] = got


def read_dense(d, info, own, got, dense):
    dense[d.hw :, :] = jnp.zeros((dense.shape[0] - d.hw, d.model), BF16)
    for b in range(d.nz // TP):
        take = pl.ds(b * d.rows, d.rows)
        at = pl.multiple_of((2 * b + info[1]) * d.rows, 16)
        dense[pl.ds(at, d.rows), :] = own[take, :]
        at = pl.multiple_of((2 * b + 1 - info[1]) * d.rows, 16)
        dense[pl.ds(at, d.rows), :] = got[take, :]


def forward_kernel(d, info, *refs):
    nz, group = d.nz, d.group
    x, cot, out_in = refs[:3]
    chunks, refs = refs[3 : 3 + nz], refs[3 + nz :]
    dense_own, dense_got, vec, bias, cos, sin = refs[:6]
    outs, refs = refs[6 : 6 + group], refs[6 + group :]
    q_out, k_out, v_out, att_out = refs[:4]
    dense_parts, refs = refs[4:8], refs[8:]
    w, dense, d_dense, out_all, cot_here, out_here, sems = refs
    seq = pl.program_id(0)
    length = x.shape[1]
    late = [
        pltpu.make_async_copy(cot.at[seq], cot_here, sems.at[0]),
        pltpu.make_async_copy(out_in.at[seq], out_here, sems.at[1]),
    ]
    for one in late:
        one.start()
    blk, wd = d.block, d.width

    @pl.when(seq == 0)
    def _():
        place_heads(d, info, chunks, w)
        read_dense(d, info, dense_own, dense_got, dense)
        d_dense[...] = jnp.zeros_like(d_dense)

    lane = lax.broadcasted_iota(jnp.int32, (blk, wd), 1)
    row = lax.broadcasted_iota(jnp.int32, (blk, wd), 0)
    row_s = lax.broadcasted_iota(jnp.int32, (blk, blk), 0)
    col_s = lax.broadcasted_iota(jnp.int32, (blk, blk), 1)
    lse_lane = d.hw + d.docs
    in_seg = (lane >= d.hw) & (lane < lse_lane)
    for i in range(length // blk):
        at = pl.ds(i * blk, blk)
        normed, _ = norm_parts(x[0, at, :].astype(F32))
        a = (normed * vec[0:1, :] + vec[1:2, :]).astype(BF16)
        proj = dot(a, w[...]) + bias[0:1, :]
        c, s = cos[at, :], sin[at, :]
        q = turn(proj[:, :wd], c, s, lane, d, 1.0).astype(BF16).astype(F32) * d.scale
        k = turn(proj[:, wd : 2 * wd], c, s, lane, d, 1.0)
        v = proj[:, 2 * wd :]
        pos = row + i * blk
        seg = jnp.zeros((blk, wd), jnp.int32)
        start = 0
        for n in range(d.docs - 1):
            start = start + info[8 + seq * d.docs + n]
            seg = seg + (pos >= start).astype(jnp.int32)
        same = (lane - d.hw) == seg
        q = jnp.where(lane < d.hw, q, jnp.where(in_seg & same, 1.0, 0.0))
        k = jnp.where(
            lane < d.hw,
            k,
            jnp.where(
                in_seg,
                jnp.where(same, 0.0, far),
                jnp.where(lane < lse_lane + 2 * d.nh, 1.0, 0.0),
            ),
        )
        v = jnp.where(lane < d.hw, v, jnp.where(lane < d.hw + 3 * d.nh, 1.0, 0.0))
        k_out[0, at, :] = k.astype(BF16)
        v_out[0, at, :] = v.astype(BF16)
        total = jnp.zeros((blk, wd), F32)
        q_final = q
        for h in range(d.nh):
            mine = head_mask(lane, h, d)
            qh = jnp.where(mine | in_seg, q, 0.0).astype(BF16)
            near = dot_nt(qh, k_out[0, at, :])
            near = jnp.where(col_s <= row_s, near, far)
            top = jnp.max(near, axis=1, keepdims=True)
            if i:
                past = dot_nt(qh, k_out[0, : i * blk, :])
                top = jnp.maximum(top, jnp.max(past, axis=1, keepdims=True))
            near = jnp.exp(near - top)
            number = jnp.sum(near, axis=1, keepdims=True)
            mixed = dot(near.astype(BF16), v_out[0, at, :])
            if i:
                past = jnp.exp(past - top)
                number = number + jnp.sum(past, axis=1, keepdims=True)
                mixed = mixed + dot(past.astype(BF16), v_out[0, : i * blk, :])
            total = jnp.where(mine, mixed / number, total)
            lse = top + jnp.log(number)
            high = lse.astype(BF16).astype(F32)
            low = lse - high
            q_final = jnp.where(lane == lse_lane + 2 * h, -high, q_final)
            q_final = jnp.where(lane == lse_lane + 2 * h + 1, -low, q_final)
        q_out[0, at, :] = q_final.astype(BF16)
        total = total.astype(BF16)
        att_out[0, at, :] = total

    for one in late:
        one.wait()
    for i in range(length // blk):
        at = pl.ds(i * blk, blk)
        out = out_here[at, :].astype(F32) + dot(att_out[0, at, :], dense[...])
        out_all[0, at, :] = out.astype(BF16)

    for n, ref in enumerate(outs):

        @pl.when(seq == n)
        def _():
            ref[...] = out_all[...]

    d_dense[...] += dot_tn(att_out[0], cot_here[...])

    @pl.when(seq == group - 1)
    def _():
        for c in range(2):
            for at_x in range(2):

                @pl.when((info[1] == c) & (info[3] == at_x))
                def _():
                    for n, ref in enumerate(dense_parts):
                        place = 2 * (c ^ (n // 2)) + (at_x ^ (n % 2))
                        ref[...] = d_dense[: d.hw, place * d.hw : (place + 1) * d.hw].astype(BF16)


def mlp_kernel(d, steps, count, info, *refs):
    nz, group = d.nz, d.group
    x_pieces, refs = refs[: group * count], refs[group * count :]
    cot_pieces, refs = refs[: group * count], refs[group * count :]
    ups, lows, refs = refs[: 2 * nz], refs[2 * nz : 4 * nz], refs[4 * nz :]
    x_out, cot_out, out, back, sums_out, vec, bias = refs[:7]
    grads, refs = refs[7 : 7 + nz], refs[7 + nz :]
    xs, cots, up, low, d_up, d_low, sums, units, sems = refs
    t = pl.program_id(0)
    rows, piece = d.rows, d.piece

    def copies(seq):
        made = []
        for n in range(count):
            size = d.block if count > 1 else xs.shape[1]
            at = 0
            if count > 1:
                y = lax.rem(info[2] + n % 2, 2)
                x_at = lax.rem(info[3] + n // 2, 2)
                at = pl.multiple_of((y * 2 + x_at) * d.block, d.block)
            for which, (pieces, target) in enumerate(((x_pieces, xs), (cot_pieces, cots))):
                source = pieces[seq * count + n]
                source = source if count > 1 else source.at[0]
                sem = sems.at[(seq * count + n) * 2 + which]
                made.append(
                    pltpu.make_async_copy(source, target.at[seq, pl.ds(at, size), :], sem)
                )
        return made

    def low_copies():
        made = []
        for which in range(2):
            for k in range(nz):
                block = lax.rem(info[0] - k + nz, nz)
                half = info[4] if which == 0 else 1 - info[4]
                at = pl.multiple_of((block * 2 + half) * (piece // 2), 16)
                sem = sems.at[2 * group * count + which * nz + k]
                target = low.at[pl.ds(at, piece // 2), :]
                made.append(pltpu.make_async_copy(lows[which * nz + k], target, sem))
        return made

    @pl.when(t == 0)
    def _():
        for one in copies(0) + low_copies():
            one.start()
        for seq in range(1, group):
            for one in copies(seq):
                one.start()

    @pl.when(t == 0)
    def _():
        read_small(d, info, ups, units, vec, bias)
        for which in range(2):
            for k in range(nz):
                block = lax.rem(info[0] - k + nz, nz)
                half = info[4] if which == 0 else 1 - info[4]
                at = pl.multiple_of((block * 2 + half) * rows, 16)
                up[pl.ds(at, rows), :] = ups[which * nz + k][:rows, :]
        for ref in (d_up, d_low, sums):
            ref[...] = jnp.zeros_like(ref)

    tile = x_out.shape[1]
    per = steps // group
    for seq in range(group):

        @pl.when(t == seq * per)
        def _():
            for one in copies(seq) + (low_copies() if seq == 0 else []):
                one.wait()

    at = pl.ds(pl.multiple_of(lax.rem(t, per) * tile, tile), tile)
    cot = cots[lax.div(t, per), at, :]
    cot_out[0] = cot
    xb = xs[lax.div(t, per), at, :]
    x_out[0] = xb
    normed, _ = norm_parts(xb.astype(F32))
    a = (normed * vec[2:3, :] + vec[3:4, :]).astype(BF16)
    upper = dot(a, up[...]) + vec[5:6, :]
    phi = 0.5 * (1.0 + lax.erf(upper * root_half))
    act = (upper * phi).astype(BF16)
    slope = phi + upper * jnp.exp(-0.5 * upper * upper) * inv_root_two_pi
    ug = dot_nt(cot, low[...]) * slope
    ugb = ug.astype(BF16)
    out[0] = dot(act, low[...]).astype(BF16)
    d_low[...] += dot_tn(act, cot)
    d_up[...] += dot_tn(a, ugb)
    mb = dot_nt(ugb, up[...])
    back[0] = (mb * vec[2:3, :]).astype(BF16)
    sums[0:1, :] += jnp.sum(mb * normed, axis=0, keepdims=True)
    sums[1:2, :] += jnp.sum(mb, axis=0, keepdims=True)
    sums[2:3, :] += jnp.sum(cot.astype(F32), axis=0, keepdims=True) * (1.0 / TP)
    sums[3:4, :] += jnp.sum(ug, axis=0, keepdims=True)

    @pl.when(t == steps - 1)
    def _():
        sums_out[...] = sums[...]
        for k in range(nz):
            block = lax.rem(info[0] + k, nz)
            at = pl.multiple_of(block * 2 * rows, 16)
            grads[k][: 2 * rows, :] = d_up[pl.ds(at, 2 * rows), :].astype(BF16)
            at = pl.multiple_of(block * piece, 16)
            grads[k][2 * rows :, :] = d_low[pl.ds(at, piece), :].astype(BF16)


def backward_kernel(d, info, *refs):
    nz, group = d.nz, d.group
    x, cots, back, att, q_in, k_in, v_in = refs[:7]
    chunks, refs = refs[7 : 7 + nz], refs[7 + nz :]
    dense_own, dense_got, vec, cos, sin, vec_mlp = refs[:6]
    d_parts = refs[6:10]
    gs, refs = refs[10 : 10 + group], refs[10 + group :]
    grads, refs = refs[:nz], refs[nz:]
    dw, sums, dw_dense, w, dense, grad, dout, douth, qh, dq, normed_in, g_all = refs[:12]
    x_here, back_here, sems = refs[12:]
    step = pl.program_id(0)
    length = x.shape[1]
    late = [
        pltpu.make_async_copy(x.at[group - 1 - step], x_here, sems.at[0]),
        pltpu.make_async_copy(back.at[group - 1 - step], back_here, sems.at[1]),
    ]
    for one in late:
        one.start()
    blk, wd, rows, hw, model = d.block, d.width, d.rows, d.hw, d.model
    nb = length // blk

    @pl.when(step == 0)
    def _():
        place_heads(d, info, chunks, w)
        read_dense(d, info, dense_own, dense_got, dense)
        dw[...] = jnp.zeros_like(dw)
        sums[...] = jnp.zeros_like(sums)

    lane = lax.broadcasted_iota(jnp.int32, (blk, wd), 1)
    row_s = lax.broadcasted_iota(jnp.int32, (blk, blk), 0)
    col_s = lax.broadcasted_iota(jnp.int32, (blk, blk), 1)
    lse_lane = d.hw + d.docs
    in_seg = (lane >= d.hw) & (lane < lse_lane)

    def block_rows(i):
        return pl.ds(pl.multiple_of(i * blk, blk), blk)

    for i in range(nb):
        at = pl.ds(i * blk, blk)
        og = dot_nt(cots[0, at, :], dense[...]).astype(BF16).astype(F32)
        both = og * att[0, at, :].astype(F32)
        full = og
        q = q_in[0, at, :].astype(F32)
        for h in range(d.nh):
            mine = head_mask(lane, h, d)
            delta = jnp.sum(jnp.where(mine, both, 0.0), axis=1, keepdims=True)
            for piece in range(3):
                part = delta.astype(BF16).astype(F32)
                delta = delta - part
                full = jnp.where(lane == d.hw + 3 * h + piece, -part, full)
            douth[h, at, :] = jnp.where(mine, og, 0.0).astype(BF16)
            qh[h, at, :] = jnp.where(mine, q, 0.0).astype(BF16)
        dout[at, :] = full.astype(BF16)
    dq[...] = jnp.zeros_like(dq)
    for j in range(nb):
        at = pl.ds(j * blk, blk)
        rest = pl.ds(j * blk, length - j * blk)
        k = k_in[0, at, :].astype(F32)
        v = v_in[0, at, :].astype(F32)
        dk = jnp.zeros((blk, wd), F32)
        dv = jnp.zeros((blk, wd), F32)
        for h in range(d.nh):
            mine = head_mask(lane, h, d)
            lse_mine = (lane >= lse_lane + 2 * h) & (lane < lse_lane + 2 * h + 2)
            delta_mine = (lane >= d.hw + 3 * h) & (lane < d.hw + 3 * h + 3)
            kh = jnp.where(mine | in_seg | lse_mine, k, 0.0).astype(BF16)
            vh = jnp.where(mine | delta_mine, v, 0.0).astype(BF16)
            st = dot_nt(kh, q_in[0, rest, :])
            dp = dot_nt(vh, dout[rest, :])
            first = jnp.where(col_s >= row_s, st[:, :blk], far)
            if j < nb - 1:
                st = jnp.concatenate([first, st[:, blk:]], axis=1)
            else:
                st = first
            p = jnp.exp(st)
            ds = (p * dp).astype(BF16)
            dv = dv + dot(p.astype(BF16), douth[h, rest, :])
            dk = dk + dot(ds, qh[h, rest, :])
            dq[rest, :] += dot_tn(ds, kh)
        dk = turn(dk, cos[at, :], sin[at, :], lane, d, -1.0)
        for n, value in ((1, dk), (2, dv)):
            sums[2:3, n * wd : (n + 1) * wd] += jnp.sum(value, axis=0, keepdims=True)
            grad[at, n * wd : (n + 1) * wd] = value.astype(BF16)

    for one in late:
        one.wait()

    def finish(i, _):
        at = block_rows(i)
        part = jnp.where(lane < d.hw, dq[at, :], 0.0) * d.scale
        part = turn(part, cos[at, :], sin[at, :], lane, d, -1.0)
        sums[2:3, :wd] += jnp.sum(part, axis=0, keepdims=True)
        grad[at, :wd] = part.astype(BF16)
        ab = dot_nt(grad[at, :], w[...])
        normed, _ = norm_parts(x_here[at, :].astype(F32))
        normed_in[at, :] = (normed * vec[0:1, :] + vec[1:2, :]).astype(BF16)
        sums[0:1, :model] += jnp.sum(ab * normed, axis=0, keepdims=True)
        sums[1:2, :model] += jnp.sum(ab, axis=0, keepdims=True)
        g_all[0, at, :] = (ab * vec[0:1, :] + back_here[at, :].astype(F32)).astype(BF16)
        return 0

    lax.fori_loop(0, nb, finish, 0)
    for n, ref in enumerate(gs):

        @pl.when(step == group - 1 - n)
        def _():
            ref[...] = g_all[...]

    dw[...] += dot_tn(normed_in[...], grad[...])

    @pl.when(step == group - 1)
    def _():
        for x_at in range(2):
            for c in range(2):

                @pl.when((info[3] == x_at) & (info[1] == c))
                def _():
                    for n, ref in enumerate(d_parts):
                        place = 2 * (c ^ (n // 2)) + (x_at ^ (n % 2))
                        dw_dense[place * hw : (place + 1) * hw, :] = ref[...]

        lines = [
            sums[0:1, :model],
            sums[1:2, :model],
            vec_mlp[0:1, :],
            vec_mlp[1:2, :],
            vec_mlp[2:3, :],
            vec_mlp[3:4, :],
        ]
        for k in range(nz):
            block = lax.rem(info[0] + k, nz)
            at = pl.multiple_of(block * 2 * rows, 16)
            part = dw[pl.ds(at, 2 * rows), :].astype(BF16)
            for t in range(3):
                grads[k][: 2 * rows, t * hw : (t + 1) * hw] = part[:, t * wd : t * wd + hw]
            grads[k][: 2 * rows, 3 * hw :] = dw_dense[pl.ds(at, 2 * rows), :]
            grads[k][2 * rows :, :] = jnp.zeros((16, 4 * hw), BF16)
            for n, line in enumerate(lines):
                grads[k][2 * rows + n : 2 * rows + n + 1, :] = line.astype(BF16)
            for t in range(3):
                grads[k][2 * rows + 6 : 2 * rows + 7, t * hw : (t + 1) * hw] = sums[
                    2:3, t * wd : t * wd + hw
                ].astype(BF16)


def chosen(c, x, info, own, core_got, x_own, x_got):
    first = jnp.where(info[3] == x, own, x_own)
    second = jnp.where(info[3] == x, core_got, x_got)
    return jnp.where(info[1] == c, first, second)


def upper_kernel(d, info, own, core_got, x_own, x_got, low, low_got, out_up, out_low):
    for c in range(2):
        for x in range(2):
            part = chosen(c, x, info, own[...], core_got[...], x_own[...], x_got[...]).astype(F32)
            for z in range(d.nz):
                at = ((z * 2 + c) * 2 + x) * d.piece
                out_up[:, at : at + d.piece] = part[:, z * d.piece : (z + 1) * d.piece]
    for x in range(2):
        mine = jnp.where(info[3] == x, low[...], low_got[...])
        out_low[x * d.piece : (x + 1) * d.piece, :] = mine.astype(F32)


def tail_kernel(d, info, own, core_got, x_own, x_got, *outs):
    out_qkv, out_dense, v0, v1, v2, v3, v4, v5, v_up, v_qkv, scratch = outs
    rows, hw, model = d.rows, d.hw, d.model
    summed = None
    ups = []
    for c in range(2):
        for x in range(2):
            part = chosen(c, x, info, own[...], core_got[...], x_own[...], x_got[...]).astype(F32)
            place = 2 * c + x
            for t in range(3):
                at = t * model + place * hw
                out_qkv[:, at : at + hw] = part[:rows, t * hw : (t + 1) * hw]
                scratch[0:1, at : at + hw] = part[rows + 6 : rows + 7, t * hw : (t + 1) * hw]
            out_dense[:, place * hw : (place + 1) * hw] = part[:rows, 3 * hw :]
            vectors = part[rows : rows + 8, :]
            summed = vectors if summed is None else summed + vectors
            ups.append(vectors[5:6, :])
    mine = info[0] * 2 + info[1]
    turned = pltpu.roll(summed, lax.rem(model - mine * rows, model), 1)
    for n, ref in enumerate((v0, v1, v2, v3, v4)):
        ref[...] = turned[n, :rows]
    v5[...] = turned[4, :rows]
    for x in range(2):
        line = jnp.where(info[1] == 0, ups[x], ups[2 + x])
        line = jnp.broadcast_to(line, (8, line.shape[1]))
        line = pltpu.roll(line, lax.rem(model - info[0] * d.piece, model), 1)
        scratch[1:2, x * d.piece : (x + 1) * d.piece] = line[0:1, : d.piece]
    v_up[...] = scratch[1, : 2 * d.piece]
    line = jnp.broadcast_to(scratch[0:1, :], (8, 3 * model))
    line = pltpu.roll(line, lax.rem(3 * model - mine * 3 * rows, 3 * model), 1)
    v_qkv[...] = line[0, : 3 * rows]


def whole(shape):
    return pl.BlockSpec(shape, lambda *_: (0,) * len(shape))


def whole_of(arrays):
    return [whole(a.shape) for a in arrays]


def per_seq(shape):
    return pl.BlockSpec((1,) + shape, lambda s, *_: (s,) + (0,) * len(shape))


def call(kernel, info, grid, inputs, in_specs, out_shape, out_specs, scratch, cost, aliases=None):
    return pl.pallas_call(
        kernel,
        grid_spec=pltpu.PrefetchScalarGridSpec(
            num_scalar_prefetch=1,
            grid=grid,
            in_specs=in_specs,
            out_specs=out_specs,
            scratch_shapes=scratch,
        ),
        out_shape=out_shape,
        input_output_aliases=aliases or {},
        cost_estimate=pl.CostEstimate(flops=cost[0], bytes_accessed=cost[1], transcendentals=0),
    )(info, *inputs)


def of(shape, dtype=BF16):
    return jax.ShapeDtypeStruct(shape, dtype)


def pick(values, index, axis=0):
    return lax.dynamic_index_in_dim(values, index, axis, keepdims=False)


def ordered(own, other, index, axis):
    return jnp.where(index == 0, jnp.stack([own, other], axis), jnp.stack([other, own], axis))


def swap(values, axis):
    return lax.ppermute(values, axis, [(0, 1), (1, 0)])


def shards(
    sizes,
    hidden_in,
    doc_lengths,
    ln1_gain,
    ln1_bias,
    ln2_gain,
    ln2_bias,
    qkv_weight,
    qkv_bias,
    dense_weight,
    dense_bias,
    fc1_weight,
    fc1_bias,
    fc2_weight,
    fc2_bias,
    cotangent,
):
    nz, ny = sizes
    zi, ci = lax.axis_index("z"), lax.axis_index("core")
    yi, xi = lax.axis_index("y"), lax.axis_index("x")
    peer = 1 - ci
    seqs, block, model = hidden_in.shape
    rows = ln1_gain.shape[0]
    hidden = fc1_weight.shape[1]
    piece = hidden // (nz * TP)
    length = block * ny * 2
    direct = ny == 2 and seqs == 2
    group = 2 * seqs // ny
    d = Dims(model // HEADS, doc_lengths.shape[1], block)
    d.nz, d.rows, d.piece, d.model, d.group = nz, rows, piece, model, group
    hw, wd = d.hw, d.width
    first = yi if ny == 2 else jnp.zeros_like(yi)

    def shift(values, k):
        return lax.ppermute(values, "z", [(i, (i + k) % nz) for i in range(nz)])

    def gathered(half, other):
        firsts = [half] + [shift(half, k) for k in range(1, nz)]
        if ny == 2:
            seconds = [other] + [swap(firsts[k], "y") for k in range(1, nz)]
        else:
            seconds = [other] + [shift(other, k) for k in range(1, nz)]
        return firsts + seconds

    def sum_z(parts):
        got = [shift(parts[k], k) for k in range(1, nz)]
        total = parts[0].astype(F32)
        for part in got:
            total = total + part.astype(F32)
        return total.astype(BF16)

    def sum_y(part):
        if ny == 2:
            got = swap(part, "y")
            return (part.astype(F32) + got.astype(F32)).astype(BF16)
        return lax.psum(part, "y")

    def gather_tokens(values):
        if direct:
            mine, sent = pick(values, yi), pick(values, 1 - yi)
            got = swap(sent, "y")
            own = [mine, got, swap(mine, "x"), swap(got, "x")]
            return [own, [swap(a, "core") for a in own]]
        plane = lax.all_gather(values, "core", axis=0, tiled=True)
        plane = lax.all_gather(plane, ("y", "x"), axis=1, tiled=True)
        plane = lax.dynamic_slice_in_dim(plane, yi * group, group, 0)
        return [[plane[n : n + 1]] for n in range(group)]

    def scatter_tokens(values):
        if direct:
            own = values[0].reshape(ny, 2, block, model)
            got = swap(values[1], "core").reshape(ny, 2, block, model)
            sent = pick(own, 1 - xi, 1).astype(F32) + pick(got, 1 - xi, 1).astype(F32)
            sent = sent.astype(BF16)
            arrived = swap(sent, "x")
            own, got, arrived = lax.optimization_barrier((own, got, arrived))
            kept = pick(own, xi, 1).astype(F32) + pick(got, xi, 1).astype(F32)
            total = (kept + arrived.astype(F32)).astype(BF16)
            got = swap(pick(total, 1 - yi), "y")
            return ordered(pick(total, yi), got, yi, 0)
        plane = jnp.zeros((2 * seqs, length, model), BF16)
        plane = lax.dynamic_update_slice_in_dim(plane, jnp.concatenate(values), yi * group, 0)
        plane = lax.psum_scatter(plane, "core", scatter_dimension=0, tiled=True)
        return lax.psum_scatter(plane, ("y", "x"), scatter_dimension=1, tiled=True)

    if direct:
        lengths = pick(doc_lengths, yi)
        lengths = jnp.concatenate([lengths, swap(lengths, "core")])
    else:
        lengths = lax.all_gather(doc_lengths, "core", axis=0, tiled=True)
        lengths = lax.dynamic_slice_in_dim(lengths, yi * group, group, 0).reshape(-1)
    places = jnp.stack([zi, ci, yi, xi, first, yi, yi, yi]).astype(jnp.int32)
    info = jnp.concatenate([places, lengths.astype(jnp.int32)])

    x_pieces = gather_tokens(hidden_in)
    count = len(x_pieces[0])

    small = [ln1_gain, ln1_bias, ln2_gain, ln2_bias, dense_bias, fc2_bias, qkv_bias, fc1_bias]
    inputs = [qkv_weight, fc1_weight, fc2_weight] + small
    q_type, f_type = of((rows, 3 * hw)), of((rows + 16, nz * piece))
    low_type = of((piece // 2, model))
    out_shape = [q_type, q_type, f_type, f_type, low_type, low_type]
    q_own, q_sent, f_own, f_sent, low_first, low_second = call(
        functools.partial(prep_kernel, d),
        places,
        (1,),
        inputs,
        whole_of(inputs),
        out_shape,
        whole_of(out_shape),
        [],
        (0, 8 * rows * hidden),
    )
    q_got, f_got = swap(q_sent, "core"), swap(f_sent, "core")
    near = first == ci
    q_pair = ordered(q_own, q_got, ci, 0)
    q_all = [q_pair] + [shift(q_pair, k) for k in range(1, nz)]
    f_all = gathered(jnp.where(near, f_own, f_got), jnp.where(near, f_got, f_own))
    low_all = gathered(low_first, low_second)

    cot_pieces = gather_tokens(cotangent)

    dense_all = [dense_weight] + [shift(dense_weight, k) for k in range(1, nz)]

    def dense_rows(place):
        blocks = []
        for b in range(nz // TP):
            total = dense_all[0]
            for k in range(1, nz):
                here = lax.rem(zi - k + nz, nz) == place * (nz // TP) + b
                total = jnp.where(here, dense_all[k], total)
            blocks.append(total)
        return jnp.concatenate(blocks, axis=0)

    dense_own = dense_rows(2 * ci + xi)
    dense_got = swap(dense_rows(2 * peer + xi), "core")

    feature = jnp.arange(math.lcm(d.hd, 128), dtype=jnp.int32) % d.hd
    turned = feature < ROT
    frequency = jnp.exp((feature % (ROT // 2)).astype(F32) * (-2.0 * math.log(10000.0) / ROT))
    angles = jnp.arange(length, dtype=F32)[:, None] * frequency[None, :]
    cos = jnp.where(turned[None, :], jnp.cos(angles), 1.0)
    sin = jnp.where(turned[None, :], jnp.sin(angles), 0.0)

    pairs = d.nh * length * length // 2
    token_type = of((1, length, model))
    tokens_type = of((group, length, model))
    tile = block
    steps = group * length // tile
    per = length // tile
    tiles = pl.BlockSpec((1, tile, model), lambda t, *_: (lax.div(t, per), lax.rem(t, per), 0))
    wide = of((8, 3 * wd), F32)
    inputs = [a for one in x_pieces for a in one] + [a for one in cot_pieces for a in one]
    inputs += f_all + low_all
    out_shape = [tokens_type] * 4 + [of((8, model), F32)] * 2 + [wide]
    out_shape += [of((2 * rows + piece, model))] * nz
    x, cot, out, back, vec_mlp, vec, bias, *up_parts = call(
        functools.partial(mlp_kernel, d, steps, count),
        info,
        (steps,),
        inputs,
        [pl.BlockSpec(memory_space=pl.ANY)] * (2 * group * count)
        + whole_of(f_all)
        + [pl.BlockSpec(memory_space=pl.ANY)] * len(low_all),
        out_shape,
        [tiles] * 4 + whole_of(out_shape[4:]),
        [
            pltpu.VMEM((group, length, model), BF16),
            pltpu.VMEM((group, length, model), BF16),
            pltpu.VMEM((model, nz * piece), BF16),
            pltpu.VMEM((nz * piece, model), BF16),
            pltpu.VMEM((model, nz * piece), F32),
            pltpu.VMEM((nz * piece, model), F32),
            pltpu.VMEM((8, model), F32),
            pltpu.VMEM((2 * nz, 16, 128), F32),
            pltpu.SemaphoreType.DMA((2 * group * count + 2 * nz,)),
        ],
        (12 * group * length * model * model, group * length * 12 * model),
    )
    rows_type = of((group, length, wd))
    inputs = [x, cot, out] + q_all + [dense_own, dense_got, vec, bias, cos, sin]
    out_shape = [token_type] * group + [rows_type] * 4 + [of((hw, hw))] * 4
    done = call(
        functools.partial(forward_kernel, d),
        info,
        (group,),
        inputs,
        [per_seq((length, model))] + [pl.BlockSpec(memory_space=pl.ANY)] * 2 + whole_of(inputs[3:]),
        out_shape,
        whole_of(out_shape[:group]) + [per_seq((length, wd))] * 4 + whole_of(out_shape[group + 4 :]),
        [
            pltpu.VMEM((model, 3 * wd), BF16),
            pltpu.VMEM((wd, model), BF16),
            pltpu.VMEM((wd, model), F32),
            pltpu.VMEM((1, length, model), BF16),
            pltpu.VMEM((length, model), BF16),
            pltpu.VMEM((length, model), BF16),
            pltpu.SemaphoreType.DMA((2,)),
        ],
        (
            group * (2 * length * model * 5 * wd + 4 * pairs * wd),
            group * length * 2 * (4 * model + 4 * wd),
        ),
    )
    outs = list(done[:group])
    q, k, v, att = done[group : group + 4]
    d_own, d_own_x, d_sent, d_sent_x = done[group + 4 :]

    out_mine = scatter_tokens(outs)
    block_out = (hidden_in.astype(F32) + out_mine.astype(F32) + vec[4]).astype(BF16)

    up_sum = sum_y(sum_z(up_parts))
    low_own = up_sum[2 * rows :]
    sent = lax.dynamic_slice_in_dim(up_sum, peer * rows, rows)
    up_own = lax.dynamic_slice_in_dim(up_sum, ci * rows, rows)
    up_got = swap(sent, "core")

    d_got, d_got_x = swap(d_sent, "core"), swap(d_sent_x, "core")
    d_parts = [d_own, swap(d_own_x, "x"), d_got, swap(d_got_x, "x")]

    anywhere = pl.BlockSpec(memory_space=pl.ANY)

    def turned_seq(width):
        return pl.BlockSpec((1, length, width), lambda s, *_: (group - 1 - s, 0, 0))

    inputs = [x, cot, back, att, q, k, v] + q_all
    inputs += [dense_own, dense_got, vec, cos, sin, vec_mlp] + d_parts
    out_shape = [token_type] * group + [of((2 * rows + 16, 4 * hw))] * nz
    done = call(
        functools.partial(backward_kernel, d),
        info,
        (group,),
        inputs,
        [anywhere, turned_seq(model), anywhere] + [turned_seq(wd)] * 4 + whole_of(inputs[7:]),
        out_shape,
        whole_of(out_shape),
        [
            pltpu.VMEM((model, 3 * wd), F32),
            pltpu.VMEM((8, 3 * wd), F32),
            pltpu.VMEM((model, hw), BF16),
            pltpu.VMEM((model, 3 * wd), BF16),
            pltpu.VMEM((wd, model), BF16),
            pltpu.VMEM((length, 3 * wd), BF16),
            pltpu.VMEM((length, wd), BF16),
            pltpu.VMEM((d.nh, length, wd), BF16),
            pltpu.VMEM((d.nh, length, wd), BF16),
            pltpu.VMEM((length, wd), F32),
            pltpu.VMEM((length, model), BF16),
            pltpu.VMEM((1, length, model), BF16),
            pltpu.VMEM((length, model), BF16),
            pltpu.VMEM((length, model), BF16),
            pltpu.SemaphoreType.DMA((2,)),
        ],
        (
            2 * group * length * model * 7 * wd + 10 * group * pairs * wd,
            group * length * 2 * (4 * model + 4 * wd),
        ),
    )
    gs, state = list(done[:group]), done[group:]
    chunk = sum_y(sum_z(state))
    tail = chunk[2 * rows :]
    own = jnp.concatenate([lax.dynamic_slice_in_dim(chunk, ci * rows, rows), tail], axis=0)
    sent = jnp.concatenate([lax.dynamic_slice_in_dim(chunk, peer * rows, rows), tail], axis=0)
    core_got = swap(sent, "core")

    inputs = [up_own, up_got, swap(up_own, "x"), swap(up_got, "x")]
    inputs += [low_own, swap(low_own, "x")]
    out_shape = [of((rows, hidden), F32), of((2 * piece, model), F32)]
    out_upper, out_lower = call(
        functools.partial(upper_kernel, d),
        info,
        (1,),
        inputs,
        whole_of(inputs),
        out_shape,
        whole_of(out_shape),
        [],
        (0, 12 * rows * hidden),
    )
    inputs = [own, core_got, swap(own, "x"), swap(core_got, "x")]
    line = of((rows,), F32)
    out_shape = [of((rows, 3 * model), F32), of((rows, model), F32)] + [line] * 6
    out_shape += [of((2 * piece,), F32), of((3 * rows,), F32)]
    out_qkv, out_dense, v0, v1, v2, v3, v4, v5, v_up, v_qkv = call(
        functools.partial(tail_kernel, d),
        info,
        (1,),
        inputs,
        whole_of(inputs),
        out_shape,
        whole_of(out_shape),
        [pltpu.VMEM((8, 3 * model), F32)],
        (0, 24 * rows * model),
    )

    scaled = scatter_tokens(gs).astype(F32)
    normed, inverse = norm_parts(hidden_in.astype(F32))
    residue = (
        scaled
        - jnp.mean(scaled, axis=-1, keepdims=True)
        - normed * jnp.mean(scaled * normed, axis=-1, keepdims=True)
    )
    input_grad = cotangent.astype(F32) + residue * inverse
    return (
        block_out,
        input_grad,
        v0,
        v1,
        v2,
        v3,
        out_qkv,
        v_qkv,
        out_dense,
        v4,
        out_upper,
        v_up,
        out_lower,
        v5,
    )


def solution(mesh):
    nz, ny = mesh.shape["dp"] // 2, mesh.shape["ctx"] // 2
    fine = Mesh(mesh.devices.reshape(nz, 2, ny, 2), ("z", "core", "y", "x"))
    dp, ctx = ("z", "core"), ("y", "x")
    tokens = P(dp, ctx, None)
    vector, matrix = P(dp), P(dp, None)

    def body(*args):
        return shards((nz, ny), *args)

    return jax.shard_map(
        body,
        mesh=fine,
        in_specs=(
            tokens,
            matrix,
            vector,
            vector,
            vector,
            vector,
            matrix,
            vector,
            matrix,
            vector,
            matrix,
            vector,
            matrix,
            vector,
            tokens,
        ),
        out_specs=(
            tokens,
            tokens,
            vector,
            vector,
            vector,
            vector,
            matrix,
            vector,
            matrix,
            vector,
            matrix,
            vector,
            matrix,
            vector,
        ),
        check_vma=False,
    )
```

```python
import functools
import math

import jax
import jax.numpy as jnp
from jax import lax
from jax.experimental import pallas as pl
from jax.experimental.pallas import tpu as pltpu
from jax.sharding import Mesh
from jax.sharding import PartitionSpec as P


HEADS = 12
ROT = 16
TP = 4

norm_eps = 1e-05
far = -1e30
root_half = 0.7071067811865476
inv_root_two_pi = 0.3989422804014327
F32 = jnp.float32
BF16 = jnp.bfloat16


def dot(a, b):
    return jnp.dot(a, b, preferred_element_type=F32)


def dot_nt(a, b):
    return lax.dot_general(a, b, (((1,), (1,)), ((), ())), preferred_element_type=F32)


def dot_tn(a, b):
    return lax.dot_general(a, b, (((0,), (0,)), ((), ())), preferred_element_type=F32)


def norm_parts(values):
    centre = jnp.mean(values, axis=-1, keepdims=True)
    centred = values - centre
    variance = jnp.mean(centred * centred, axis=-1, keepdims=True)
    inverse = lax.rsqrt(variance + norm_eps)
    return centred * inverse, inverse


class Dims:
    def __init__(self, head_dim, docs, block):
        self.nh = HEADS // TP
        self.hd = head_dim
        self.hw = self.nh * head_dim
        self.docs = docs
        extra = max(docs + 2 * self.nh, 3 * self.nh)
        self.width = -(-(self.hw + extra) // 128) * 128
        self.block = block
        self.scale = head_dim ** (-0.5)


def turn(values, cos, sin, lane, d, direction):
    half = ROT // 2
    ahead = pltpu.roll(values, d.width - half, 1)
    behind = pltpu.roll(values, half, 1)
    partner = jnp.where(lane % d.hd < half, -ahead, behind)
    copies = values.shape[1] // cos.shape[1]
    cos = jnp.concatenate([cos] * copies, axis=1)
    sin = jnp.concatenate([sin] * copies, axis=1)
    return values * cos + partner * (sin * direction)


def head_mask(lane, h, d):
    return (lane >= h * d.hd) & (lane < (h + 1) * d.hd)


def prep_kernel(d, info, qkv, fc1, fc2, *rest):
    small, (q_own, q_sent, f_own, f_sent, low_first, low_second) = rest[:8], rest[8:]
    core, x_at, first = info[1], info[3], info[4]
    rows, hw = d.rows, d.hw
    for c in range(2):
        for x in range(2):

            @pl.when(x_at == x)
            def _():
                wide = fc1[...]
                parts = []
                for z in range(d.nz):
                    at = ((z * 2 + c) * 2 + x) * d.piece
                    parts.append(wide[:, at : at + d.piece])
                chunk = jnp.concatenate(parts, axis=1)
                at = (2 * c + x) * hw
                heads = jnp.concatenate(
                    [qkv[:, t * d.model + at : t * d.model + at + hw] for t in range(3)], axis=1
                )

                @pl.when(core == c)
                def _():
                    f_own[:rows, :] = chunk
                    q_own[...] = heads

                @pl.when(core != c)
                def _():
                    f_sent[:rows, :] = chunk
                    q_sent[...] = heads

    for out in (f_own, f_sent):
        out[rows:, :] = jnp.zeros((out.shape[0] - rows, out.shape[1]), BF16)
        n = rows
        for ref in small:
            line = ref[...].reshape(1, ref.shape[0])
            for e in range(ref.shape[0] // rows):
                out[n : n + 1, :rows] = line[:, e * rows : (e + 1) * rows]
                n += 1
    half = d.piece // 2
    for out, which in ((low_first, first), (low_second, 1 - first)):
        for x in range(2):
            for y in range(2):

                @pl.when((x_at == x) & (which == y))
                def _():
                    at = x * d.piece + y * half
                    out[...] = fc2[at : at + half, :]


def place_heads(d, info, chunks, w):
    w[...] = jnp.zeros_like(w)
    for k, ref in enumerate(chunks):
        block = lax.rem(info[0] - k + d.nz, d.nz)
        for c in range(2):
            at = pl.multiple_of((block * 2 + c) * d.rows, 16)
            for t in range(3):
                w[pl.ds(at, d.rows), t * d.width : t * d.width + d.hw] = ref[
                    c, : d.rows, t * d.hw : (t + 1) * d.hw
                ]


def read_small(d, info, chunks, units, vec, bias):
    nz, rows, hw, wd = d.nz, d.rows, d.hw, d.width
    for which in range(2):
        for k in range(nz):
            block = lax.rem(info[0] - k + nz, nz)
            half = info[4] if which == 0 else 1 - info[4]
            units[block * 2 + half] = chunks[which * nz + k][rows : rows + 16, :128].astype(F32)
    vec[...] = jnp.zeros_like(vec)
    bias[...] = jnp.zeros_like(bias)
    for n in range(4):
        for o in range(2 * nz):
            vec[n : n + 1, o * rows : (o + 1) * rows] = units[o, n : n + 1, :rows]
    for o in range(2 * nz):
        vec[4:5, o * rows : (o + 1) * rows] = units[o, 4:5, :rows] + units[o, 5:6, :rows]
    per = d.piece // rows
    for z in range(nz):
        for e in range(per):
            got = units[2 * z + info[1], pl.ds(9 + per * info[3] + e, 1), :rows]
            vec[5:6, z * d.piece + e * rows : z * d.piece + (e + 1) * rows] = got
    place = 2 * info[1] + info[3]
    for t in range(3):
        for e in range(hw // rows):
            u = t * (d.model // rows) + place * (hw // rows) + e
            got = units[lax.div(u, 3), pl.ds(6 + lax.rem(u, 3), 1), :rows]
            bias[0:1, t * wd + e * rows : t * wd + (e + 1) * rows] = got


def read_dense(d, info, own, got, dense):
    dense[d.hw :, :] = jnp.zeros((dense.shape[0] - d.hw, d.model), BF16)
    for b in range(d.nz // TP):
        take = pl.ds(b * d.rows, d.rows)
        at = pl.multiple_of((2 * b + info[1]) * d.rows, 16)
        dense[pl.ds(at, d.rows), :] = own[take, :]
        at = pl.multiple_of((2 * b + 1 - info[1]) * d.rows, 16)
        dense[pl.ds(at, d.rows), :] = got[take, :]


def forward_kernel(d, info, *refs):
    nz, group = d.nz, d.group
    x, cot, out_in = refs[:3]
    chunks, refs = refs[3 : 3 + nz], refs[3 + nz :]
    dense_own, dense_got, vec, bias, cos, sin = refs[:6]
    outs, refs = refs[6 : 6 + group], refs[6 + group :]
    q_out, k_out, v_out, att_out = refs[:4]
    dense_parts, refs = refs[4:8], refs[8:]
    w, dense, d_dense, out_all, cot_here, out_here, sems = refs
    seq = pl.program_id(0)
    length = x.shape[1]
    late = [
        pltpu.make_async_copy(cot.at[seq], cot_here, sems.at[0]),
        pltpu.make_async_copy(out_in.at[seq], out_here, sems.at[1]),
    ]
    for one in late:
        one.start()
    blk, wd = d.block, d.width

    @pl.when(seq == 0)
    def _():
        place_heads(d, info, chunks, w)
        read_dense(d, info, dense_own, dense_got, dense)
        d_dense[...] = jnp.zeros_like(d_dense)

    lane = lax.broadcasted_iota(jnp.int32, (blk, wd), 1)
    row = lax.broadcasted_iota(jnp.int32, (blk, wd), 0)
    row_s = lax.broadcasted_iota(jnp.int32, (blk, blk), 0)
    col_s = lax.broadcasted_iota(jnp.int32, (blk, blk), 1)
    lse_lane = d.hw + d.docs
    in_seg = (lane >= d.hw) & (lane < lse_lane)
    for i in range(length // blk):
        at = pl.ds(i * blk, blk)
        normed, _ = norm_parts(x[0, at, :].astype(F32))
        a = (normed * vec[0:1, :] + vec[1:2, :]).astype(BF16)
        proj = dot(a, w[...]) + bias[0:1, :]
        c, s = cos[at, :], sin[at, :]
        q = turn(proj[:, :wd], c, s, lane, d, 1.0).astype(BF16).astype(F32) * d.scale
        k = turn(proj[:, wd : 2 * wd], c, s, lane, d, 1.0)
        v = proj[:, 2 * wd :]
        pos = row + i * blk
        seg = jnp.zeros((blk, wd), jnp.int32)
        start = 0
        for n in range(d.docs - 1):
            start = start + info[8 + seq * d.docs + n]
            seg = seg + (pos >= start).astype(jnp.int32)
        same = (lane - d.hw) == seg
        q = jnp.where(lane < d.hw, q, jnp.where(in_seg & same, 1.0, 0.0))
        k = jnp.where(
            lane < d.hw,
            k,
            jnp.where(
                in_seg,
                jnp.where(same, 0.0, far),
                jnp.where(lane < lse_lane + 2 * d.nh, 1.0, 0.0),
            ),
        )
        v = jnp.where(lane < d.hw, v, jnp.where(lane < d.hw + 3 * d.nh, 1.0, 0.0))
        k_out[0, at, :] = k.astype(BF16)
        v_out[0, at, :] = v.astype(BF16)
        total = jnp.zeros((blk, wd), F32)
        q_final = q
        for h in range(d.nh):
            mine = head_mask(lane, h, d)
            qh = jnp.where(mine | in_seg, q, 0.0).astype(BF16)
            near = dot_nt(qh, k_out[0, at, :])
            near = jnp.where(col_s <= row_s, near, far)
            top = jnp.max(near, axis=1, keepdims=True)
            if i:
                past = dot_nt(qh, k_out[0, : i * blk, :])
                top = jnp.maximum(top, jnp.max(past, axis=1, keepdims=True))
            near = jnp.exp(near - top)
            number = jnp.sum(near, axis=1, keepdims=True)
            mixed = dot(near.astype(BF16), v_out[0, at, :])
            if i:
                past = jnp.exp(past - top)
                number = number + jnp.sum(past, axis=1, keepdims=True)
                mixed = mixed + dot(past.astype(BF16), v_out[0, : i * blk, :])
            total = jnp.where(mine, mixed / number, total)
            lse = top + jnp.log(number)
            high = lse.astype(BF16).astype(F32)
            low = lse - high
            q_final = jnp.where(lane == lse_lane + 2 * h, -high, q_final)
            q_final = jnp.where(lane == lse_lane + 2 * h + 1, -low, q_final)
        q_out[0, at, :] = q_final.astype(BF16)
        total = total.astype(BF16)
        att_out[0, at, :] = total

    for one in late:
        one.wait()
    for i in range(length // blk):
        at = pl.ds(i * blk, blk)
        out = out_here[at, :].astype(F32) + dot(att_out[0, at, :], dense[...])
        out_all[0, at, :] = out.astype(BF16)

    for n, ref in enumerate(outs):

        @pl.when(seq == n)
        def _():
            ref[...] = out_all[...]

    d_dense[...] += dot_tn(att_out[0], cot_here[...])

    @pl.when(seq == group - 1)
    def _():
        for c in range(2):
            for at_x in range(2):

                @pl.when((info[1] == c) & (info[3] == at_x))
                def _():
                    for n, ref in enumerate(dense_parts):
                        place = 2 * (c ^ (n // 2)) + (at_x ^ (n % 2))
                        ref[...] = d_dense[: d.hw, place * d.hw : (place + 1) * d.hw].astype(BF16)


def mlp_kernel(d, steps, count, info, *refs):
    nz, group = d.nz, d.group
    x_pieces, refs = refs[: group * count], refs[group * count :]
    cot_pieces, refs = refs[: group * count], refs[group * count :]
    ups, lows, refs = refs[: 2 * nz], refs[2 * nz : 4 * nz], refs[4 * nz :]
    x_out, cot_out, out, back, sums_out, vec, bias = refs[:7]
    grads, refs = refs[7 : 7 + nz], refs[7 + nz :]
    xs, cots, up, low, d_up, d_low, sums, units, sems = refs
    t = pl.program_id(0)
    rows, piece = d.rows, d.piece

    def copies(seq):
        made = []
        for n in range(count):
            size = d.block if count > 1 else xs.shape[1]
            at = 0
            if count > 1:
                y = lax.rem(info[2] + n % 2, 2)
                x_at = lax.rem(info[3] + n // 2, 2)
                at = pl.multiple_of((y * 2 + x_at) * d.block, d.block)
            for which, (pieces, target) in enumerate(((x_pieces, xs), (cot_pieces, cots))):
                source = pieces[seq * count + n]
                source = source if count > 1 else source.at[0]
                sem = sems.at[(seq * count + n) * 2 + which]
                made.append(
                    pltpu.make_async_copy(source, target.at[seq, pl.ds(at, size), :], sem)
                )
        return made

    def low_copies():
        made = []
        for which in range(2):
            for k in range(nz):
                block = lax.rem(info[0] - k + nz, nz)
                half = info[4] if which == 0 else 1 - info[4]
                at = pl.multiple_of((block * 2 + half) * (piece // 2), 16)
                sem = sems.at[2 * group * count + which * nz + k]
                target = low.at[pl.ds(at, piece // 2), :]
                made.append(pltpu.make_async_copy(lows[which * nz + k], target, sem))
        return made

    @pl.when(t == 0)
    def _():
        for one in copies(0) + low_copies():
            one.start()
        for seq in range(1, group):
            for one in copies(seq):
                one.start()

    @pl.when(t == 0)
    def _():
        read_small(d, info, ups, units, vec, bias)
        for which in range(2):
            for k in range(nz):
                block = lax.rem(info[0] - k + nz, nz)
                half = info[4] if which == 0 else 1 - info[4]
                at = pl.multiple_of((block * 2 + half) * rows, 16)
                up[pl.ds(at, rows), :] = ups[which * nz + k][:rows, :]
        for ref in (d_up, d_low, sums):
            ref[...] = jnp.zeros_like(ref)

    tile = x_out.shape[1]
    per = steps // group
    for seq in range(group):

        @pl.when(t == seq * per)
        def _():
            for one in copies(seq) + (low_copies() if seq == 0 else []):
                one.wait()

    at = pl.ds(pl.multiple_of(lax.rem(t, per) * tile, tile), tile)
    cot = cots[lax.div(t, per), at, :]
    cot_out[0] = cot
    xb = xs[lax.div(t, per), at, :]
    x_out[0] = xb
    normed, _ = norm_parts(xb.astype(F32))
    a = (normed * vec[2:3, :] + vec[3:4, :]).astype(BF16)
    upper = dot(a, up[...]) + vec[5:6, :]
    phi = 0.5 * (1.0 + lax.erf(upper * root_half))
    act = (upper * phi).astype(BF16)
    slope = phi + upper * jnp.exp(-0.5 * upper * upper) * inv_root_two_pi
    ug = dot_nt(cot, low[...]) * slope
    ugb = ug.astype(BF16)
    out[0] = dot(act, low[...]).astype(BF16)
    d_low[...] += dot_tn(act, cot)
    d_up[...] += dot_tn(a, ugb)
    mb = dot_nt(ugb, up[...])
    back[0] = (mb * vec[2:3, :]).astype(BF16)
    sums[0:1, :] += jnp.sum(mb * normed, axis=0, keepdims=True)
    sums[1:2, :] += jnp.sum(mb, axis=0, keepdims=True)
    sums[2:3, :] += jnp.sum(cot.astype(F32), axis=0, keepdims=True) * (1.0 / TP)
    sums[3:4, :] += jnp.sum(ug, axis=0, keepdims=True)

    @pl.when(t == steps - 1)
    def _():
        sums_out[...] = sums[...]
        for k in range(nz):
            block = lax.rem(info[0] + k, nz)
            at = pl.multiple_of(block * 2 * rows, 16)
            grads[k][: 2 * rows, :] = d_up[pl.ds(at, 2 * rows), :].astype(BF16)
            at = pl.multiple_of(block * piece, 16)
            grads[k][2 * rows :, :] = d_low[pl.ds(at, piece), :].astype(BF16)


def backward_kernel(d, info, *refs):
    nz, group = d.nz, d.group
    x, cots, back, att, q_in, k_in, v_in = refs[:7]
    chunks, refs = refs[7 : 7 + nz], refs[7 + nz :]
    dense_own, dense_got, vec, cos, sin, vec_mlp = refs[:6]
    d_parts = refs[6:10]
    gs, refs = refs[10 : 10 + group], refs[10 + group :]
    grads, refs = refs[:nz], refs[nz:]
    dw, sums, dw_dense, w, dense, grad, dout, douth, qh, dq, normed_in, g_all = refs[:12]
    x_here, back_here, sems = refs[12:]
    step = pl.program_id(0)
    length = x.shape[1]
    late = [
        pltpu.make_async_copy(x.at[group - 1 - step], x_here, sems.at[0]),
        pltpu.make_async_copy(back.at[group - 1 - step], back_here, sems.at[1]),
    ]
    for one in late:
        one.start()
    blk, wd, rows, hw, model = d.block, d.width, d.rows, d.hw, d.model
    nb = length // blk

    @pl.when(step == 0)
    def _():
        place_heads(d, info, chunks, w)
        read_dense(d, info, dense_own, dense_got, dense)
        dw[...] = jnp.zeros_like(dw)
        sums[...] = jnp.zeros_like(sums)

    lane = lax.broadcasted_iota(jnp.int32, (blk, wd), 1)
    row_s = lax.broadcasted_iota(jnp.int32, (blk, blk), 0)
    col_s = lax.broadcasted_iota(jnp.int32, (blk, blk), 1)
    lse_lane = d.hw + d.docs
    in_seg = (lane >= d.hw) & (lane < lse_lane)

    def block_rows(i):
        return pl.ds(pl.multiple_of(i * blk, blk), blk)

    for i in range(nb):
        at = pl.ds(i * blk, blk)
        og = dot_nt(cots[0, at, :], dense[...]).astype(BF16).astype(F32)
        both = og * att[0, at, :].astype(F32)
        full = og
        q = q_in[0, at, :].astype(F32)
        for h in range(d.nh):
            mine = head_mask(lane, h, d)
            delta = jnp.sum(jnp.where(mine, both, 0.0), axis=1, keepdims=True)
            for piece in range(3):
                part = delta.astype(BF16).astype(F32)
                delta = delta - part
                full = jnp.where(lane == d.hw + 3 * h + piece, -part, full)
            douth[h, at, :] = jnp.where(mine, og, 0.0).astype(BF16)
            qh[h, at, :] = jnp.where(mine, q, 0.0).astype(BF16)
        dout[at, :] = full.astype(BF16)
    dq[...] = jnp.zeros_like(dq)
    for j in range(nb):
        at = pl.ds(j * blk, blk)
        rest = pl.ds(j * blk, length - j * blk)
        k = k_in[0, at, :].astype(F32)
        v = v_in[0, at, :].astype(F32)
        dk = jnp.zeros((blk, wd), F32)
        dv = jnp.zeros((blk, wd), F32)
        for h in range(d.nh):
            mine = head_mask(lane, h, d)
            lse_mine = (lane >= lse_lane + 2 * h) & (lane < lse_lane + 2 * h + 2)
            delta_mine = (lane >= d.hw + 3 * h) & (lane < d.hw + 3 * h + 3)
            kh = jnp.where(mine | in_seg | lse_mine, k, 0.0).astype(BF16)
            vh = jnp.where(mine | delta_mine, v, 0.0).astype(BF16)
            st = dot_nt(kh, q_in[0, rest, :])
            dp = dot_nt(vh, dout[rest, :])
            first = jnp.where(col_s >= row_s, st[:, :blk], far)
            if j < nb - 1:
                st = jnp.concatenate([first, st[:, blk:]], axis=1)
            else:
                st = first
            p = jnp.exp(st)
            ds = (p * dp).astype(BF16)
            dv = dv + dot(p.astype(BF16), douth[h, rest, :])
            dk = dk + dot(ds, qh[h, rest, :])
            dq[rest, :] += dot_tn(ds, kh)
        dk = turn(dk, cos[at, :], sin[at, :], lane, d, -1.0)
        for n, value in ((1, dk), (2, dv)):
            sums[2:3, n * wd : (n + 1) * wd] += jnp.sum(value, axis=0, keepdims=True)
            grad[at, n * wd : (n + 1) * wd] = value.astype(BF16)

    for one in late:
        one.wait()

    def finish(i, _):
        at = block_rows(i)
        part = jnp.where(lane < d.hw, dq[at, :], 0.0) * d.scale
        part = turn(part, cos[at, :], sin[at, :], lane, d, -1.0)
        sums[2:3, :wd] += jnp.sum(part, axis=0, keepdims=True)
        grad[at, :wd] = part.astype(BF16)
        ab = dot_nt(grad[at, :], w[...])
        normed, _ = norm_parts(x_here[at, :].astype(F32))
        normed_in[at, :] = (normed * vec[0:1, :] + vec[1:2, :]).astype(BF16)
        sums[0:1, :model] += jnp.sum(ab * normed, axis=0, keepdims=True)
        sums[1:2, :model] += jnp.sum(ab, axis=0, keepdims=True)
        g_all[0, at, :] = (ab * vec[0:1, :] + back_here[at, :].astype(F32)).astype(BF16)
        return 0

    lax.fori_loop(0, nb, finish, 0)
    for n, ref in enumerate(gs):

        @pl.when(step == group - 1 - n)
        def _():
            ref[...] = g_all[...]

    dw[...] += dot_tn(normed_in[...], grad[...])

    @pl.when(step == group - 1)
    def _():
        for x_at in range(2):
            for c in range(2):

                @pl.when((info[3] == x_at) & (info[1] == c))
                def _():
                    for n, ref in enumerate(d_parts):
                        place = 2 * (c ^ (n // 2)) + (x_at ^ (n % 2))
                        dw_dense[place * hw : (place + 1) * hw, :] = ref[...]

        lines = [
            sums[0:1, :model],
            sums[1:2, :model],
            vec_mlp[0:1, :],
            vec_mlp[1:2, :],
            vec_mlp[2:3, :],
            vec_mlp[3:4, :],
        ]
        for k in range(nz):
            block = lax.rem(info[0] + k, nz)
            at = pl.multiple_of(block * 2 * rows, 16)
            part = dw[pl.ds(at, 2 * rows), :].astype(BF16)
            beside = dw_dense[pl.ds(at, 2 * rows), :]
            for c in range(2):
                to = slice(c * (rows + 16), c * (rows + 16) + rows)
                half = slice(c * rows, (c + 1) * rows)
                for t in range(3):
                    grads[k][to, t * hw : (t + 1) * hw] = part[half, t * wd : t * wd + hw]
                grads[k][to, 3 * hw :] = beside[half, :]
            grads[k][rows : rows + 16, :] = jnp.zeros((16, 4 * hw), BF16)
            for n, line in enumerate(lines):
                grads[k][rows + n : rows + n + 1, :] = line.astype(BF16)
            for t in range(3):
                grads[k][rows + 6 : rows + 7, t * hw : (t + 1) * hw] = sums[
                    2:3, t * wd : t * wd + hw
                ].astype(BF16)


def chosen(c, x, info, own, core_got, x_own, x_got):
    first = jnp.where(info[3] == x, own, x_own)
    second = jnp.where(info[3] == x, core_got, x_got)
    return jnp.where(info[1] == c, first, second)


def upper_kernel(d, info, own, core_got, x_own, x_got, low, low_got, out_up, out_low):
    for c in range(2):
        for x in range(2):
            part = chosen(c, x, info, own[...], core_got[...], x_own[...], x_got[...]).astype(F32)
            for z in range(d.nz):
                at = ((z * 2 + c) * 2 + x) * d.piece
                out_up[:, at : at + d.piece] = part[:, z * d.piece : (z + 1) * d.piece]
    for x in range(2):
        mine = jnp.where(info[3] == x, low[...], low_got[...])
        out_low[x * d.piece : (x + 1) * d.piece, :] = mine.astype(F32)


def tail_kernel(d, info, own, core_got, x_own, x_got, *outs):
    out_qkv, out_dense, v0, v1, v2, v3, v4, v5, v_up, v_qkv, scratch = outs
    rows, hw, model = d.rows, d.hw, d.model
    here = pl.ds(pl.multiple_of(info[1] * 16, 16), rows)
    after = pl.ds(pl.multiple_of((1 - info[1]) * rows, 16), 16)
    summed = None
    ups = []
    for c in range(2):
        for x in range(2):
            lines, vectors = (
                chosen(c, x, info, *(ref[at, :] for ref in (own, core_got, x_own, x_got))).astype(F32)
                for at in (here, after)
            )
            place = 2 * c + x
            for t in range(3):
                at = t * model + place * hw
                out_qkv[:, at : at + hw] = lines[:, t * hw : (t + 1) * hw]
                scratch[0:1, at : at + hw] = vectors[6:7, t * hw : (t + 1) * hw]
            out_dense[:, place * hw : (place + 1) * hw] = lines[:, 3 * hw :]
            vectors = vectors[:8, :]
            summed = vectors if summed is None else summed + vectors
            ups.append(vectors[5:6, :])
    mine = info[0] * 2 + info[1]
    turned = pltpu.roll(summed, lax.rem(model - mine * rows, model), 1)
    for n, ref in enumerate((v0, v1, v2, v3, v4)):
        ref[...] = turned[n, :rows]
    v5[...] = turned[4, :rows]
    for x in range(2):
        line = jnp.where(info[1] == 0, ups[x], ups[2 + x])
        line = jnp.broadcast_to(line, (8, line.shape[1]))
        line = pltpu.roll(line, lax.rem(model - info[0] * d.piece, model), 1)
        scratch[1:2, x * d.piece : (x + 1) * d.piece] = line[0:1, : d.piece]
    v_up[...] = scratch[1, : 2 * d.piece]
    line = jnp.broadcast_to(scratch[0:1, :], (8, 3 * model))
    line = pltpu.roll(line, lax.rem(3 * model - mine * 3 * rows, 3 * model), 1)
    v_qkv[...] = line[0, : 3 * rows]


def whole(shape):
    return pl.BlockSpec(shape, lambda *_: (0,) * len(shape))


def whole_of(arrays):
    return [whole(a.shape) for a in arrays]


def per_seq(shape):
    return pl.BlockSpec((1,) + shape, lambda s, *_: (s,) + (0,) * len(shape))


def call(kernel, info, grid, inputs, in_specs, out_shape, out_specs, scratch, cost, aliases=None):
    return pl.pallas_call(
        kernel,
        grid_spec=pltpu.PrefetchScalarGridSpec(
            num_scalar_prefetch=1,
            grid=grid,
            in_specs=in_specs,
            out_specs=out_specs,
            scratch_shapes=scratch,
        ),
        out_shape=out_shape,
        input_output_aliases=aliases or {},
        cost_estimate=pl.CostEstimate(flops=cost[0], bytes_accessed=cost[1], transcendentals=0),
    )(info, *inputs)


def of(shape, dtype=BF16):
    return jax.ShapeDtypeStruct(shape, dtype)


def pick(values, index, axis=0):
    return lax.dynamic_index_in_dim(values, index, axis, keepdims=False)


def ordered(own, other, index, axis):
    return jnp.where(index == 0, jnp.stack([own, other], axis), jnp.stack([other, own], axis))


def swap(values, axis):
    return lax.ppermute(values, axis, [(0, 1), (1, 0)])


def shards(
    sizes,
    hidden_in,
    doc_lengths,
    ln1_gain,
    ln1_bias,
    ln2_gain,
    ln2_bias,
    qkv_weight,
    qkv_bias,
    dense_weight,
    dense_bias,
    fc1_weight,
    fc1_bias,
    fc2_weight,
    fc2_bias,
    cotangent,
):
    nz, ny = sizes
    zi, ci = lax.axis_index("z"), lax.axis_index("core")
    yi, xi = lax.axis_index("y"), lax.axis_index("x")
    peer = 1 - ci
    seqs, block, model = hidden_in.shape
    rows = ln1_gain.shape[0]
    hidden = fc1_weight.shape[1]
    piece = hidden // (nz * TP)
    length = block * ny * 2
    direct = ny == 2 and seqs == 2
    group = 2 * seqs // ny
    d = Dims(model // HEADS, doc_lengths.shape[1], block)
    d.nz, d.rows, d.piece, d.model, d.group = nz, rows, piece, model, group
    hw, wd = d.hw, d.width
    first = yi if ny == 2 else jnp.zeros_like(yi)

    def shift(values, k):
        return lax.ppermute(values, "z", [(i, (i + k) % nz) for i in range(nz)])

    def gathered(half, other):
        firsts = [half] + [shift(half, k) for k in range(1, nz)]
        if ny == 2:
            seconds = [other] + [swap(firsts[k], "y") for k in range(1, nz)]
        else:
            seconds = [other] + [shift(other, k) for k in range(1, nz)]
        return firsts + seconds

    def sum_z(parts):
        got = [shift(parts[k], k) for k in range(1, nz)]
        total = parts[0].astype(F32)
        for part in got:
            total = total + part.astype(F32)
        return total.astype(BF16)

    def sum_y(part):
        if ny == 2:
            got = swap(part, "y")
            return (part.astype(F32) + got.astype(F32)).astype(BF16)
        return lax.psum(part, "y")

    def gather_tokens(values):
        if direct:
            mine, sent = pick(values, yi), pick(values, 1 - yi)
            got = swap(sent, "y")
            own = [mine, got, swap(mine, "x"), swap(got, "x")]
            return [own, [swap(a, "core") for a in own]]
        plane = lax.all_gather(values, "core", axis=0, tiled=True)
        plane = lax.all_gather(plane, ("y", "x"), axis=1, tiled=True)
        plane = lax.dynamic_slice_in_dim(plane, yi * group, group, 0)
        return [[plane[n : n + 1]] for n in range(group)]

    def scatter_tokens(values):
        if direct:
            own = values[0].reshape(ny, 2, block, model)
            got = swap(values[1], "core").reshape(ny, 2, block, model)
            sent = pick(own, 1 - xi, 1).astype(F32) + pick(got, 1 - xi, 1).astype(F32)
            sent = sent.astype(BF16)
            arrived = swap(sent, "x")
            own, got, arrived = lax.optimization_barrier((own, got, arrived))
            kept = pick(own, xi, 1).astype(F32) + pick(got, xi, 1).astype(F32)
            total = (kept + arrived.astype(F32)).astype(BF16)
            got = swap(pick(total, 1 - yi), "y")
            return ordered(pick(total, yi), got, yi, 0)
        plane = jnp.zeros((2 * seqs, length, model), BF16)
        plane = lax.dynamic_update_slice_in_dim(plane, jnp.concatenate(values), yi * group, 0)
        plane = lax.psum_scatter(plane, "core", scatter_dimension=0, tiled=True)
        return lax.psum_scatter(plane, ("y", "x"), scatter_dimension=1, tiled=True)

    if direct:
        lengths = pick(doc_lengths, yi)
        lengths = jnp.concatenate([lengths, swap(lengths, "core")])
    else:
        lengths = lax.all_gather(doc_lengths, "core", axis=0, tiled=True)
        lengths = lax.dynamic_slice_in_dim(lengths, yi * group, group, 0).reshape(-1)
    places = jnp.stack([zi, ci, yi, xi, first, yi, yi, yi]).astype(jnp.int32)
    info = jnp.concatenate([places, lengths.astype(jnp.int32)])

    x_pieces = gather_tokens(hidden_in)
    count = len(x_pieces[0])

    small = [ln1_gain, ln1_bias, ln2_gain, ln2_bias, dense_bias, fc2_bias, qkv_bias, fc1_bias]
    inputs = [qkv_weight, fc1_weight, fc2_weight] + small
    q_type, f_type = of((rows, 3 * hw)), of((rows + 16, nz * piece))
    low_type = of((piece // 2, model))
    out_shape = [q_type, q_type, f_type, f_type, low_type, low_type]
    q_own, q_sent, f_own, f_sent, low_first, low_second = call(
        functools.partial(prep_kernel, d),
        places,
        (1,),
        inputs,
        whole_of(inputs),
        out_shape,
        whole_of(out_shape),
        [],
        (0, 8 * rows * hidden),
    )
    q_got, f_got = swap(q_sent, "core"), swap(f_sent, "core")
    near = first == ci
    q_pair = ordered(q_own, q_got, ci, 0)
    q_all = [q_pair] + [shift(q_pair, k) for k in range(1, nz)]
    f_all = gathered(jnp.where(near, f_own, f_got), jnp.where(near, f_got, f_own))
    low_all = gathered(low_first, low_second)

    cot_pieces = gather_tokens(cotangent)

    dense_all = [dense_weight] + [shift(dense_weight, k) for k in range(1, nz)]

    def dense_rows(place):
        blocks = []
        for b in range(nz // TP):
            total = dense_all[0]
            for k in range(1, nz):
                here = lax.rem(zi - k + nz, nz) == place * (nz // TP) + b
                total = jnp.where(here, dense_all[k], total)
            blocks.append(total)
        return jnp.concatenate(blocks, axis=0)

    dense_own = dense_rows(2 * ci + xi)
    dense_got = swap(dense_rows(2 * peer + xi), "core")

    feature = jnp.arange(math.lcm(d.hd, 128), dtype=jnp.int32) % d.hd
    turned = feature < ROT
    frequency = jnp.exp((feature % (ROT // 2)).astype(F32) * (-2.0 * math.log(10000.0) / ROT))
    angles = jnp.arange(length, dtype=F32)[:, None] * frequency[None, :]
    cos = jnp.where(turned[None, :], jnp.cos(angles), 1.0)
    sin = jnp.where(turned[None, :], jnp.sin(angles), 0.0)

    pairs = d.nh * length * length // 2
    token_type = of((1, length, model))
    tokens_type = of((group, length, model))
    tile = 512 if length % 512 == 0 else block
    steps = group * length // tile
    per = length // tile
    tiles = pl.BlockSpec((1, tile, model), lambda t, *_: (lax.div(t, per), lax.rem(t, per), 0))
    wide = of((8, 3 * wd), F32)
    inputs = [a for one in x_pieces for a in one] + [a for one in cot_pieces for a in one]
    inputs += f_all + low_all
    out_shape = [tokens_type] * 4 + [of((8, model), F32)] * 2 + [wide]
    out_shape += [of((2 * rows + piece, model))] * nz
    x, cot, out, back, vec_mlp, vec, bias, *up_parts = call(
        functools.partial(mlp_kernel, d, steps, count),
        info,
        (steps,),
        inputs,
        [pl.BlockSpec(memory_space=pl.ANY)] * (2 * group * count)
        + whole_of(f_all)
        + [pl.BlockSpec(memory_space=pl.ANY)] * len(low_all),
        out_shape,
        [tiles] * 4 + whole_of(out_shape[4:]),
        [
            pltpu.VMEM((group, length, model), BF16),
            pltpu.VMEM((group, length, model), BF16),
            pltpu.VMEM((model, nz * piece), BF16),
            pltpu.VMEM((nz * piece, model), BF16),
            pltpu.VMEM((model, nz * piece), F32),
            pltpu.VMEM((nz * piece, model), F32),
            pltpu.VMEM((8, model), F32),
            pltpu.VMEM((2 * nz, 16, 128), F32),
            pltpu.SemaphoreType.DMA((2 * group * count + 2 * nz,)),
        ],
        (12 * group * length * model * model, group * length * 12 * model),
    )
    rows_type = of((group, length, wd))
    inputs = [x, cot, out] + q_all + [dense_own, dense_got, vec, bias, cos, sin]
    out_shape = [token_type] * group + [rows_type] * 4 + [of((hw, hw))] * 4
    done = call(
        functools.partial(forward_kernel, d),
        info,
        (group,),
        inputs,
        [per_seq((length, model))] + [pl.BlockSpec(memory_space=pl.ANY)] * 2 + whole_of(inputs[3:]),
        out_shape,
        whole_of(out_shape[:group]) + [per_seq((length, wd))] * 4 + whole_of(out_shape[group + 4 :]),
        [
            pltpu.VMEM((model, 3 * wd), BF16),
            pltpu.VMEM((wd, model), BF16),
            pltpu.VMEM((wd, model), F32),
            pltpu.VMEM((1, length, model), BF16),
            pltpu.VMEM((length, model), BF16),
            pltpu.VMEM((length, model), BF16),
            pltpu.SemaphoreType.DMA((2,)),
        ],
        (
            group * (2 * length * model * 5 * wd + 4 * pairs * wd),
            group * length * 2 * (4 * model + 4 * wd),
        ),
    )
    outs = list(done[:group])
    q, k, v, att = done[group : group + 4]
    d_own, d_own_x, d_sent, d_sent_x = done[group + 4 :]

    out_mine = scatter_tokens(outs)
    block_out = (hidden_in.astype(F32) + out_mine.astype(F32) + vec[4]).astype(BF16)

    up_sum = sum_y(sum_z(up_parts))
    low_own = up_sum[2 * rows :]
    sent = lax.dynamic_slice_in_dim(up_sum, peer * rows, rows)
    up_own = lax.dynamic_slice_in_dim(up_sum, ci * rows, rows)
    up_got = swap(sent, "core")

    d_got, d_got_x = swap(d_sent, "core"), swap(d_sent_x, "core")
    d_parts = [d_own, swap(d_own_x, "x"), d_got, swap(d_got_x, "x")]

    anywhere = pl.BlockSpec(memory_space=pl.ANY)

    def turned_seq(width):
        return pl.BlockSpec((1, length, width), lambda s, *_: (group - 1 - s, 0, 0))

    inputs = [x, cot, back, att, q, k, v] + q_all
    inputs += [dense_own, dense_got, vec, cos, sin, vec_mlp] + d_parts
    out_shape = [token_type] * group + [of((2 * rows + 16, 4 * hw))] * nz
    done = call(
        functools.partial(backward_kernel, d),
        info,
        (group,),
        inputs,
        [anywhere, turned_seq(model), anywhere] + [turned_seq(wd)] * 4 + whole_of(inputs[7:]),
        out_shape,
        whole_of(out_shape),
        [
            pltpu.VMEM((model, 3 * wd), F32),
            pltpu.VMEM((8, 3 * wd), F32),
            pltpu.VMEM((model, hw), BF16),
            pltpu.VMEM((model, 3 * wd), BF16),
            pltpu.VMEM((wd, model), BF16),
            pltpu.VMEM((length, 3 * wd), BF16),
            pltpu.VMEM((length, wd), BF16),
            pltpu.VMEM((d.nh, length, wd), BF16),
            pltpu.VMEM((d.nh, length, wd), BF16),
            pltpu.VMEM((length, wd), F32),
            pltpu.VMEM((length, model), BF16),
            pltpu.VMEM((1, length, model), BF16),
            pltpu.VMEM((length, model), BF16),
            pltpu.VMEM((length, model), BF16),
            pltpu.SemaphoreType.DMA((2,)),
        ],
        (
            2 * group * length * model * 7 * wd + 10 * group * pairs * wd,
            group * length * 2 * (4 * model + 4 * wd),
        ),
    )
    gs, state = list(done[:group]), done[group:]
    chunk = sum_y(sum_z(state))
    own = lax.dynamic_slice_in_dim(chunk, ci * rows, rows + 16)
    sent = lax.dynamic_slice_in_dim(chunk, peer * rows, rows + 16)
    core_got = swap(sent, "core")

    inputs = [up_own, up_got, swap(up_own, "x"), swap(up_got, "x")]
    inputs += [low_own, swap(low_own, "x")]
    out_shape = [of((rows, hidden), F32), of((2 * piece, model), F32)]
    out_upper, out_lower = call(
        functools.partial(upper_kernel, d),
        info,
        (1,),
        inputs,
        whole_of(inputs),
        out_shape,
        whole_of(out_shape),
        [],
        (0, 12 * rows * hidden),
    )
    inputs = [own, core_got, swap(own, "x"), swap(core_got, "x")]
    line = of((rows,), F32)
    out_shape = [of((rows, 3 * model), F32), of((rows, model), F32)] + [line] * 6
    out_shape += [of((2 * piece,), F32), of((3 * rows,), F32)]
    out_qkv, out_dense, v0, v1, v2, v3, v4, v5, v_up, v_qkv = call(
        functools.partial(tail_kernel, d),
        info,
        (1,),
        inputs,
        whole_of(inputs),
        out_shape,
        whole_of(out_shape),
        [pltpu.VMEM((8, 3 * model), F32)],
        (0, 24 * rows * model),
    )

    scaled = scatter_tokens(gs).astype(F32)
    normed, inverse = norm_parts(hidden_in.astype(F32))
    residue = (
        scaled
        - jnp.mean(scaled, axis=-1, keepdims=True)
        - normed * jnp.mean(scaled * normed, axis=-1, keepdims=True)
    )
    input_grad = cotangent.astype(F32) + residue * inverse
    return (
        block_out,
        input_grad,
        v0,
        v1,
        v2,
        v3,
        out_qkv,
        v_qkv,
        out_dense,
        v4,
        out_upper,
        v_up,
        out_lower,
        v5,
    )


def solution(mesh):
    nz, ny = mesh.shape["dp"] // 2, mesh.shape["ctx"] // 2
    fine = Mesh(mesh.devices.reshape(nz, 2, ny, 2), ("z", "core", "y", "x"))
    dp, ctx = ("z", "core"), ("y", "x")
    tokens = P(dp, ctx, None)
    vector, matrix = P(dp), P(dp, None)

    def body(*args):
        return shards((nz, ny), *args)

    return jax.shard_map(
        body,
        mesh=fine,
        in_specs=(
            tokens,
            matrix,
            vector,
            vector,
            vector,
            vector,
            matrix,
            vector,
            matrix,
            vector,
            matrix,
            vector,
            matrix,
            vector,
            tokens,
        ),
        out_specs=(
            tokens,
            tokens,
            vector,
            vector,
            vector,
            vector,
            matrix,
            vector,
            matrix,
            vector,
            matrix,
            vector,
            matrix,
            vector,
        ),
        check_vma=False,
    )
```
